32 devices in a mesh: facet: 2 (over y), sub: 16 (over z, x, core).
Axes of the slice: x: 2, y: 2, z: 4, core: 2. Of those that a mesh axis runs over, the one named last changes fastest.
Arguments:
- contributions: bfloat16 [16, 16, 2, 2, 192, 192], P('facet', 'sub'), may hold values from -6 to 6
- slot_subgrid: int32 [16, 2, 2], P('sub'), may hold values from -1 to 1, as said below
- vis_count: int32 [2, 16, 2], P('facet', 'sub'), may hold values from 0 to 384, as said below
- vis_uv: float32 [2, 16, 2, 2, 384], P('facet', 'sub'), may hold values from 0 to 512
- vis_obs: float32 [2, 16, 2, 2, 384], P('facet', 'sub'), may hold values from -6 to 6
- vis_weight: float32 [2, 16, 2, 384], P('facet', 'sub'), may hold values from 0.25 to 2
- subgrid_offset: int32 [16, 2, 2], P('sub'), may hold values from 0 to 511
Outputs:
- facet_residual: float32 [16, 2, 512, 512], P('facet', None, 'sub')
The draws below stay inside these ranges and needn't reach their ends.
Inputs may be any that keep to these rules, and one draw needn't show every extreme that they name: `slot_subgrid`: in every column each of the 2 subgrids sits in exactly one of the 2 x 2 slots and the other slots hold -1; in every column the 2 slots of some device are all used. `vis_count`: 0 exactly for slots that hold no subgrid, from 384 // 4 to 384 for the others, and 384 in some slot of every column.
All inputs are finite; a program needn't handle non-finite values.
Results may differ from the reference program's by a relative error of at most 0.013.
Values may be sent and summed in bfloat16 or wider, within the bound.
A program may use at most 128 MiB of HBM per device.

```python
import math
import jax
import jax.numpy as jnp
from jax import lax

SUBGRID = 512
CONTRIB = 192
FACET_SIDE = 4
WIN = 512
VCAP = 384
FACETS = 16
GROUPS = 2
COLUMNS = 16
SG_COL = 2
SLOTS = 2


def slot_layout(key):
    base_key = jax.random.fold_in(key, 7)
    column_keys = jax.random.split(base_key, COLUMNS)

    def one_column(column_key):
        key_group, key_order, key_ids, key_lengths = jax.random.split(column_key, 4)
        capacity = GROUPS * SLOTS
        full_group = jax.random.randint(key_group, (), 0, GROUPS)
        scores = jax.random.permutation(key_order, capacity).astype(jnp.int32)
        owner = jnp.arange(capacity) // SLOTS
        ranked = jnp.where(owner == full_group, scores - capacity, scores)
        ranking = jnp.argsort(ranked, stable=True)
        subgrid_ids = jax.random.permutation(key_ids, SG_COL).astype(jnp.int32)
        slot_table = jnp.full((capacity,), -1, jnp.int32).at[ranking[:SG_COL]].set(subgrid_ids)
        lengths = jax.random.randint(key_lengths, (capacity,), VCAP // 4, VCAP + 1).astype(jnp.int32)
        lengths = lengths.at[ranking[0]].set(VCAP)
        lengths = jnp.where(slot_table >= 0, lengths, 0).astype(jnp.int32)
        return (slot_table.reshape(GROUPS, SLOTS), lengths.reshape(GROUPS, SLOTS))
    return jax.vmap(one_column)(column_keys)


def draw_slot_subgrid(key, part):
    return slot_layout(key)[0]


def draw_vis_count(key, part):
    return jnp.transpose(slot_layout(key)[1], (1, 0, 2))


def plant(drawn, key, least, top_value):
    longest = drawn.shape.index(max(drawn.shape))
    spots = []
    for shift in (0, 1):
        where = [jax.random.randint(jax.random.fold_in(key, axis), (), 0, length) for axis, length in enumerate(drawn.shape)]
        where[longest] = (where[longest] + shift) % drawn.shape[longest]
        spots.append(tuple(where))
    return drawn.at[spots[0]].set(least).at[spots[1]].set(top_value)


def levels(stream_key, extent, cuts, smallest, top_value):
    level, own = 1.0, jax.random.fold_in(stream_key, 6)
    for dim, shards_of in cuts:
        steps = jnp.exp(jax.random.uniform(jax.random.fold_in(own, dim), (shards_of,), jnp.float32, smallest / len(cuts), top_value / len(cuts)))
        level = level * jnp.repeat(steps, extent[dim] // shards_of).reshape([-1 if axis == dim else 1 for axis in range(len(extent))])
    return level


def normal_values(key, extent, scale, reach, cuts=(), kind=jnp.bfloat16):
    drawn = jax.random.normal(key, extent, jnp.float32) * scale
    if len(cuts) > 0:
        drawn = levels(key, extent, cuts, -0.22, 0.18) * drawn
    return jnp.clip(drawn, min=-reach, max=reach).astype(kind)


def setup_inputs(seed: int = 0) -> dict:
    splits = jax.random.split(jax.random.key(seed), 8)
    contributions = normal_values(splits[0], (FACETS, COLUMNS, SG_COL, 2, CONTRIB, CONTRIB), 1.0, 6.0, ((0, 2), (1, 16)))
    slot_subgrid = draw_slot_subgrid(jax.random.fold_in(splits[7], 71), 0)
    vis_count = draw_vis_count(jax.random.fold_in(splits[7], 71), 0)
    vis_uv = jnp.clip(512.0 * jax.random.uniform(splits[3], (GROUPS, COLUMNS, SLOTS, 2, VCAP), jnp.float32) ** levels(splits[3], (GROUPS, COLUMNS, SLOTS, 2, VCAP), ((0, 2), (1, 16)), -0.2, 0.2), 0.0, 512.0)
    vis_obs = normal_values(splits[4], (GROUPS, COLUMNS, SLOTS, 2, VCAP), 1.0, 6.0, ((0, 2), (1, 16)), jnp.float32)
    vis_weight = jnp.clip(jnp.exp(math.log(2.0) - 2.0794415 * jax.random.uniform(splits[5], (GROUPS, COLUMNS, SLOTS, VCAP), jnp.float32) ** levels(splits[5], (GROUPS, COLUMNS, SLOTS, VCAP), ((0, 2), (1, 16)), -0.2, 0.2)), 0.25, 2.0)
    subgrid_offset = plant(jax.random.randint(splits[6], (COLUMNS, SG_COL, 2), 0, WIN), jax.random.fold_in(splits[6], 1), 0, WIN - 1).astype(jnp.int32)
    return dict(contributions=contributions, slot_subgrid=slot_subgrid, vis_count=vis_count, vis_uv=vis_uv, vis_obs=vis_obs, vis_weight=vis_weight, subgrid_offset=subgrid_offset)


def corner_cells(facet_index):
    stride = (SUBGRID - CONTRIB) // (FACET_SIDE - 1)
    return (facet_index // FACET_SIDE * stride, facet_index % FACET_SIDE * stride)

def assemble(blocks):
    subgrid_image = None
    for facet_index in range(FACETS):
        start_row, start_column = corner_cells(facet_index)
        padded = jnp.pad(blocks[facet_index].astype(jnp.float32), ((0, 0), (start_row, SUBGRID - start_row - CONTRIB), (start_column, SUBGRID - start_column - CONTRIB)))
        subgrid_image = padded if subgrid_image is None else subgrid_image + padded
    return subgrid_image.astype(jnp.bfloat16)

def phase_tables(coordinate):
    cell_grid = jnp.arange(SUBGRID, dtype=jnp.float32)
    phase_angle = 2.0 * math.pi / SUBGRID * cell_grid[:, None] * coordinate[None, :]
    return (jnp.cos(phase_angle).astype(jnp.bfloat16), (-jnp.sin(phase_angle)).astype(jnp.bfloat16))

def visit_subgrid(subgrid_image, coordinates, observed, weight, visible_count):
    first_real, first_imaginary = phase_tables(coordinates[0])
    second_real, second_imaginary = phase_tables(coordinates[1])
    cells = SUBGRID
    visits = coordinates.shape[1]
    stacked = jnp.concatenate([subgrid_image[0], subgrid_image[1]], axis=0)
    partial_sums = jnp.dot(stacked, jnp.concatenate([second_real, second_imaginary], axis=1), preferred_element_type=jnp.float32)
    inner_real = partial_sums[:cells, :visits] - partial_sums[cells:, visits:]
    inner_imaginary = partial_sums[:cells, visits:] + partial_sums[cells:, :visits]
    first_rf = first_real.astype(jnp.float32)
    first_if = first_imaginary.astype(jnp.float32)
    model_real = lax.optimization_barrier(jnp.sum(first_rf * inner_real - first_if * inner_imaginary, axis=0)) / SUBGRID
    model_imaginary = lax.optimization_barrier(jnp.sum(first_rf * inner_imaginary + first_if * inner_real, axis=0)) / SUBGRID
    active = jnp.arange(visits) < visible_count
    residual_real = jnp.where(active, weight * (observed[0] - model_real), 0.0).astype(jnp.bfloat16)
    residual_imaginary = jnp.where(active, weight * (observed[1] - model_imaginary), 0.0).astype(jnp.bfloat16)
    real_float = residual_real.astype(jnp.float32)
    imaginary_float = residual_imaginary.astype(jnp.float32)
    lift_real = (first_rf * real_float + first_if * imaginary_float).astype(jnp.bfloat16)
    lift_imaginary = (first_rf * imaginary_float - first_if * real_float).astype(jnp.bfloat16)
    lifted = jnp.concatenate([lift_real, lift_imaginary], axis=0)
    tables = jnp.concatenate([second_real, second_imaginary], axis=0)
    gridded = lax.dot_general(lifted, tables, (((1,), (1,)), ((), ())), preferred_element_type=jnp.float32)
    grid_scale = 1.0 / math.sqrt(VCAP)
    grid_real = (gridded[:cells, :cells] + gridded[cells:, cells:]) * grid_scale
    grid_imaginary = (gridded[cells:, :cells] - gridded[:cells, cells:]) * grid_scale
    grid_both = jnp.stack([grid_real, grid_imaginary])
    pieces = []
    for facet_index in range(FACETS):
        start_row, start_column = corner_cells(facet_index)
        pieces.append(grid_both[:, start_row:start_row + CONTRIB, start_column:start_column + CONTRIB])
    return jnp.stack(pieces).astype(jnp.bfloat16)

def place_piece(accum, pieces, offset):
    anchor = jnp.zeros((), jnp.int32)
    corner_start = (anchor, anchor, offset[0].astype(jnp.int32), offset[1].astype(jnp.int32))
    current = lax.dynamic_slice(accum, corner_start, pieces.shape)
    return lax.dynamic_update_slice(accum, current + pieces.astype(jnp.float32), corner_start)

def fold_edges(accum):
    upper = accum[:, :, :WIN].at[:, :, :CONTRIB].add(accum[:, :, WIN:])
    return upper[..., :WIN].at[..., :CONTRIB].add(upper[..., WIN:])

def reference(contributions, slot_subgrid, vis_count, vis_uv, vis_obs, vis_weight, subgrid_offset):
    padded_width = WIN + CONTRIB
    start_accum = jnp.zeros((FACETS, 2, padded_width, padded_width), jnp.float32)

    def visit_one(position_index, accum):
        column = position_index // SG_COL
        member = position_index % SG_COL
        flattened = slot_subgrid[column].reshape(-1)
        where_slot = jnp.argmax(flattened == member).astype(jnp.int32)
        group_index = where_slot // SLOTS
        slot_index = where_slot % SLOTS
        subgrid_image = assemble(contributions[:, column, member])
        returned = visit_subgrid(subgrid_image, vis_uv[group_index, column, slot_index], vis_obs[group_index, column, slot_index], vis_weight[group_index, column, slot_index], vis_count[group_index, column, slot_index])
        return place_piece(accum, returned, subgrid_offset[column, member])
    accum = lax.fori_loop(0, COLUMNS * SG_COL, visit_one, start_accum)
    window_gain = WIN / (CONTRIB * math.sqrt(SG_COL * COLUMNS))
    return fold_edges(accum) * window_gain
```

```python
import functools
import math

import jax
import jax.numpy as jnp
from jax import lax
from jax.experimental import pallas as pl
from jax.experimental.pallas import tpu as pltpu
from jax.sharding import PartitionSpec as P

SUBGRID = 512
FACET_SIDE = 4
WIN = 512
BLOCK = 16
MESH = pl.DeviceIdType.MESH


def cis(turn):
    turn = turn - jnp.floor(turn + 0.5)
    x = turn * math.pi
    q = x * x
    s = -1.0 / math.factorial(11)
    for order in (9, 7, 5, 3, 1):
        sign = 1.0 if order % 4 == 1 else -1.0
        s = s * q + sign / math.factorial(order)
    s = s * x
    c = 1.0 / math.factorial(12)
    for order in (10, 8, 6, 4, 2, 0):
        sign = 1.0 if order % 4 == 0 else -1.0
        c = c * q + sign / math.factorial(order)
    return 1.0 - 2.0 * s * s, 2.0 * s * c


def turns(k, w):
    high = jnp.floor(w * 4096.0) * (1.0 / 4096.0)
    low = w - high
    p = k * high
    return (p - jnp.floor(p + 0.5)) + k * low


def cmul(a, b):
    return a[0] * b[0] - a[1] * b[1], a[0] * b[1] + a[1] * b[0]


def row_iota(rows, lanes):
    return lax.broadcasted_iota(jnp.int32, (rows, lanes), 0)


def corner(index, stride):
    return lax.div(index, FACET_SIDE) * stride, lax.rem(index, FACET_SIDE) * stride


def blocks_in(c_ref, cs, j):
    per_group, _, _, side, _ = c_ref.shape
    across = min(per_group, FACET_SIDE)
    for a in range(per_group // across):
        for part in range(2):
            strip = jnp.concatenate([c_ref[a * across + b, j, part] for b in range(across)], axis=1)
            cs[j, a, part * side : (part + 1) * side, :] = strip


def column_tables(first_col, stride, side, v, rhs):
    lanes = rhs.shape[1] // 2
    lines = row_iota(BLOCK, lanes)
    wv = v * (1.0 / SUBGRID)
    step = tuple(jnp.broadcast_to(t, (BLOCK, lanes)) for t in cis(turns(float(BLOCK), wv)))
    for b in range(rhs.shape[0] // side):
        k = (lines + (first_col + b * stride)).astype(jnp.float32)
        now = cis(turns(k, wv))
        for h in range(side // BLOCK):
            at = b * side + h * BLOCK
            rhs[at : at + BLOCK, :lanes] = now[0].astype(jnp.bfloat16)
            rhs[at : at + BLOCK, lanes:] = (-now[1]).astype(jnp.bfloat16)
            now = cmul(now, step)


def partial_model(first_row, stride, side, u, images, rhs):
    lanes = rhs.shape[1] // 2
    lines = row_iota(BLOCK, lanes)
    wu = u * (1.0 / SUBGRID)
    step = tuple(jnp.broadcast_to(t, (BLOCK, lanes)) for t in cis(turns(float(BLOCK), wu)))
    total_r = jnp.zeros((BLOCK, lanes), jnp.float32)
    total_i = jnp.zeros((BLOCK, lanes), jnp.float32)
    for a in range(images.shape[0]):
        res = jnp.dot(images[a], rhs[...], preferred_element_type=jnp.float32)
        k = (lines + (first_row + a * stride)).astype(jnp.float32)
        now = cis(turns(k, wu))
        for h in range(side // BLOCK):
            top = res[h * BLOCK : (h + 1) * BLOCK]
            low = res[side + h * BLOCK : side + (h + 1) * BLOCK]
            inner_r = top[:, :lanes] - low[:, lanes:]
            inner_i = top[:, lanes:] + low[:, :lanes]
            total_r = total_r + (now[0] * inner_r + now[1] * inner_i)
            total_i = total_i + (now[0] * inner_i - now[1] * inner_r)
            now = cmul(now, step)
    return (
        jnp.sum(total_r, axis=0, keepdims=True) * (1.0 / SUBGRID),
        jnp.sum(total_i, axis=0, keepdims=True) * (1.0 / SUBGRID),
    )


def exchange_kernel(
    groups,
    columns,
    per_group,
    table_ref,
    count_ref,
    off_ref,
    c_hbm,
    uv_ref,
    obs_ref,
    weight_ref,
    all_ref,
    where_ref,
    c_ref,
    cs,
    rhs,
    uv_all,
    ow_all,
    ow_mine,
    uv_mine,
    uv_cols,
    part_mine,
    part_all,
    resid_mine,
    resid_cols,
    c_sem,
    uv_send,
    uv_recv,
    ow_send,
    ow_recv,
    cols_send,
    cols_recv,
    part_send,
    part_recv,
    resid_send,
    resid_recv,
):
    members = c_ref.shape[1]
    slots = uv_ref.shape[2]
    lanes = uv_ref.shape[-1]
    halves = part_send.shape[0]
    each = members // halves
    group = lax.axis_index("facet")
    column = lax.axis_index("sub")
    loads = [
        pltpu.make_async_copy(c_hbm.at[:, 0, j], c_ref.at[:, j], c_sem.at[j]) for j in range(members)
    ]
    for load in loads:
        load.start()

    barrier = pltpu.get_barrier_semaphore()

    def peer_group(p):
        return lax.rem(group + p, groups)

    def peer_column(p):
        return lax.rem(column + p, columns)

    @pl.loop(1, groups)
    def _(p):
        pl.semaphore_signal(barrier, inc=1, device_id={"facet": peer_group(p)}, device_id_type=MESH)

    @pl.loop(1, columns)
    def _(p):
        pl.semaphore_signal(barrier, inc=1, device_id={"sub": peer_column(p)}, device_id_type=MESH)

    lane = lax.broadcasted_iota(jnp.int32, (1, lanes), 1)
    for k in range(slots):
        ow_mine[k, 0:2, :] = obs_ref[0, 0, k]
        live = jnp.where(lane < count_ref[0, 0, k], 1.0, 0.0)
        ow_mine[k, 2:3, :] = weight_ref[0, 0, k : k + 1, :] * live
    uv_all[group] = uv_ref[0, 0]
    ow_all[group] = ow_mine[...]
    pl.semaphore_wait(barrier, groups - 1 + columns - 1)

    def to_group(src, dst, send, recv, p):
        return pltpu.make_async_remote_copy(
            src_ref=src,
            dst_ref=dst,
            send_sem=send.at[p],
            recv_sem=recv.at[p],
            device_id={"facet": peer_group(p)},
            device_id_type=MESH,
        )

    def to_column(src, dst, send, recv, p):
        return pltpu.make_async_remote_copy(
            src_ref=src,
            dst_ref=dst,
            send_sem=send.at[p],
            recv_sem=recv.at[p],
            device_id={"sub": peer_column(p)},
            device_id_type=MESH,
        )

    def each_group(make, act):
        @pl.loop(1, groups)
        def _(p):
            act(make(p))

    def each_column(make, act):
        @pl.loop(1, columns)
        def _(p):
            act(make(p))

    def uv_copy(p):
        return to_group(uv_ref.at[0, 0], uv_all.at[group], uv_send, uv_recv, p)

    def ow_copy(p):
        return to_group(ow_mine, ow_all.at[group], ow_send, ow_recv, p)

    def cols_copy(p):
        return to_column(uv_mine, uv_cols.at[column], cols_send, cols_recv, p)

    def part_copy(h):
        return lambda p: to_group(
            part_mine.at[h], part_all.at[h, group], part_send.at[h], part_recv.at[h], p
        )

    def resid_copy(h):
        return lambda p: to_column(
            resid_mine.at[h], resid_cols.at[column, h], resid_send.at[h], resid_recv.at[h], p
        )

    def start(copy):
        copy.start()

    def wait(copy):
        copy.wait()

    each_group(uv_copy, start)
    each_group(ow_copy, start)
    for load in loads:
        load.wait()

    @pl.loop(0, members)
    def _(j):
        blocks_in(c_ref, cs, j)

    each_group(uv_copy, wait)

    def holds(g, k, j):
        return jnp.where(table_ref[0, g, k] == j, 1.0, 0.0)

    @pl.loop(0, members)
    def _(j):
        picked = jnp.zeros((2, lanes), jnp.float32)
        for g in range(groups):
            for k in range(slots):
                picked = picked + uv_all[g, k] * holds(g, k, j)
        uv_mine[j, 0:2, :] = picked
        uv_mine[j, 2:3, :] = jnp.where(
            lane == 0, off_ref[0, j, 0], jnp.where(lane == 1, off_ref[0, j, 1], 0)
        ).astype(jnp.float32)

    uv_cols[column] = uv_mine[...]
    each_column(cols_copy, start)

    side = c_ref.shape[-1]
    stride = (SUBGRID - side) // (FACET_SIDE - 1)
    first_row, first_col = corner(group * per_group, stride)

    def tables(j, slot):
        column_tables(first_col, stride, side, uv_mine[j, 1:2, :], rhs[slot])

    def models(h, j, slot):
        real, imaginary = partial_model(
            first_row, stride, side, uv_mine[j, 0:1, :], cs.at[j], rhs[slot]
        )
        part_mine[h, j - h * each, 0:1, :] = real
        part_mine[h, j - h * each, 1:2, :] = imaginary

    if each == 1:
        tables(0, 0)
    for h in range(halves):
        if each == 1:
            if h + 1 < halves:
                tables(h + 1, (h + 1) % 2)
            models(h, h, h % 2)
        else:

            @pl.loop(h * each, (h + 1) * each)
            def _(j):
                tables(j, 0)
                models(h, j, 0)

        part_all[h, group] = part_mine[h]
        each_group(part_copy(h), start)

    each_group(ow_copy, wait)
    for h in range(halves):
        each_group(part_copy(h), wait)

        @pl.loop(0, each)
        def _(i):
            picked = jnp.zeros((3, lanes), jnp.float32)
            model = jnp.zeros((2, lanes), jnp.float32)
            for g in range(groups):
                model = model + part_all[h, g, i]
                for k in range(slots):
                    picked = picked + ow_all[g, k] * holds(g, k, h * each + i)
            resid = picked[2:3] * (picked[0:2] - model)
            resid_mine[h, i] = resid.astype(jnp.bfloat16)

        resid_cols[column, h] = resid_mine[h]
        each_column(resid_copy(h), start)

    each_column(cols_copy, wait)

    @pl.loop(0, columns)
    def _(c):
        for j in range(members):
            all_ref[c, j : j + 1, :] = uv_cols[c, j, 0:1, :]
            all_ref[c, members + j : members + j + 1, :] = uv_cols[c, j, 1:2, :]
            where_ref[c, j : j + 1, :] = uv_cols[c, j, 2:3, :128].astype(jnp.int32)

    for h in range(halves):
        each_column(resid_copy(h), wait)

    @pl.loop(0, columns)
    def _(c):
        for j in range(members):
            resid = resid_cols[c, j // each, j % each].astype(jnp.float32)
            all_ref[c, 2 * members + j : 2 * members + j + 1, :] = resid[0:1]
            all_ref[c, 3 * members + j : 3 * members + j + 1, :] = resid[1:2]


SIN = (3.14159264, -5.16771008, 2.55007752, -0.59829129, 0.07765766)
COS = (1.0, -4.93480214, 4.05870916, -1.335212, 0.23493731, -0.02439632)


def fraction(w):
    t = w * (1.0 / SUBGRID)
    t = t - jnp.where(t >= 0.5, 1.0, 0.0)
    return (t * 4294967296.0).astype(jnp.int32)


def wave(phase):
    t = phase.astype(jnp.float32) * (1.0 / 4294967296.0)
    q = t * t
    s = SIN[4]
    for a in SIN[3::-1]:
        s = s * q + a
    s = s * t
    c = COS[5]
    for a in COS[4::-1]:
        c = c * q + a
    s2 = s + s
    return 1.0 - s2 * s, s2 * c


def grid_kernel(per_group, side, gain, off_ref, all_ref, out_ref, front, back, lefts, rights, lead, hits):
    columns, depth, lanes = all_ref.shape
    members = depth // 4
    rows = out_ref.shape[2]
    chunks = front.shape[0] // 2
    half = side // 2
    base = lefts[0].shape[0] // 2
    stride = (SUBGRID - side) // (FACET_SIDE - 1)
    facet_here = lax.axis_index("facet") * per_group
    first_line = lax.axis_index("sub") * rows
    facet_rows = lead.shape[1]
    first_a = lax.div(facet_here, FACET_SIDE)
    lines8 = row_iota(8, lanes)
    facet = row_iota(facet_rows, lanes) + facet_here
    lead_u = (lax.div(facet, FACET_SIDE) - first_a) * stride
    lead_v = lax.rem(facet, FACET_SIDE) * (2 * stride) + (side - 1)
    front[...] = jnp.zeros_like(front)
    back[...] = jnp.zeros_like(back)
    if base > per_group * rows:
        for left in lefts:
            left[...] = jnp.zeros_like(left)

    total = columns * members

    def begin(s):
        start = lax.rem(first_line - off_ref[lax.div(s, members), lax.rem(s, members), 0] + WIN, WIN)
        return jnp.where(start > WIN - rows, start - WIN, start)

    def scan(s, found):
        hits[found] = s
        return found + jnp.where(begin(s) < side, 1, 0)

    found = lax.fori_loop(0, total, scan, jnp.int32(0), unroll=min(total, 32))

    def wide(x):
        return jnp.broadcast_to(x, (8, lanes))

    def conj_mul(a, b):
        return a[0] * b[0] + a[1] * b[1], a[1] * b[0] - a[0] * b[1]

    def chebyshev(first, step, count):
        double = step[0] + step[0]
        seq = [first]
        if count > 1:
            seq.append(cmul(first, step))
        while len(seq) < count:
            seq.append(tuple(double * p - q for p, q in zip(seq[-1], seq[-2])))
        return seq

    def fill(index, left, right):
        s = jnp.where(index < found, hits[jnp.minimum(index, total - 1)], 0)
        scale = jnp.where(index < found, gain, 0.0)
        column = lax.div(s, members)
        j = lax.rem(s, members)
        start = begin(s)
        fu = fraction(all_ref[column, pl.ds(j, 1), :])
        hv = lax.shift_right_arithmetic(fraction(all_ref[column, pl.ds(members + j, 1), :]), 1)
        rr = all_ref[column, pl.ds(2 * members + j, 1), :] * scale
        ri = all_ref[column, pl.ds(3 * members + j, 1), :] * scale
        head = cmul(wave(lead_u * fu + lead_v * hv), (rr, ri))
        lead[0] = head[0]
        lead[1] = head[1]

        now = wave((2 * lines8 + 1) * hv)
        step = cmul(tuple(wide(t[7:8]) for t in now), tuple(wide(t[0:1]) for t in now))
        seq = chebyshev(now, step, half // 8)
        for h in range(half // 16):
            for part in range(2):
                both = jnp.concatenate([seq[2 * h][part], seq[2 * h + 1][part]], axis=0)
                right[part * half + h * 16 : part * half + (h + 1) * 16, :] = both.astype(jnp.bfloat16)

        now = wave((lines8 + (start + first_a * stride)) * fu)
        step = conj_mul(tuple(wide(t[4:5]) for t in now), tuple(wide(t[0:1]) for t in now))
        step = cmul(step, step)
        seq = chebyshev(now, step, rows // 8)
        shown = []
        for h in range(rows // 8):
            cell = lines8 + (h * 8 + start)
            live = (cell >= 0) & (cell < side)
            shown.append(tuple(jnp.where(live, t, 0.0) for t in seq[h]))
        tall = min(rows, 16)
        per = 16 // tall
        if per == 2:
            table = [tuple(jnp.concatenate([t, t], axis=0).astype(jnp.bfloat16) for t in shown[0])]
        else:
            table = [
                tuple(jnp.concatenate([p, q], axis=0).astype(jnp.bfloat16) for p, q in zip(a, b))
                for a, b in zip(shown[0::2], shown[1::2])
            ]
        for f in range(0, per_group, per):
            own = tuple(
                jnp.concatenate(
                    [jnp.broadcast_to(lead[part, f + i : f + i + 1, :], (tall, lanes)) for i in range(per)], axis=0
                ).astype(jnp.bfloat16)
                for part in range(2)
            )
            for h, t in enumerate(table):
                at = f * rows + h * 16
                value = cmul(t, own)
                left[at : at + 16, :] = value[0]
                left[base + at : base + at + 16, :] = value[1]
        return off_ref[column, j, 1]

    def add(offset, left, right):
        prod = lax.dot_general(
            right[...], left[...], (((1,), (1,)), ((), ())), preferred_element_type=jnp.float32
        )
        ahead = pl.ds(offset, half)
        behind = pl.ds(WIN - offset, half)
        for k in range(chunks):
            real = slice(128 * k, 128 * (k + 1))
            imag = slice(base + 128 * k, base + 128 * (k + 1))
            front[k, ahead, :] += prod[:half, real] - prod[half:, imag]
            back[k, behind, :] += prod[:half, real] + prod[half:, imag]
            front[chunks + k, ahead, :] += prod[:half, imag] + prod[half:, real]
            back[chunks + k, behind, :] += prod[:half, imag] - prod[half:, real]

    def pair(i, offset):
        later = fill(2 * i + 1, lefts[1], rights[1])
        add(offset, lefts[0], rights[0])
        offset = fill(2 * i + 2, lefts[0], rights[0])
        add(later, lefts[1], rights[1])
        return offset

    first = fill(0, lefts[0], rights[0])
    lax.fori_loop(0, lax.div(found + 1, 2), pair, first)

    turned = 7 - row_iota(8, 128)
    for part in range(2):
        for k in range(chunks):
            x = front.at[part * chunks + k]
            y = back.at[part * chunks + k]
            ahead = [x[WIN - half : WIN], x[0:half] + x[WIN : WIN + half], x[half : WIN - half]]
            behind = []
            for at in range(WIN + half - 8, half - 8, -8):
                tile = y[at : at + 8]
                if at >= WIN:
                    tile = tile + y[at - WIN : at - WIN + 8]
                behind.append(jnp.take_along_axis(tile, turned, axis=0))
            whole = (jnp.concatenate(ahead, axis=0) + jnp.concatenate(behind, axis=0)).T
            for f in range(per_group):
                at = f * rows - 128 * k
                if 0 <= at < 128:
                    out_ref[f, part] = whole[at : at + rows]


def exchange_call(groups, columns, slot_subgrid, vis_count, offset, contributions, uv, obs, weight):
    per_group, _, members, _, side, _ = contributions.shape
    slots, lanes = weight.shape[2:]
    across = min(per_group, FACET_SIDE)
    halves = 2 if members % 2 == 0 else 1
    each = members // halves
    smem = pl.BlockSpec(memory_space=pltpu.SMEM)
    vmem = pl.BlockSpec(memory_space=pltpu.VMEM)
    dma = pltpu.SemaphoreType.DMA
    f32, bf16 = jnp.float32, jnp.bfloat16
    return pl.pallas_call(
        functools.partial(exchange_kernel, groups, columns, per_group),
        out_shape=(
            jax.ShapeDtypeStruct((columns, 4 * members, lanes), f32),
            jax.ShapeDtypeStruct((columns, members, 128), jnp.int32),
        ),
        in_specs=[smem, smem, smem, pl.BlockSpec(memory_space=pl.ANY), vmem, vmem, vmem],
        out_specs=(vmem, vmem),
        scratch_shapes=[
            pltpu.VMEM((per_group, members, 2, side, side), bf16),
            pltpu.VMEM((members, per_group // across, 2 * side, across * side), bf16),
            [pltpu.VMEM((across * side, 2 * lanes), bf16)] * 2,
            pltpu.VMEM((groups, slots, 2, lanes), f32),
            pltpu.VMEM((groups, slots, 3, lanes), f32),
            pltpu.VMEM((slots, 3, lanes), f32),
            pltpu.VMEM((members, 3, lanes), f32),
            pltpu.VMEM((columns, members, 3, lanes), f32),
            pltpu.VMEM((halves, each, 2, lanes), f32),
            pltpu.VMEM((halves, groups, each, 2, lanes), f32),
            pltpu.VMEM((halves, each, 2, lanes), bf16),
            pltpu.VMEM((columns, halves, each, 2, lanes), bf16),
            dma((members,)),
            dma((groups,)),
            dma((groups,)),
            dma((groups,)),
            dma((groups,)),
            dma((columns,)),
            dma((columns,)),
            dma((halves, groups)),
            dma((halves, groups)),
            dma((halves, columns)),
            dma((halves, columns)),
        ],
        compiler_params=pltpu.CompilerParams(collective_id=0, has_side_effects=True),
    )(slot_subgrid, vis_count, offset, contributions, uv, obs, weight)


def grid_call(offsets, gathered, per_group, side, rows, gain):
    lanes = gathered.shape[-1]
    base = -(-per_group * rows // 128) * 128
    half = side // 2
    return pl.pallas_call(
        functools.partial(grid_kernel, per_group, side, gain),
        out_shape=jax.ShapeDtypeStruct((per_group, 2, rows, WIN), jnp.float32),
        in_specs=[
            pl.BlockSpec(memory_space=pltpu.SMEM),
            pl.BlockSpec(memory_space=pltpu.VMEM),
        ],
        out_specs=pl.BlockSpec(memory_space=pltpu.VMEM),
        scratch_shapes=[
            pltpu.VMEM((base // 64, WIN + half, 128), jnp.float32),
            pltpu.VMEM((base // 64, WIN + half, 128), jnp.float32),
            [pltpu.VMEM((2 * base, lanes), jnp.bfloat16)] * 2,
            [pltpu.VMEM((2 * half, lanes), jnp.bfloat16)] * 2,
            pltpu.VMEM((2, -(-per_group // 8) * 8, lanes), jnp.float32),
            pltpu.SMEM((offsets.shape[0] * offsets.shape[1] + 8,), jnp.int32),
        ],
    )(offsets, gathered)


def body(contributions, slot_subgrid, vis_count, vis_uv, vis_obs, vis_weight, subgrid_offset):
    groups = lax.axis_size("facet")
    columns = lax.axis_size("sub")
    per_group, _, members, _, side, _ = contributions.shape
    lanes = vis_weight.shape[-1]
    gathered, offsets = exchange_call(
        groups,
        columns,
        slot_subgrid,
        vis_count,
        subgrid_offset,
        contributions,
        vis_uv,
        vis_obs,
        vis_weight,
    )
    gain = WIN / (side * math.sqrt(members * columns)) / math.sqrt(lanes)
    return grid_call(offsets, gathered, per_group, side, WIN // columns, gain)


def solution(mesh):
    placed = (
        P("facet", "sub", None, None, None, None),
        P("sub", None, None),
        P("facet", "sub", None),
        P("facet", "sub", None, None, None),
        P("facet", "sub", None, None, None),
        P("facet", "sub", None, None),
        P("sub", None, None),
    )
    return jax.shard_map(
        body, mesh=mesh, in_specs=placed, out_specs=P("facet", None, "sub", None), check_vma=False
    )
```

```python
import functools
import math

import jax
import jax.numpy as jnp
from jax import lax
from jax.experimental import pallas as pl
from jax.experimental.pallas import tpu as pltpu
from jax.sharding import PartitionSpec as P

SUBGRID = 512
FACET_SIDE = 4
WIN = 512
MESH = pl.DeviceIdType.MESH


def cmul(a, b):
    return a[0] * b[0] - a[1] * b[1], a[0] * b[1] + a[1] * b[0]


def row_iota(rows, lanes):
    return lax.broadcasted_iota(jnp.int32, (rows, lanes), 0)


SIN = (3.14159264, -5.16771008, 2.55007752, -0.59829129, 0.07765766)
COS = (1.0, -4.93480214, 4.05870916, -1.335212, 0.23493731, -0.02439632)


def fraction(w):
    t = w * (1.0 / SUBGRID)
    t = t - jnp.where(t >= 0.5, 1.0, 0.0)
    return (t * 4294967296.0).astype(jnp.int32)


def wave(phase):
    t = phase.astype(jnp.float32) * (1.0 / 4294967296.0)
    q = t * t
    s = SIN[4]
    for a in SIN[3::-1]:
        s = s * q + a
    s = s * t
    c = COS[5]
    for a in COS[4::-1]:
        c = c * q + a
    s2 = s + s
    return 1.0 - s2 * s, s2 * c


def chebyshev(first, step, count):
    double = step[0] + step[0]
    seq = [first]
    if count > 1:
        seq.append(cmul(first, step))
    while len(seq) < count:
        seq.append(tuple(double * p - q for p, q in zip(seq[-1], seq[-2])))
    return seq


def fold_matrix(across, side, stride, fold):
    rows, cols = fold.shape
    kept = cols // 2
    low = side // 128 * 128
    high = side - low
    width = (across - 1) * stride + side
    spans = [(b, y, 64) for b in range(across) for y in range(0, low, 64)]
    spans += [(b, low, high) for b in range(across)]
    lines = lax.broadcasted_iota(jnp.int32, (64, 128), 0)
    lane = lax.broadcasted_iota(jnp.int32, (64, 128), 1)
    at = 0
    for b, y, count in spans:
        turn = 2 * (b * stride + y) - (width - 1) + 2 * lines
        sign = jnp.where(turn < 0, -1.0, 1.0)
        cell = lax.shift_right_arithmetic(jnp.abs(turn), 1) - lane
        for k in range(0, kept, 128):
            hit = cell == k
            fold[at : at + count, k : k + 128] = jnp.where(hit, 1.0, 0.0)[:count].astype(jnp.bfloat16)
            fold[at : at + count, kept + k : kept + k + 128] = jnp.where(hit, sign, 0.0)[:count].astype(
                jnp.bfloat16
            )
        at += count


def fold_image(c_ref, fold, images, j):
    per_group, _, _, side, _ = c_ref.shape
    across = min(per_group, FACET_SIDE)
    low = side // 128 * 128
    kept = fold.shape[1] // 2
    for a in range(per_group // across):
        for part in range(2):
            blocks = [c_ref[a * across + b, j, part] for b in range(across)]
            strip = jnp.concatenate([x[:, :low] for x in blocks] + [x[:, low:] for x in blocks], axis=1)
            res = jnp.dot(strip, fold[...], preferred_element_type=jnp.float32)
            images[j, a, part * side : (part + 1) * side, :kept] = res[:, :kept].astype(jnp.bfloat16)
            odd = res[:, kept:] if part == 1 else -res[:, kept:]
            images[j, a, (1 - part) * side : (2 - part) * side, kept:] = odd.astype(jnp.bfloat16)


def partial_model(first_a, first_b, stride, across, u, v, images, rhs):
    kept, lanes = rhs.shape[0] // 2, rhs.shape[1]
    side = images.shape[1] // 2
    width = (across - 1) * stride + side
    lines8 = row_iota(8, lanes)
    fu = fraction(u)
    hv = lax.shift_right_arithmetic(fraction(v), 1)

    def wide(x):
        return jnp.broadcast_to(x, (8, lanes))

    now = wave((2 * lines8 + 1) * hv)
    step = cmul(tuple(wide(t[7:8]) for t in now), tuple(wide(t[0:1]) for t in now))
    seq = chebyshev(now, step, kept // 8)
    for h in range(kept // 16):
        for part in range(2):
            both = jnp.concatenate([seq[2 * h][part], seq[2 * h + 1][part]], axis=0)
            rhs[part * kept + h * 16 : part * kept + (h + 1) * 16, :] = both.astype(jnp.bfloat16)

    now = wave(lines8 * fu)
    half = tuple(wide(t[4:5]) for t in now)
    seq = chebyshev(now, cmul(half, half), side // 8)
    model_r = jnp.zeros((1, lanes), jnp.float32)
    model_i = jnp.zeros((1, lanes), jnp.float32)
    for a in range(images.shape[0]):
        res = jnp.dot(images[a], rhs[...], preferred_element_type=jnp.float32)
        total_r = jnp.zeros((8, lanes), jnp.float32)
        total_i = jnp.zeros((8, lanes), jnp.float32)
        for h in range(side // 8):
            real = res[h * 8 : (h + 1) * 8]
            imag = res[side + h * 8 : side + (h + 1) * 8]
            c, s = seq[h]
            total_r = total_r + (c * real + s * imag)
            total_i = total_i + (c * imag - s * real)
        total_r = jnp.sum(total_r, axis=0, keepdims=True)
        total_i = jnp.sum(total_i, axis=0, keepdims=True)
        c, s = wave(((first_a + a) * stride) * fu + (2 * stride * first_b + (width - 1)) * hv)
        model_r = model_r + (c * total_r + s * total_i)
        model_i = model_i + (c * total_i - s * total_r)
    return model_r * (1.0 / SUBGRID), model_i * (1.0 / SUBGRID)


def exchange_kernel(
    groups,
    columns,
    per_group,
    table_ref,
    count_ref,
    off_ref,
    c_hbm,
    uv_ref,
    obs_ref,
    weight_ref,
    phase_ref,
    where_ref,
    resid_ref,
    c_ref,
    fold,
    images,
    rhs,
    uv_all,
    ow_all,
    uv_mine,
    uv_cols,
    part_mine,
    part_all,
    resid_wide,
    resid_mine,
    c_sem,
    uv_send,
    uv_recv,
    ow_send,
    ow_recv,
    part_send,
    part_recv,
    cols_sem,
    resid_sem,
):
    members = c_ref.shape[1]
    side = c_ref.shape[-1]
    slots = uv_ref.shape[2]
    lanes = uv_ref.shape[-1]
    tiles = lanes // 128
    across = min(per_group, FACET_SIDE)
    stride = (SUBGRID - side) // (FACET_SIDE - 1)
    group = lax.axis_index("facet")
    column = lax.axis_index("sub")
    loads = [
        pltpu.make_async_copy(c_hbm.at[:, 0, j], c_ref.at[:, j], c_sem.at[j]) for j in range(members)
    ]
    for load in loads:
        load.start()

    barrier = pltpu.get_barrier_semaphore()

    def peer_group(p):
        return lax.rem(group + p, groups)

    def peer_column(p):
        return lax.rem(column + p, columns)

    @pl.loop(1, groups)
    def _(p):
        pl.semaphore_signal(barrier, inc=1, device_id={"facet": peer_group(p)}, device_id_type=MESH)

    @pl.loop(1, columns)
    def _(p):
        pl.semaphore_signal(barrier, inc=1, device_id={"sub": peer_column(p)}, device_id_type=MESH)

    lane = lax.broadcasted_iota(jnp.int32, (1, 128), 1)
    for k in range(slots):
        for i in range(tiles):
            part = slice(128 * i, 128 * (i + 1))
            for p in range(2):
                uv_all[group, (2 * k + p) * tiles + i : (2 * k + p) * tiles + i + 1, :] = uv_ref[0, 0, k, p : p + 1, part]
                ow_all[group, (3 * k + p) * tiles + i : (3 * k + p) * tiles + i + 1, :] = obs_ref[0, 0, k, p : p + 1, part]
            live = jnp.where(lane + 128 * i < count_ref[0, 0, k], 1.0, 0.0)
            at = (3 * k + 2) * tiles + i
            ow_all[group, at : at + 1, :] = weight_ref[0, 0, k : k + 1, part] * live
    pl.semaphore_wait(barrier, groups - 1 + columns - 1)

    def to_group(buf, send, recv, p):
        return pltpu.make_async_remote_copy(
            src_ref=buf.at[group],
            dst_ref=buf.at[group],
            send_sem=send.at[p],
            recv_sem=recv.at[p],
            device_id={"facet": peer_group(p)},
            device_id_type=MESH,
        )

    def each_group(buf, send, recv, act):
        @pl.loop(1, groups)
        def _(p):
            act(to_group(buf, send, recv, p))

    def send_columns(src, dst, sem):
        @pl.loop(1, columns)
        def _(p):
            pltpu.make_async_remote_copy(
                src_ref=src,
                dst_ref=dst.at[column],
                send_sem=sem.at[0],
                recv_sem=sem.at[1],
                device_id={"sub": peer_column(p)},
                device_id_type=MESH,
            ).start()

    def wait_columns(dst, sem, i):
        shown = dst.at[pl.ds(0, columns - 1)]
        pltpu.make_async_copy(shown, shown, sem.at[i]).wait()

    def start(copy):
        copy.start()

    def wait(copy):
        copy.wait()

    each_group(uv_all, uv_send, uv_recv, start)
    each_group(ow_all, ow_send, ow_recv, start)
    fold_matrix(across, side, stride, fold)
    for load in loads:
        load.wait()
    if members <= 2:
        for j in range(members):
            fold_image(c_ref, fold, images, j)
    else:

        @pl.loop(0, members)
        def _(j):
            fold_image(c_ref, fold, images, j)

    each_group(uv_all, uv_send, uv_recv, wait)

    def holds(g, k, j):
        return jnp.where(table_ref[0, g, k] == j, 1.0, 0.0)

    spots = jnp.zeros((1, 128), jnp.float32)
    for j in range(members):
        picked = jnp.zeros((2 * tiles, 128), jnp.float32)
        for g in range(groups):
            for k in range(slots):
                at = 2 * tiles * k
                picked = picked + uv_all[g, at : at + 2 * tiles, :] * holds(g, k, j)
        uv_mine[2 * tiles * j : 2 * tiles * (j + 1), :] = picked
        for axis in range(2):
            spots = jnp.where(lane == 2 * j + axis, off_ref[0, j, axis].astype(jnp.float32), spots)
    place = 2 * tiles * members
    uv_mine[place : place + 1, :] = spots
    uv_cols[column] = uv_mine[...]
    send_columns(uv_mine, uv_cols, cols_sem)

    first_a = lax.div(group * per_group, FACET_SIDE)
    first_b = lax.rem(group * per_group, FACET_SIDE)

    def models(j, slot):
        at = 2 * tiles * j
        u = jnp.concatenate([uv_mine[pl.ds(at + i, 1), :] for i in range(tiles)], axis=1)
        v = jnp.concatenate([uv_mine[pl.ds(at + tiles + i, 1), :] for i in range(tiles)], axis=1)
        both = partial_model(first_a, first_b, stride, across, u, v, images.at[j], rhs[slot])
        for p in range(2):
            for i in range(tiles):
                part_mine[pl.ds(at + p * tiles + i, 1), :] = both[p][:, 128 * i : 128 * (i + 1)]

    if members <= 2:
        for j in range(members):
            models(j, j % 2)
    else:

        @pl.loop(0, members)
        def _(j):
            models(j, 0)

    part_all[group] = part_mine[...]
    each_group(part_all, part_send, part_recv, start)
    each_group(ow_all, ow_send, ow_recv, wait)
    each_group(part_all, part_send, part_recv, wait)

    for j in range(members):
        picked = jnp.zeros((3 * tiles, 128), jnp.float32)
        model = jnp.zeros((2 * tiles, 128), jnp.float32)
        at = 2 * tiles * j
        for g in range(groups):
            model = model + part_all[g, at : at + 2 * tiles, :]
            for k in range(slots):
                first = 3 * tiles * k
                picked = picked + ow_all[g, first : first + 3 * tiles, :] * holds(g, k, j)
        weight = picked[2 * tiles :]
        weight = jnp.concatenate([weight, weight], axis=0)
        resid_wide[at : at + 2 * tiles, :] = weight * (picked[: 2 * tiles] - model)
    resid_mine[...] = resid_wide[...].astype(jnp.bfloat16)
    resid_ref[column] = resid_mine[...]
    send_columns(resid_mine, resid_ref, resid_sem)

    wait_columns(uv_cols, cols_sem, 1)
    row = row_iota(uv_cols.shape[1], 128)
    halved = lax.rem(row, 2 * tiles) >= tiles

    @pl.loop(0, columns)
    def _(c):
        full = fraction(uv_cols[c])
        phase_ref[c] = jnp.where(halved, lax.shift_right_arithmetic(full, 1), full)
        where_ref[pl.ds(c, 1), :] = uv_cols[c, place : place + 1, :].astype(jnp.int32)

    wait_columns(uv_cols, cols_sem, 0)
    wait_columns(resid_ref, resid_sem, 1)
    wait_columns(resid_ref, resid_sem, 0)


def grid_kernel(
    per_group, members, side, gain, off_ref, phase_ref, resid_ref, out_ref, front, back, lefts, rights, lead, resid_f, hits
):
    columns = phase_ref.shape[0]
    lanes = lefts[0].shape[1]
    tiles = lanes // 128
    rows = out_ref.shape[2]
    chunks = front.shape[0] // 2
    half = side // 2
    base = lefts[0].shape[0] // 2
    stride = (SUBGRID - side) // (FACET_SIDE - 1)
    facet_here = lax.axis_index("facet") * per_group
    first_line = lax.axis_index("sub") * rows
    facet_rows = lead.shape[1]
    first_a = lax.div(facet_here, FACET_SIDE)
    lines8 = row_iota(8, lanes)
    facet = row_iota(facet_rows, lanes) + facet_here
    lead_u = (lax.div(facet, FACET_SIDE) - first_a) * stride
    lead_v = lax.rem(facet, FACET_SIDE) * (2 * stride) + (side - 1)
    front[...] = jnp.zeros_like(front)
    back[...] = jnp.zeros_like(back)
    resid_f[...] = resid_ref[...].astype(jnp.float32)
    if base > per_group * rows:
        for left in lefts:
            left[...] = jnp.zeros_like(left)

    total = columns * members

    def begin(s):
        start = lax.rem(first_line - off_ref[lax.div(s, members), 2 * lax.rem(s, members)] + WIN, WIN)
        return jnp.where(start > WIN - rows, start - WIN, start)

    def scan(s, found):
        hits[found] = s
        return found + jnp.where(begin(s) < side, 1, 0)

    found = lax.fori_loop(0, total, scan, jnp.int32(0), unroll=min(total, 32))

    def wide(x):
        return jnp.broadcast_to(x, (8, lanes))

    def conj_mul(a, b):
        return a[0] * b[0] + a[1] * b[1], a[1] * b[0] - a[0] * b[1]

    def lane_row(ref, c, at):
        return jnp.concatenate([ref[c, pl.ds(at + i, 1), :] for i in range(tiles)], axis=1)

    def fill(index, left, right):
        s = jnp.where(index < found, hits[jnp.minimum(index, total - 1)], 0)
        scale = jnp.where(index < found, gain, 0.0)
        column = lax.div(s, members)
        j = lax.rem(s, members)
        start = begin(s)
        fu = lane_row(phase_ref, column, 2 * tiles * j)
        hv = lane_row(phase_ref, column, 2 * tiles * j + tiles)
        rr = lane_row(resid_f, column, 2 * tiles * j) * scale
        ri = lane_row(resid_f, column, 2 * tiles * j + tiles) * scale
        head = cmul(wave(lead_u * fu + lead_v * hv), (rr, ri))
        lead[0] = head[0]
        lead[1] = head[1]

        now = wave((2 * lines8 + 1) * hv)
        step = cmul(tuple(wide(t[7:8]) for t in now), tuple(wide(t[0:1]) for t in now))
        seq = chebyshev(now, step, half // 8)
        for h in range(half // 16):
            for part in range(2):
                both = jnp.concatenate([seq[2 * h][part], seq[2 * h + 1][part]], axis=0)
                right[part * half + h * 16 : part * half + (h + 1) * 16, :] = both.astype(jnp.bfloat16)

        now = wave((lines8 + (start + first_a * stride)) * fu)
        step = conj_mul(tuple(wide(t[4:5]) for t in now), tuple(wide(t[0:1]) for t in now))
        step = cmul(step, step)
        seq = chebyshev(now, step, rows // 8)
        shown = []
        for h in range(rows // 8):
            cell = lines8 + (h * 8 + start)
            live = (cell >= 0) & (cell < side)
            shown.append(tuple(jnp.where(live, t, 0.0) for t in seq[h]))
        tall = min(rows, 16)
        per = 16 // tall
        if per == 2:
            table = [tuple(jnp.concatenate([t, t], axis=0).astype(jnp.bfloat16) for t in shown[0])]
        else:
            table = [
                tuple(jnp.concatenate([p, q], axis=0).astype(jnp.bfloat16) for p, q in zip(a, b))
                for a, b in zip(shown[0::2], shown[1::2])
            ]
        for f in range(0, per_group, per):
            own = tuple(
                jnp.concatenate(
                    [jnp.broadcast_to(lead[part, f + i : f + i + 1, :], (tall, lanes)) for i in range(per)], axis=0
                ).astype(jnp.bfloat16)
                for part in range(2)
            )
            for h, t in enumerate(table):
                at = f * rows + h * 16
                value = cmul(t, own)
                left[at : at + 16, :] = value[0]
                left[base + at : base + at + 16, :] = value[1]
        return off_ref[column, 2 * j + 1]

    def add(offset, left, right):
        prod = lax.dot_general(
            right[...], left[...], (((1,), (1,)), ((), ())), preferred_element_type=jnp.float32
        )
        ahead = pl.ds(offset, half)
        behind = pl.ds(WIN - offset, half)
        for k in range(chunks):
            real = slice(128 * k, 128 * (k + 1))
            imag = slice(base + 128 * k, base + 128 * (k + 1))
            front[k, ahead, :] += prod[:half, real] - prod[half:, imag]
            back[k, behind, :] += prod[:half, real] + prod[half:, imag]
            front[chunks + k, ahead, :] += prod[:half, imag] + prod[half:, real]
            back[chunks + k, behind, :] += prod[:half, imag] - prod[half:, real]

    def pair(i, offset):
        later = fill(2 * i + 1, lefts[1], rights[1])
        add(offset, lefts[0], rights[0])
        offset = fill(2 * i + 2, lefts[0], rights[0])
        add(later, lefts[1], rights[1])
        return offset

    first = fill(0, lefts[0], rights[0])
    lax.fori_loop(0, lax.div(found + 1, 2), pair, first)

    turned = 7 - row_iota(8, 128)
    for part in range(2):
        for k in range(chunks):
            x = front.at[part * chunks + k]
            y = back.at[part * chunks + k]
            ahead = [x[WIN - half : WIN], x[0:half] + x[WIN : WIN + half], x[half : WIN - half]]
            behind = []
            for at in range(WIN + half - 8, half - 8, -8):
                tile = y[at : at + 8]
                if at >= WIN:
                    tile = tile + y[at - WIN : at - WIN + 8]
                behind.append(jnp.take_along_axis(tile, turned, axis=0))
            whole = (jnp.concatenate(ahead, axis=0) + jnp.concatenate(behind, axis=0)).T
            for f in range(per_group):
                at = f * rows - 128 * k
                if 0 <= at < 128:
                    out_ref[f, part] = whole[at : at + rows]


def exchange_call(groups, columns, slot_subgrid, vis_count, offset, contributions, uv, obs, weight):
    per_group, _, members, _, side, _ = contributions.shape
    slots, lanes = weight.shape[2:]
    tiles = lanes // 128
    across = min(per_group, FACET_SIDE)
    width = (SUBGRID - side) // (FACET_SIDE - 1) * (across - 1) + side
    kept = -(-width // 256) * 128
    smem = pl.BlockSpec(memory_space=pltpu.SMEM)
    vmem = pl.BlockSpec(memory_space=pltpu.VMEM)
    dma = pltpu.SemaphoreType.DMA
    f32, bf16 = jnp.float32, jnp.bfloat16

    def rows(n, unit=8):
        return -(-n // unit) * unit

    uv_rows = rows(2 * members * tiles + 1)
    resid_rows = rows(2 * members * tiles, 16)
    return pl.pallas_call(
        functools.partial(exchange_kernel, groups, columns, per_group),
        out_shape=(
            jax.ShapeDtypeStruct((columns, uv_rows, 128), jnp.int32),
            jax.ShapeDtypeStruct((columns, 128), jnp.int32),
            jax.ShapeDtypeStruct((columns, resid_rows, 128), bf16),
        ),
        in_specs=[smem, smem, smem, pl.BlockSpec(memory_space=pl.ANY), vmem, vmem, vmem],
        out_specs=(vmem, vmem, vmem),
        scratch_shapes=[
            pltpu.VMEM((per_group, members, 2, side, side), bf16),
            pltpu.VMEM((across * side, 2 * kept), bf16),
            pltpu.VMEM((members, per_group // across, 2 * side, 2 * kept), bf16),
            [pltpu.VMEM((2 * kept, lanes), bf16)] * 2,
            pltpu.VMEM((groups, rows(2 * slots * tiles), 128), f32),
            pltpu.VMEM((groups, rows(3 * slots * tiles), 128), f32),
            pltpu.VMEM((uv_rows, 128), f32),
            pltpu.VMEM((columns, uv_rows, 128), f32),
            pltpu.VMEM((rows(2 * members * tiles), 128), f32),
            pltpu.VMEM((groups, rows(2 * members * tiles), 128), f32),
            pltpu.VMEM((resid_rows, 128), f32),
            pltpu.VMEM((resid_rows, 128), bf16),
            dma((members,)),
            dma((groups,)),
            dma((groups,)),
            dma((groups,)),
            dma((groups,)),
            dma((groups,)),
            dma((groups,)),
            dma((2,)),
            dma((2,)),
        ],
        compiler_params=pltpu.CompilerParams(collective_id=0, has_side_effects=True),
    )(slot_subgrid, vis_count, offset, contributions, uv, obs, weight)


def grid_call(phases, offsets, resid, per_group, members, lanes, side, rows, gain):
    base = -(-per_group * rows // 128) * 128
    half = side // 2
    return pl.pallas_call(
        functools.partial(grid_kernel, per_group, members, side, gain),
        out_shape=jax.ShapeDtypeStruct((per_group, 2, rows, WIN), jnp.float32),
        in_specs=[
            pl.BlockSpec(memory_space=pltpu.SMEM),
            pl.BlockSpec(memory_space=pltpu.VMEM),
            pl.BlockSpec(memory_space=pltpu.VMEM),
        ],
        out_specs=pl.BlockSpec(memory_space=pltpu.VMEM),
        scratch_shapes=[
            pltpu.VMEM((base // 64, WIN + half, 128), jnp.float32),
            pltpu.VMEM((base // 64, WIN + half, 128), jnp.float32),
            [pltpu.VMEM((2 * base, lanes), jnp.bfloat16)] * 2,
            [pltpu.VMEM((2 * half, lanes), jnp.bfloat16)] * 2,
            pltpu.VMEM((2, -(-per_group // 8) * 8, lanes), jnp.float32),
            pltpu.VMEM(resid.shape, jnp.float32),
            pltpu.SMEM((offsets.shape[0] * members + 8,), jnp.int32),
        ],
    )(offsets, phases, resid)


def body(contributions, slot_subgrid, vis_count, vis_uv, vis_obs, vis_weight, subgrid_offset):
    groups = lax.axis_size("facet")
    columns = lax.axis_size("sub")
    per_group, _, members, _, side, _ = contributions.shape
    lanes = vis_weight.shape[-1]
    phases, offsets, resid = exchange_call(
        groups,
        columns,
        slot_subgrid,
        vis_count,
        subgrid_offset,
        contributions,
        vis_uv,
        vis_obs,
        vis_weight,
    )
    gain = WIN / (side * math.sqrt(members * columns)) / math.sqrt(lanes)
    return grid_call(phases, offsets, resid, per_group, members, lanes, side, WIN // columns, gain)


def solution(mesh):
    placed = (
        P("facet", "sub", None, None, None, None),
        P("sub", None, None),
        P("facet", "sub", None),
        P("facet", "sub", None, None, None),
        P("facet", "sub", None, None, None),
        P("facet", "sub", None, None),
        P("sub", None, None),
    )
    return jax.shard_map(
        body, mesh=mesh, in_specs=placed, out_specs=P("facet", None, "sub", None), check_vma=False
    )
```

```python
import functools
import math

import jax
import jax.numpy as jnp
from jax import lax
from jax.experimental import pallas as pl
from jax.experimental.pallas import tpu as pltpu
from jax.sharding import PartitionSpec as P

SUBGRID = 512
FACET_SIDE = 4
WIN = 512
MESH = pl.DeviceIdType.MESH


def cmul(a, b):
    return a[0] * b[0] - a[1] * b[1], a[0] * b[1] + a[1] * b[0]


def row_iota(rows, lanes):
    return lax.broadcasted_iota(jnp.int32, (rows, lanes), 0)


SIN = (3.14159264, -5.16771008, 2.55007752, -0.59829129, 0.07765766)
COS = (1.0, -4.93480214, 4.05870916, -1.335212, 0.23493731, -0.02439632)


def fraction(w):
    t = w * (1.0 / SUBGRID)
    t = t - jnp.where(t >= 0.5, 1.0, 0.0)
    return (t * 4294967296.0).astype(jnp.int32)


def wave(phase):
    t = phase.astype(jnp.float32) * (1.0 / 4294967296.0)
    q = t * t
    s = SIN[4]
    for a in SIN[3::-1]:
        s = s * q + a
    s = s * t
    c = COS[5]
    for a in COS[4::-1]:
        c = c * q + a
    s2 = s + s
    return 1.0 - s2 * s, s2 * c


def chebyshev(first, step, count):
    double = step[0] + step[0]
    seq = [first]
    if count > 1:
        seq.append(cmul(first, step))
    while len(seq) < count:
        seq.append(tuple(double * p - q for p, q in zip(seq[-1], seq[-2])))
    return seq


def fold_matrix(across, side, stride, fold):
    rows, cols = fold.shape
    kept = cols // 2
    low = side // 128 * 128
    high = side - low
    width = (across - 1) * stride + side
    spans = [(b, y, 64) for b in range(across) for y in range(0, low, 64)]
    spans += [(b, low, high) for b in range(across)]
    lines = lax.broadcasted_iota(jnp.int32, (64, 128), 0)
    lane = lax.broadcasted_iota(jnp.int32, (64, 128), 1)
    at = 0
    for b, y, count in spans:
        turn = 2 * (b * stride + y) - (width - 1) + 2 * lines
        sign = jnp.where(turn < 0, -1.0, 1.0)
        cell = lax.shift_right_arithmetic(jnp.abs(turn), 1) - lane
        for k in range(0, kept, 128):
            hit = cell == k
            fold[at : at + count, k : k + 128] = jnp.where(hit, 1.0, 0.0)[:count].astype(jnp.bfloat16)
            fold[at : at + count, kept + k : kept + k + 128] = jnp.where(hit, sign, 0.0)[:count].astype(
                jnp.bfloat16
            )
        at += count


def fold_image(c_ref, fold, images, j):
    per_group, _, _, side, _ = c_ref.shape
    across = min(per_group, FACET_SIDE)
    low = side // 128 * 128
    kept = fold.shape[1] // 2
    for a in range(per_group // across):
        for part in range(2):
            blocks = [c_ref[a * across + b, j, part] for b in range(across)]
            strip = jnp.concatenate([x[:, :low] for x in blocks] + [x[:, low:] for x in blocks], axis=1)
            res = jnp.dot(strip, fold[...], preferred_element_type=jnp.float32)
            images[j, a, part * side : (part + 1) * side, :kept] = res[:, :kept].astype(jnp.bfloat16)
            odd = res[:, kept:] if part == 1 else -res[:, kept:]
            images[j, a, (1 - part) * side : (2 - part) * side, kept:] = odd.astype(jnp.bfloat16)


def partial_model(first_a, first_b, stride, across, u, v, images, rhs):
    kept, lanes = rhs.shape[0] // 2, rhs.shape[1]
    side = images.shape[1] // 2
    width = (across - 1) * stride + side
    lines8 = row_iota(8, lanes)
    fu = fraction(u)
    hv = lax.shift_right_arithmetic(fraction(v), 1)

    def wide(x):
        return jnp.broadcast_to(x, (8, lanes))

    now = wave((2 * lines8 + 1) * hv)
    step = cmul(tuple(wide(t[7:8]) for t in now), tuple(wide(t[0:1]) for t in now))
    seq = chebyshev(now, step, kept // 8)
    for h in range(kept // 16):
        for part in range(2):
            both = jnp.concatenate([seq[2 * h][part], seq[2 * h + 1][part]], axis=0)
            rhs[part * kept + h * 16 : part * kept + (h + 1) * 16, :] = both.astype(jnp.bfloat16)

    now = wave(lines8 * fu)
    half = tuple(wide(t[4:5]) for t in now)
    seq = chebyshev(now, cmul(half, half), side // 8)
    model_r = jnp.zeros((1, lanes), jnp.float32)
    model_i = jnp.zeros((1, lanes), jnp.float32)
    for a in range(images.shape[0]):
        res = jnp.dot(images[a], rhs[...], preferred_element_type=jnp.float32)
        total_r = jnp.zeros((8, lanes), jnp.float32)
        total_i = jnp.zeros((8, lanes), jnp.float32)
        for h in range(side // 8):
            real = res[h * 8 : (h + 1) * 8]
            imag = res[side + h * 8 : side + (h + 1) * 8]
            c, s = seq[h]
            total_r = total_r + (c * real + s * imag)
            total_i = total_i + (c * imag - s * real)
        total_r = jnp.sum(total_r, axis=0, keepdims=True)
        total_i = jnp.sum(total_i, axis=0, keepdims=True)
        c, s = wave(((first_a + a) * stride) * fu + (2 * stride * first_b + (width - 1)) * hv)
        model_r = model_r + (c * total_r + s * total_i)
        model_i = model_i + (c * total_i - s * total_r)
    return model_r * (1.0 / SUBGRID), model_i * (1.0 / SUBGRID)


def exchange_kernel(
    groups,
    columns,
    per_group,
    table_hbm,
    count_hbm,
    off_hbm,
    c_hbm,
    uv_hbm,
    obs_hbm,
    weight_hbm,
    phase_ref,
    where_ref,
    resid_ref,
    table_ref,
    count_ref,
    off_ref,
    uv_ref,
    obs_ref,
    weight_ref,
    c_ref,
    fold,
    images,
    rhs,
    uv_all,
    ow_all,
    uv_mine,
    uv_cols,
    part_mine,
    part_all,
    resid_wide,
    resid_mine,
    in_sem,
    c_sem,
    known,
    uv_send,
    uv_recv,
    ow_send,
    ow_recv,
    part_send,
    part_recv,
    cols_sem,
    resid_sem,
):
    members = c_ref.shape[1]
    side = c_ref.shape[-1]
    slots = uv_ref.shape[2]
    lanes = uv_ref.shape[-1]
    tiles = lanes // 128
    across = min(per_group, FACET_SIDE)
    stride = (SUBGRID - side) // (FACET_SIDE - 1)
    group = lax.axis_index("facet")
    column = lax.axis_index("sub")
    barrier = pltpu.get_barrier_semaphore()
    rounds = columns.bit_length() - 1
    paired = columns == 1 << rounds

    def peer_group(p):
        return lax.rem(group + p, groups)

    def peer_column(p):
        return lax.rem(column + p, columns)

    def partner(r):
        bit = 1 << r
        return column + bit - 2 * bit * lax.rem(lax.div(column, bit), 2)

    for p in range(1, groups):
        pl.semaphore_signal(barrier, inc=1, device_id={"facet": peer_group(p)}, device_id_type=MESH)
    near = [partner(r) for r in range(rounds)] if paired else [peer_column(p) for p in range(1, columns)]
    for other in near:
        pl.semaphore_signal(barrier, inc=1, device_id={"sub": other}, device_id_type=MESH)

    def tell(r):
        if paired and 1 <= r < rounds:
            pl.semaphore_signal(known.at[r], inc=1, device_id={"sub": partner(r)}, device_id_type=MESH)

    def hear(r):
        if paired and 1 <= r < rounds:
            pl.semaphore_wait(known.at[r], 1)

    smalls = [
        pltpu.make_async_copy(src, dst, in_sem.at[i])
        for i, (src, dst) in enumerate(
            (
                (uv_hbm, uv_ref),
                (count_hbm, count_ref),
                (obs_hbm, obs_ref),
                (weight_hbm, weight_ref),
                (table_hbm, table_ref),
                (off_hbm, off_ref),
            )
        )
    ]
    loads = [
        pltpu.make_async_copy(c_hbm.at[:, 0, j], c_ref.at[:, j], c_sem.at[j]) for j in range(members)
    ]
    for load in smalls + loads:
        load.start()
    fold_matrix(across, side, stride, fold)
    for load in smalls:
        load.wait()

    lane = lax.broadcasted_iota(jnp.int32, (1, 128), 1)
    for k in range(slots):
        for i in range(tiles):
            part = slice(128 * i, 128 * (i + 1))
            for p in range(2):
                uv_all[group, (2 * k + p) * tiles + i : (2 * k + p) * tiles + i + 1, :] = uv_ref[0, 0, k, p : p + 1, part]
                ow_all[group, (3 * k + p) * tiles + i : (3 * k + p) * tiles + i + 1, :] = obs_ref[0, 0, k, p : p + 1, part]
            live = jnp.where(lane + 128 * i < count_ref[0, 0, k], 1.0, 0.0)
            at = (3 * k + 2) * tiles + i
            ow_all[group, at : at + 1, :] = weight_ref[0, 0, k : k + 1, part] * live
    pl.semaphore_wait(barrier, groups - 1 + len(near))
    tell(1)

    def to_group(buf, send, recv, p):
        return pltpu.make_async_remote_copy(
            src_ref=buf.at[group],
            dst_ref=buf.at[group],
            send_sem=send.at[p],
            recv_sem=recv.at[p],
            device_id={"facet": peer_group(p)},
            device_id_type=MESH,
        )

    def each_group(buf, send, recv, act):
        @pl.loop(1, groups)
        def _(p):
            act(to_group(buf, send, recv, p))

    def send_columns(src, dst, sem):
        @pl.loop(1, columns)
        def _(p):
            pltpu.make_async_remote_copy(
                src_ref=src,
                dst_ref=dst.at[column],
                send_sem=sem.at[0],
                recv_sem=sem.at[1],
                device_id={"sub": peer_column(p)},
                device_id_type=MESH,
            ).start()

    def wait_columns(dst, sem, i):
        shown = dst.at[pl.ds(0, columns - 1)]
        pltpu.make_async_copy(shown, shown, sem.at[i]).wait()

    def start(copy):
        copy.start()

    def wait(copy):
        copy.wait()

    each_group(uv_all, uv_send, uv_recv, start)
    each_group(ow_all, ow_send, ow_recv, start)
    for load in loads:
        load.wait()
    if members <= 2:
        for j in range(members):
            fold_image(c_ref, fold, images, j)
    else:

        @pl.loop(0, members)
        def _(j):
            fold_image(c_ref, fold, images, j)

    each_group(uv_all, uv_send, uv_recv, wait)

    def holds(g, k, j):
        return jnp.where(table_ref[0, g, k] == j, 1.0, 0.0)

    spots = jnp.zeros((1, 128), jnp.float32)
    for j in range(members):
        picked = jnp.zeros((2 * tiles, 128), jnp.float32)
        for g in range(groups):
            for k in range(slots):
                at = 2 * tiles * k
                picked = picked + uv_all[g, at : at + 2 * tiles, :] * holds(g, k, j)
        uv_mine[2 * tiles * j : 2 * tiles * (j + 1), :] = picked
        for axis in range(2):
            spots = jnp.where(lane == 2 * j + axis, off_ref[0, j, axis].astype(jnp.float32), spots)
    place = 2 * tiles * members
    uv_mine[place : place + 1, :] = spots
    uv_cols[column] = uv_mine[...]
    hear(1)
    tell(2)

    first_a = lax.div(group * per_group, FACET_SIDE)
    first_b = lax.rem(group * per_group, FACET_SIDE)

    def models(j, slot):
        at = 2 * tiles * j
        u = jnp.concatenate([uv_mine[pl.ds(at + i, 1), :] for i in range(tiles)], axis=1)
        v = jnp.concatenate([uv_mine[pl.ds(at + tiles + i, 1), :] for i in range(tiles)], axis=1)
        both = partial_model(first_a, first_b, stride, across, u, v, images.at[j], rhs[slot])
        for p in range(2):
            for i in range(tiles):
                part_mine[pl.ds(at + p * tiles + i, 1), :] = both[p][:, 128 * i : 128 * (i + 1)]

    if members <= 2:
        for j in range(members):
            models(j, j % 2)
    else:

        @pl.loop(0, members)
        def _(j):
            models(j, 0)

    part_all[group] = part_mine[...]
    each_group(part_all, part_send, part_recv, start)
    for r in range(2, rounds):
        hear(r)
        tell(r + 1)
    send_columns(uv_mine, uv_cols, cols_sem)
    each_group(ow_all, ow_send, ow_recv, wait)
    each_group(part_all, part_send, part_recv, wait)

    for j in range(members):
        picked = jnp.zeros((3 * tiles, 128), jnp.float32)
        model = jnp.zeros((2 * tiles, 128), jnp.float32)
        at = 2 * tiles * j
        for g in range(groups):
            model = model + part_all[g, at : at + 2 * tiles, :]
            for k in range(slots):
                first = 3 * tiles * k
                picked = picked + ow_all[g, first : first + 3 * tiles, :] * holds(g, k, j)
        weight = picked[2 * tiles :]
        weight = jnp.concatenate([weight, weight], axis=0)
        resid_wide[at : at + 2 * tiles, :] = weight * (picked[: 2 * tiles] - model)
    resid_mine[...] = resid_wide[...].astype(jnp.bfloat16)
    resid_ref[column] = resid_mine[...]
    send_columns(resid_mine, resid_ref, resid_sem)

    wait_columns(uv_cols, cols_sem, 1)
    row = row_iota(uv_cols.shape[1], 128)
    halved = lax.rem(row, 2 * tiles) >= tiles

    @pl.loop(0, columns)
    def _(c):
        full = fraction(uv_cols[c])
        phase_ref[c] = jnp.where(halved, lax.shift_right_arithmetic(full, 1), full)
        where_ref[pl.ds(c, 1), :] = uv_cols[c, place : place + 1, :].astype(jnp.int32)

    wait_columns(uv_cols, cols_sem, 0)
    wait_columns(resid_ref, resid_sem, 1)
    wait_columns(resid_ref, resid_sem, 0)


def grid_kernel(
    per_group, members, side, gain, off_ref, phase_ref, resid_ref, out_ref, front, back, lefts, rights, lead, resid_f, hits
):
    columns = phase_ref.shape[0]
    lanes = lefts[0].shape[1]
    tiles = lanes // 128
    rows = out_ref.shape[2]
    chunks = front.shape[0] // 2
    half = side // 2
    base = lefts[0].shape[0] // 2
    stride = (SUBGRID - side) // (FACET_SIDE - 1)
    facet_here = lax.axis_index("facet") * per_group
    first_line = lax.axis_index("sub") * rows
    facet_rows = lead.shape[1]
    first_a = lax.div(facet_here, FACET_SIDE)
    lines8 = row_iota(8, lanes)
    facet = row_iota(facet_rows, lanes) + facet_here
    lead_u = (lax.div(facet, FACET_SIDE) - first_a) * stride
    lead_v = lax.rem(facet, FACET_SIDE) * (2 * stride) + (side - 1)
    front[...] = jnp.zeros_like(front)
    back[...] = jnp.zeros_like(back)
    resid_f[...] = resid_ref[...].astype(jnp.float32)
    if base > per_group * rows:
        for left in lefts:
            left[...] = jnp.zeros_like(left)

    total = columns * members

    def begin(s):
        start = lax.rem(first_line - off_ref[lax.div(s, members), 2 * lax.rem(s, members)] + WIN, WIN)
        return jnp.where(start > WIN - rows, start - WIN, start)

    def scan(s, found):
        hits[found] = s
        return found + jnp.where(begin(s) < side, 1, 0)

    found = lax.fori_loop(0, total, scan, jnp.int32(0), unroll=min(total, 32))

    def wide(x):
        return jnp.broadcast_to(x, (8, lanes))

    def conj_mul(a, b):
        return a[0] * b[0] + a[1] * b[1], a[1] * b[0] - a[0] * b[1]

    def lane_row(ref, c, at):
        return jnp.concatenate([ref[c, pl.ds(at + i, 1), :] for i in range(tiles)], axis=1)

    def fill(index, left, right):
        s = jnp.where(index < found, hits[jnp.minimum(index, total - 1)], 0)
        scale = jnp.where(index < found, gain, 0.0)
        column = lax.div(s, members)
        j = lax.rem(s, members)
        start = begin(s)
        fu = lane_row(phase_ref, column, 2 * tiles * j)
        hv = lane_row(phase_ref, column, 2 * tiles * j + tiles)
        rr = lane_row(resid_f, column, 2 * tiles * j) * scale
        ri = lane_row(resid_f, column, 2 * tiles * j + tiles) * scale
        head = cmul(wave(lead_u * fu + lead_v * hv), (rr, ri))
        lead[0] = head[0]
        lead[1] = head[1]

        now = wave((2 * lines8 + 1) * hv)
        step = cmul(tuple(wide(t[7:8]) for t in now), tuple(wide(t[0:1]) for t in now))
        seq = chebyshev(now, step, half // 8)
        for h in range(half // 16):
            for part in range(2):
                both = jnp.concatenate([seq[2 * h][part], seq[2 * h + 1][part]], axis=0)
                right[part * half + h * 16 : part * half + (h + 1) * 16, :] = both.astype(jnp.bfloat16)

        now = wave((lines8 + (start + first_a * stride)) * fu)
        step = conj_mul(tuple(wide(t[4:5]) for t in now), tuple(wide(t[0:1]) for t in now))
        step = cmul(step, step)
        seq = chebyshev(now, step, rows // 8)
        shown = []
        for h in range(rows // 8):
            cell = lines8 + (h * 8 + start)
            live = (cell >= 0) & (cell < side)
            shown.append(tuple(jnp.where(live, t, 0.0) for t in seq[h]))
        tall = min(rows, 16)
        per = 16 // tall
        if per == 2:
            table = [tuple(jnp.concatenate([t, t], axis=0).astype(jnp.bfloat16) for t in shown[0])]
        else:
            table = [
                tuple(jnp.concatenate([p, q], axis=0).astype(jnp.bfloat16) for p, q in zip(a, b))
                for a, b in zip(shown[0::2], shown[1::2])
            ]
        for f in range(0, per_group, per):
            own = tuple(
                jnp.concatenate(
                    [jnp.broadcast_to(lead[part, f + i : f + i + 1, :], (tall, lanes)) for i in range(per)], axis=0
                ).astype(jnp.bfloat16)
                for part in range(2)
            )
            for h, t in enumerate(table):
                at = f * rows + h * 16
                value = cmul(t, own)
                left[at : at + 16, :] = value[0]
                left[base + at : base + at + 16, :] = value[1]
        return off_ref[column, 2 * j + 1]

    def add(offset, left, right):
        prod = lax.dot_general(
            right[...], left[...], (((1,), (1,)), ((), ())), preferred_element_type=jnp.float32
        )
        ahead = pl.ds(offset, half)
        behind = pl.ds(WIN - offset, half)
        for k in range(chunks):
            real = slice(128 * k, 128 * (k + 1))
            imag = slice(base + 128 * k, base + 128 * (k + 1))
            front[k, ahead, :] += prod[:half, real] - prod[half:, imag]
            back[k, behind, :] += prod[:half, real] + prod[half:, imag]
            front[chunks + k, ahead, :] += prod[:half, imag] + prod[half:, real]
            back[chunks + k, behind, :] += prod[:half, imag] - prod[half:, real]

    def pair(i, offset):
        later = fill(2 * i + 1, lefts[1], rights[1])
        add(offset, lefts[0], rights[0])
        offset = fill(2 * i + 2, lefts[0], rights[0])
        add(later, lefts[1], rights[1])
        return offset

    first = fill(0, lefts[0], rights[0])
    lax.fori_loop(0, lax.div(found + 1, 2), pair, first)

    turned = 7 - row_iota(8, 128)
    for part in range(2):
        for k in range(chunks):
            x = front.at[part * chunks + k]
            y = back.at[part * chunks + k]
            ahead = [x[WIN - half : WIN], x[0:half] + x[WIN : WIN + half], x[half : WIN - half]]
            behind = []
            for at in range(WIN + half - 8, half - 8, -8):
                tile = y[at : at + 8]
                if at >= WIN:
                    tile = tile + y[at - WIN : at - WIN + 8]
                behind.append(jnp.take_along_axis(tile, turned, axis=0))
            whole = (jnp.concatenate(ahead, axis=0) + jnp.concatenate(behind, axis=0)).T
            for f in range(per_group):
                at = f * rows - 128 * k
                if 0 <= at < 128:
                    out_ref[f, part] = whole[at : at + rows]


def exchange_call(groups, columns, slot_subgrid, vis_count, offset, contributions, uv, obs, weight):
    per_group, _, members, _, side, _ = contributions.shape
    slots, lanes = weight.shape[2:]
    tiles = lanes // 128
    across = min(per_group, FACET_SIDE)
    width = (SUBGRID - side) // (FACET_SIDE - 1) * (across - 1) + side
    kept = -(-width // 256) * 128
    vmem = pl.BlockSpec(memory_space=pltpu.VMEM)
    dma = pltpu.SemaphoreType.DMA
    f32, bf16 = jnp.float32, jnp.bfloat16

    def rows(n, unit=8):
        return -(-n // unit) * unit

    uv_rows = 2 * members * tiles + 1
    resid_rows = rows(2 * members * tiles, 16)
    return pl.pallas_call(
        functools.partial(exchange_kernel, groups, columns, per_group),
        out_shape=(
            jax.ShapeDtypeStruct((columns, uv_rows, 128), jnp.int32),
            jax.ShapeDtypeStruct((columns, 128), jnp.int32),
            jax.ShapeDtypeStruct((columns, resid_rows, 128), bf16),
        ),
        in_specs=[pl.BlockSpec(memory_space=pl.ANY)] * 7,
        out_specs=(vmem, vmem, vmem),
        scratch_shapes=[
            pltpu.SMEM(slot_subgrid.shape, jnp.int32),
            pltpu.SMEM(vis_count.shape, jnp.int32),
            pltpu.SMEM(offset.shape, jnp.int32),
            pltpu.VMEM(uv.shape, f32),
            pltpu.VMEM(obs.shape, f32),
            pltpu.VMEM(weight.shape, f32),
            pltpu.VMEM((per_group, members, 2, side, side), bf16),
            pltpu.VMEM((across * side, 2 * kept), bf16),
            pltpu.VMEM((members, per_group // across, 2 * side, 2 * kept), bf16),
            [pltpu.VMEM((2 * kept, lanes), bf16)] * 2,
            pltpu.VMEM((groups, rows(2 * slots * tiles), 128), f32),
            pltpu.VMEM((groups, rows(3 * slots * tiles), 128), f32),
            pltpu.VMEM((uv_rows, 128), f32),
            pltpu.VMEM((columns, uv_rows, 128), f32),
            pltpu.VMEM((rows(2 * members * tiles), 128), f32),
            pltpu.VMEM((groups, rows(2 * members * tiles), 128), f32),
            pltpu.VMEM((resid_rows, 128), f32),
            pltpu.VMEM((resid_rows, 128), bf16),
            dma((6,)),
            dma((members,)),
            pltpu.SemaphoreType.REGULAR((max(columns.bit_length(), 1),)),
            dma((groups,)),
            dma((groups,)),
            dma((groups,)),
            dma((groups,)),
            dma((groups,)),
            dma((groups,)),
            dma((2,)),
            dma((2,)),
        ],
        compiler_params=pltpu.CompilerParams(collective_id=0, has_side_effects=True),
    )(slot_subgrid, vis_count, offset, contributions, uv, obs, weight)


def grid_call(phases, offsets, resid, per_group, members, lanes, side, rows, gain):
    base = -(-per_group * rows // 128) * 128
    half = side // 2
    return pl.pallas_call(
        functools.partial(grid_kernel, per_group, members, side, gain),
        out_shape=jax.ShapeDtypeStruct((per_group, 2, rows, WIN), jnp.float32),
        in_specs=[
            pl.BlockSpec(memory_space=pltpu.SMEM),
            pl.BlockSpec(memory_space=pltpu.VMEM),
            pl.BlockSpec(memory_space=pltpu.VMEM),
        ],
        out_specs=pl.BlockSpec(memory_space=pltpu.VMEM),
        scratch_shapes=[
            pltpu.VMEM((base // 64, WIN + half, 128), jnp.float32),
            pltpu.VMEM((base // 64, WIN + half, 128), jnp.float32),
            [pltpu.VMEM((2 * base, lanes), jnp.bfloat16)] * 2,
            [pltpu.VMEM((2 * half, lanes), jnp.bfloat16)] * 2,
            pltpu.VMEM((2, -(-per_group // 8) * 8, lanes), jnp.float32),
            pltpu.VMEM(resid.shape, jnp.float32),
            pltpu.SMEM((offsets.shape[0] * members + 8,), jnp.int32),
        ],
    )(offsets, phases, resid)


def body(contributions, slot_subgrid, vis_count, vis_uv, vis_obs, vis_weight, subgrid_offset):
    groups = lax.axis_size("facet")
    columns = lax.axis_size("sub")
    per_group, _, members, _, side, _ = contributions.shape
    lanes = vis_weight.shape[-1]
    phases, offsets, resid = exchange_call(
        groups,
        columns,
        slot_subgrid,
        vis_count,
        subgrid_offset,
        contributions,
        vis_uv,
        vis_obs,
        vis_weight,
    )
    gain = WIN / (side * math.sqrt(members * columns)) / math.sqrt(lanes)
    return grid_call(phases, offsets, resid, per_group, members, lanes, side, WIN // columns, gain)


def solution(mesh):
    placed = (
        P("facet", "sub", None, None, None, None),
        P("sub", None, None),
        P("facet", "sub", None),
        P("facet", "sub", None, None, None),
        P("facet", "sub", None, None, None),
        P("facet", "sub", None, None),
        P("sub", None, None),
    )
    return jax.shard_map(
        body, mesh=mesh, in_specs=placed, out_specs=P("facet", None, "sub", None), check_vma=False
    )
```

```python
import functools
import math

import jax
import jax.numpy as jnp
from jax import lax
from jax.experimental import pallas as pl
from jax.experimental.pallas import tpu as pltpu
from jax.sharding import PartitionSpec as P

SUBGRID = 512
FACET_SIDE = 4
WIN = 512
MESH = pl.DeviceIdType.MESH


def cmul(a, b):
    return a[0] * b[0] - a[1] * b[1], a[0] * b[1] + a[1] * b[0]


def row_iota(rows, lanes):
    return lax.broadcasted_iota(jnp.int32, (rows, lanes), 0)


SIN = (3.14159027, -5.16740673, 2.54401052, -0.55946246)
COS = (0.99999995, -4.93479283, 4.05841135, -1.33187657, 0.21968961)


def fraction(w):
    t = w * (1.0 / SUBGRID)
    t = t - jnp.where(t >= 0.5, 1.0, 0.0)
    return (t * 4294967296.0).astype(jnp.int32)


def wave(phase):
    t = phase.astype(jnp.float32) * (1.0 / 4294967296.0)
    q = t * t
    s = SIN[3]
    for a in SIN[2::-1]:
        s = s * q + a
    s = s * t
    c = COS[4]
    for a in COS[3::-1]:
        c = c * q + a
    s2 = s + s
    return 1.0 - s2 * s, s2 * c


def chebyshev(first, step, count):
    double = step[0] + step[0]
    seq = [first]
    if count > 1:
        seq.append(cmul(first, step))
    while len(seq) < count:
        seq.append(tuple(double * p - q for p, q in zip(seq[-1], seq[-2])))
    return seq


def fold_matrix(across, side, stride, fold):
    rows, cols = fold.shape
    kept = cols // 2
    low = side // 128 * 128
    high = side - low
    width = (across - 1) * stride + side
    spans = [(b, y, 64) for b in range(across) for y in range(0, low, 64)]
    spans += [(b, low, high) for b in range(across)]
    lines = lax.broadcasted_iota(jnp.int32, (64, 128), 0)
    lane = lax.broadcasted_iota(jnp.int32, (64, 128), 1)
    at = 0
    for b, y, count in spans:
        turn = 2 * (b * stride + y) - (width - 1) + 2 * lines
        sign = jnp.where(turn < 0, -1.0, 1.0)
        cell = lax.shift_right_arithmetic(jnp.abs(turn), 1) - lane
        for k in range(0, kept, 128):
            hit = cell == k
            fold[at : at + count, k : k + 128] = jnp.where(hit, 1.0, 0.0)[:count].astype(jnp.bfloat16)
            fold[at : at + count, kept + k : kept + k + 128] = jnp.where(hit, sign, 0.0)[:count].astype(
                jnp.bfloat16
            )
        at += count


def fold_image(c_ref, fold, images, j):
    per_group, _, _, side, _ = c_ref.shape
    across = min(per_group, FACET_SIDE)
    low = side // 128 * 128
    kept = fold.shape[1] // 2
    for a in range(per_group // across):
        for part in range(2):
            blocks = [c_ref[a * across + b, j, part] for b in range(across)]
            strip = jnp.concatenate([x[:, :low] for x in blocks] + [x[:, low:] for x in blocks], axis=1)
            res = jnp.dot(strip, fold[...], preferred_element_type=jnp.float32)
            images[j, a, part * side : (part + 1) * side, :kept] = res[:, :kept].astype(jnp.bfloat16)
            odd = res[:, kept:] if part == 1 else -res[:, kept:]
            images[j, a, (1 - part) * side : (2 - part) * side, kept:] = odd.astype(jnp.bfloat16)


def partial_model(first_a, first_b, stride, across, u, v, images, rhs):
    kept, lanes = rhs.shape[0] // 2, rhs.shape[1]
    side = images.shape[1] // 2
    width = (across - 1) * stride + side
    lines8 = row_iota(8, lanes)
    fu = fraction(u)
    hv = lax.shift_right_arithmetic(fraction(v), 1)

    def wide(x):
        return jnp.broadcast_to(x, (8, lanes))

    now = wave((2 * lines8 + 1) * hv)
    step = cmul(tuple(wide(t[7:8]) for t in now), tuple(wide(t[0:1]) for t in now))
    seq = chebyshev(now, step, kept // 8)
    for h in range(kept // 16):
        for part in range(2):
            both = jnp.concatenate([seq[2 * h][part], seq[2 * h + 1][part]], axis=0)
            rhs[part * kept + h * 16 : part * kept + (h + 1) * 16, :] = both.astype(jnp.bfloat16)

    now = wave(lines8 * fu)
    half = tuple(wide(t[4:5]) for t in now)
    seq = chebyshev(now, cmul(half, half), side // 8)
    model_r = jnp.zeros((1, lanes), jnp.float32)
    model_i = jnp.zeros((1, lanes), jnp.float32)
    for a in range(images.shape[0]):
        res = jnp.dot(images[a], rhs[...], preferred_element_type=jnp.float32)
        total_r = jnp.zeros((8, lanes), jnp.float32)
        total_i = jnp.zeros((8, lanes), jnp.float32)
        for h in range(side // 8):
            real = res[h * 8 : (h + 1) * 8]
            imag = res[side + h * 8 : side + (h + 1) * 8]
            c, s = seq[h]
            total_r = total_r + (c * real + s * imag)
            total_i = total_i + (c * imag - s * real)
        total_r = jnp.sum(total_r, axis=0, keepdims=True)
        total_i = jnp.sum(total_i, axis=0, keepdims=True)
        c, s = wave(((first_a + a) * stride) * fu + (2 * stride * first_b + (width - 1)) * hv)
        model_r = model_r + (c * total_r + s * total_i)
        model_i = model_i + (c * total_i - s * total_r)
    return model_r * (1.0 / SUBGRID), model_i * (1.0 / SUBGRID)


def exchange_kernel(
    groups,
    columns,
    per_group,
    table_hbm,
    count_hbm,
    off_hbm,
    c_hbm,
    uv_hbm,
    obs_hbm,
    weight_hbm,
    phase_ref,
    where_ref,
    resid_ref,
    table_ref,
    count_ref,
    off_ref,
    uv_ref,
    obs_ref,
    weight_ref,
    c_ref,
    fold,
    images,
    rhs,
    uv_all,
    ow_all,
    uv_mine,
    uv_cols,
    part_mine,
    part_all,
    resid_wide,
    resid_mine,
    phases,
    where,
    in_sem,
    c_sem,
    known,
    uv_send,
    uv_recv,
    ow_send,
    ow_recv,
    part_send,
    part_recv,
    high_sem,
    low_sem,
    resid_sem,
    out_sem,
):
    members = c_ref.shape[1]
    side = c_ref.shape[-1]
    slots = uv_ref.shape[2]
    lanes = uv_ref.shape[-1]
    tiles = lanes // 128
    across = min(per_group, FACET_SIDE)
    stride = (SUBGRID - side) // (FACET_SIDE - 1)
    group = lax.axis_index("facet")
    column = lax.axis_index("sub")
    barrier = pltpu.get_barrier_semaphore()
    rounds = columns.bit_length() - 1
    paired = columns == 1 << rounds
    low_bits = rounds // 2 if paired else 0
    low = 1 << low_bits
    high = columns // low
    order = list(range(low_bits, rounds)) + list(range(low_bits))
    mine_low = lax.rem(column, low)
    mine_high = lax.div(column, low)
    mine = mine_low * high + mine_high

    def peer_group(p):
        return lax.rem(group + p, groups)

    def peer_column(p):
        return lax.rem(column + p, columns)

    def partner(r):
        bit = 1 << r
        return column + bit - 2 * bit * lax.rem(lax.div(column, bit), 2)

    for p in range(1, groups):
        pl.semaphore_signal(barrier, inc=1, device_id={"facet": peer_group(p)}, device_id_type=MESH)
    near = [partner(r) for r in order] if paired else [peer_column(p) for p in range(1, columns)]
    for other in near:
        pl.semaphore_signal(barrier, inc=1, device_id={"sub": other}, device_id_type=MESH)

    def tell(r):
        if paired and 1 <= r < rounds:
            pl.semaphore_signal(known.at[r], inc=1, device_id={"sub": partner(order[r])}, device_id_type=MESH)

    def hear(r):
        if paired and 1 <= r < rounds:
            pl.semaphore_wait(known.at[r], 1)

    smalls = [
        pltpu.make_async_copy(src, dst, in_sem.at[i])
        for i, (src, dst) in enumerate(
            (
                (uv_hbm, uv_ref),
                (count_hbm, count_ref),
                (obs_hbm, obs_ref),
                (weight_hbm, weight_ref),
                (table_hbm, table_ref),
                (off_hbm, off_ref),
            )
        )
    ]
    loads = [
        pltpu.make_async_copy(c_hbm.at[:, 0, j], c_ref.at[:, j], c_sem.at[j]) for j in range(members)
    ]
    for load in smalls + loads:
        load.start()
    fold_matrix(across, side, stride, fold)
    for load in smalls:
        load.wait()

    lane = lax.broadcasted_iota(jnp.int32, (1, 128), 1)
    for k in range(slots):
        for i in range(tiles):
            part = slice(128 * i, 128 * (i + 1))
            for p in range(2):
                uv_all[group, (2 * k + p) * tiles + i : (2 * k + p) * tiles + i + 1, :] = uv_ref[0, 0, k, p : p + 1, part]
                ow_all[group, (3 * k + p) * tiles + i : (3 * k + p) * tiles + i + 1, :] = obs_ref[0, 0, k, p : p + 1, part]
            live = jnp.where(lane + 128 * i < count_ref[0, 0, k], 1.0, 0.0)
            at = (3 * k + 2) * tiles + i
            ow_all[group, at : at + 1, :] = weight_ref[0, 0, k : k + 1, part] * live
    pl.semaphore_wait(barrier, groups - 1 + len(near))
    tell(1)

    def to_group(buf, send, recv, p):
        return pltpu.make_async_remote_copy(
            src_ref=buf.at[group],
            dst_ref=buf.at[group],
            send_sem=send.at[p],
            recv_sem=recv.at[p],
            device_id={"facet": peer_group(p)},
            device_id_type=MESH,
        )

    def each_group(buf, send, recv, act):
        @pl.loop(1, groups)
        def _(p):
            act(to_group(buf, send, recv, p))

    def send(src, dst, sems, other):
        copy = pltpu.make_async_remote_copy(
            src_ref=src,
            dst_ref=dst,
            send_sem=sems.at[0],
            recv_sem=sems.at[1],
            device_id={"sub": other},
            device_id_type=MESH,
        )
        copy.start()

    def send_high():
        for p in range(1, high):
            other = lax.rem(mine_high + p, high) * low + mine_low
            send(uv_mine, uv_cols.at[mine], high_sem, other)

    def send_low():
        block = uv_cols.at[pl.ds(mine_low * high, high)]
        for p in range(1, low):
            send(block, block, low_sem, mine_high * low + lax.rem(mine_low + p, low))

    def send_resid():
        @pl.loop(1, columns)
        def _(p):
            send(resid_mine, resid_ref.at[column], resid_sem, peer_column(p))

    def wait_bytes(dst, count, sem):
        if count > 0:
            shown = dst.at[pl.ds(0, count)]
            pltpu.make_async_copy(shown, shown, sem).wait()

    def start(copy):
        copy.start()

    def wait(copy):
        copy.wait()

    each_group(uv_all, uv_send, uv_recv, start)
    each_group(ow_all, ow_send, ow_recv, start)
    for load in loads:
        load.wait()
    if members <= 2:
        for j in range(members):
            fold_image(c_ref, fold, images, j)
    else:

        @pl.loop(0, members)
        def _(j):
            fold_image(c_ref, fold, images, j)

    each_group(uv_all, uv_send, uv_recv, wait)

    def holds(g, k, j):
        return jnp.where(table_ref[0, g, k] == j, 1.0, 0.0)

    spots = jnp.zeros((1, 128), jnp.float32)
    for j in range(members):
        picked = jnp.zeros((2 * tiles, 128), jnp.float32)
        for g in range(groups):
            for k in range(slots):
                at = 2 * tiles * k
                picked = picked + uv_all[g, at : at + 2 * tiles, :] * holds(g, k, j)
        uv_mine[2 * tiles * j : 2 * tiles * (j + 1), :] = picked
        for axis in range(2):
            spots = jnp.where(lane == 2 * j + axis, off_ref[0, j, axis].astype(jnp.float32), spots)
    place = 2 * tiles * members
    uv_mine[place : place + 1, :] = spots
    uv_cols[mine] = uv_mine[...]
    for r in range(1, rounds - low_bits):
        hear(r)
        tell(r + 1)
    send_high()

    first_a = lax.div(group * per_group, FACET_SIDE)
    first_b = lax.rem(group * per_group, FACET_SIDE)

    def models(j, slot):
        at = 2 * tiles * j
        u = jnp.concatenate([uv_mine[pl.ds(at + i, 1), :] for i in range(tiles)], axis=1)
        v = jnp.concatenate([uv_mine[pl.ds(at + tiles + i, 1), :] for i in range(tiles)], axis=1)
        both = partial_model(first_a, first_b, stride, across, u, v, images.at[j], rhs[slot])
        for p in range(2):
            for i in range(tiles):
                part_mine[pl.ds(at + p * tiles + i, 1), :] = both[p][:, 128 * i : 128 * (i + 1)]

    if members <= 2:
        for j in range(members):
            models(j, j % 2)
    else:

        @pl.loop(0, members)
        def _(j):
            models(j, 0)

    part_all[group] = part_mine[...]
    each_group(part_all, part_send, part_recv, start)
    for r in range(max(rounds - low_bits, 1), rounds):
        hear(r)
        tell(r + 1)
    wait_bytes(uv_cols, high - 1, high_sem.at[1])
    send_low()
    each_group(ow_all, ow_send, ow_recv, wait)
    each_group(part_all, part_send, part_recv, wait)

    for j in range(members):
        picked = jnp.zeros((3 * tiles, 128), jnp.float32)
        model = jnp.zeros((2 * tiles, 128), jnp.float32)
        at = 2 * tiles * j
        for g in range(groups):
            model = model + part_all[g, at : at + 2 * tiles, :]
            for k in range(slots):
                first = 3 * tiles * k
                picked = picked + ow_all[g, first : first + 3 * tiles, :] * holds(g, k, j)
        weight = picked[2 * tiles :]
        weight = jnp.concatenate([weight, weight], axis=0)
        resid_wide[at : at + 2 * tiles, :] = weight * (picked[: 2 * tiles] - model)
    resid_mine[...] = resid_wide[...].astype(jnp.bfloat16)
    send_resid()
    own = pltpu.make_async_copy(resid_mine, resid_ref.at[column], out_sem.at[0])
    own.start()

    wait_bytes(uv_cols, columns - high, low_sem.at[1])
    row = row_iota(uv_cols.shape[1], 128)
    halved = lax.rem(row, 2 * tiles) >= tiles
    for i in range(columns):
        c = i % high * low + i // high
        full = fraction(uv_cols[i])
        phases[c] = jnp.where(halved, lax.shift_right_arithmetic(full, 1), full)
        where[c : c + 1, :] = uv_cols[i, place : place + 1, :].astype(jnp.int32)
    outs = [
        pltpu.make_async_copy(phases, phase_ref, out_sem.at[1]),
        pltpu.make_async_copy(where, where_ref, out_sem.at[2]),
    ]
    for out in outs:
        out.start()
    wait_bytes(uv_cols, high - 1, high_sem.at[0])
    wait_bytes(uv_cols, columns - high, low_sem.at[0])
    for out in [own] + outs:
        out.wait()
    wait_bytes(resid_ref, columns - 1, resid_sem.at[0])
    wait_bytes(resid_ref, columns - 1, resid_sem.at[1])


def grid_kernel(
    per_group,
    members,
    side,
    gain,
    off_hbm,
    phase_hbm,
    resid_hbm,
    out_hbm,
    off_ref,
    phase_ref,
    resid_ref,
    out_ref,
    front,
    back,
    lefts,
    rights,
    lead,
    resid_f,
    hits,
    in_sem,
    out_sem,
):
    loads = [
        pltpu.make_async_copy(off_hbm, off_ref, in_sem.at[0]),
        pltpu.make_async_copy(phase_hbm, phase_ref, in_sem.at[1]),
        pltpu.make_async_copy(resid_hbm, resid_ref, in_sem.at[2]),
    ]
    for load in loads:
        load.start()
    columns = phase_ref.shape[0]
    lanes = lefts[0].shape[1]
    tiles = lanes // 128
    rows = out_ref.shape[2]
    chunks = front.shape[0] // 2
    half = side // 2
    base = lefts[0].shape[0] // 2
    stride = (SUBGRID - side) // (FACET_SIDE - 1)
    facet_here = lax.axis_index("facet") * per_group
    first_line = lax.axis_index("sub") * rows
    facet_rows = lead.shape[1]
    first_a = lax.div(facet_here, FACET_SIDE)
    lines8 = row_iota(8, lanes)
    facet = row_iota(facet_rows, lanes) + facet_here
    lead_u = (lax.div(facet, FACET_SIDE) - first_a) * stride
    lead_v = lax.rem(facet, FACET_SIDE) * (2 * stride) + (side - 1)
    front[...] = jnp.zeros_like(front)
    back[...] = jnp.zeros_like(back)
    if base > per_group * rows:
        for left in lefts:
            left[...] = jnp.zeros_like(left)
    for load in loads:
        load.wait()
    resid_f[...] = resid_ref[...].astype(jnp.float32)

    total = columns * members

    def begin(s):
        start = lax.rem(first_line - off_ref[lax.div(s, members), 2 * lax.rem(s, members)] + WIN, WIN)
        return jnp.where(start > WIN - rows, start - WIN, start)

    def scan(s, found):
        hits[found] = s
        return found + jnp.where(begin(s) < side, 1, 0)

    found = lax.fori_loop(0, total, scan, jnp.int32(0), unroll=min(total, 32))

    def wide(x):
        return jnp.broadcast_to(x, (8, lanes))

    def conj_mul(a, b):
        return a[0] * b[0] + a[1] * b[1], a[1] * b[0] - a[0] * b[1]

    def lane_row(ref, c, at):
        return jnp.concatenate([ref[c, pl.ds(at + i, 1), :] for i in range(tiles)], axis=1)

    def fill(index, left, right):
        s = jnp.where(index < found, hits[jnp.minimum(index, total - 1)], 0)
        scale = jnp.where(index < found, gain, 0.0)
        column = lax.div(s, members)
        j = lax.rem(s, members)
        start = begin(s)
        fu = lane_row(phase_ref, column, 2 * tiles * j)
        hv = lane_row(phase_ref, column, 2 * tiles * j + tiles)
        rr = lane_row(resid_f, column, 2 * tiles * j) * scale
        ri = lane_row(resid_f, column, 2 * tiles * j + tiles) * scale
        head = cmul(wave(lead_u * fu + lead_v * hv), (rr, ri))
        lead[0] = head[0]
        lead[1] = head[1]

        now = wave((2 * lines8 + 1) * hv)
        step = cmul(tuple(wide(t[7:8]) for t in now), tuple(wide(t[0:1]) for t in now))
        seq = chebyshev(now, step, half // 8)
        for h in range(half // 16):
            for part in range(2):
                both = jnp.concatenate([seq[2 * h][part], seq[2 * h + 1][part]], axis=0)
                right[part * half + h * 16 : part * half + (h + 1) * 16, :] = both.astype(jnp.bfloat16)

        now = wave((lines8 + (start + first_a * stride)) * fu)
        step = conj_mul(tuple(wide(t[4:5]) for t in now), tuple(wide(t[0:1]) for t in now))
        step = cmul(step, step)
        seq = chebyshev(now, step, rows // 8)
        shown = []
        for h in range(rows // 8):
            cell = lines8 + (h * 8 + start)
            live = (cell >= 0) & (cell < side)
            shown.append(tuple(jnp.where(live, t, 0.0) for t in seq[h]))
        tall = min(rows, 16)
        per = 16 // tall
        if per == 2:
            table = [tuple(jnp.concatenate([t, t], axis=0).astype(jnp.bfloat16) for t in shown[0])]
        else:
            table = [
                tuple(jnp.concatenate([p, q], axis=0).astype(jnp.bfloat16) for p, q in zip(a, b))
                for a, b in zip(shown[0::2], shown[1::2])
            ]
        for f in range(0, per_group, per):
            own = tuple(
                jnp.concatenate(
                    [jnp.broadcast_to(lead[part, f + i : f + i + 1, :], (tall, lanes)) for i in range(per)], axis=0
                ).astype(jnp.bfloat16)
                for part in range(2)
            )
            for h, t in enumerate(table):
                at = f * rows + h * 16
                value = cmul(t, own)
                left[at : at + 16, :] = value[0]
                left[base + at : base + at + 16, :] = value[1]
        return off_ref[column, 2 * j + 1]

    def add(offset, left, right):
        prod = lax.dot_general(
            right[...], left[...], (((1,), (1,)), ((), ())), preferred_element_type=jnp.float32
        )
        ahead = pl.ds(offset, half)
        behind = pl.ds(WIN - offset, half)
        for k in range(chunks):
            real = slice(128 * k, 128 * (k + 1))
            imag = slice(base + 128 * k, base + 128 * (k + 1))
            front[k, ahead, :] += prod[:half, real] - prod[half:, imag]
            back[k, behind, :] += prod[:half, real] + prod[half:, imag]
            front[chunks + k, ahead, :] += prod[:half, imag] + prod[half:, real]
            back[chunks + k, behind, :] += prod[:half, imag] - prod[half:, real]

    def pair(i, offset):
        later = fill(2 * i + 1, lefts[1], rights[1])
        add(offset, lefts[0], rights[0])
        offset = fill(2 * i + 2, lefts[0], rights[0])
        add(later, lefts[1], rights[1])
        return offset

    first = fill(0, lefts[0], rights[0])
    lax.fori_loop(0, lax.div(found + 1, 2), pair, first)

    turned = 7 - row_iota(8, 128)
    done = []
    for part in range(2):
        for k in range(chunks):
            x = front.at[part * chunks + k]
            y = back.at[part * chunks + k]
            ahead = [x[WIN - half : WIN], x[0:half] + x[WIN : WIN + half], x[half : WIN - half]]
            behind = []
            for at in range(WIN + half - 8, half - 8, -8):
                tile = y[at : at + 8]
                if at >= WIN:
                    tile = tile + y[at - WIN : at - WIN + 8]
                behind.append(jnp.take_along_axis(tile, turned, axis=0))
            whole = (jnp.concatenate(ahead, axis=0) + jnp.concatenate(behind, axis=0)).T
            facets = [f for f in range(per_group) if 0 <= f * rows - 128 * k < 128]
            for f in facets:
                at = f * rows - 128 * k
                out_ref[f, part] = whole[at : at + rows]
            if facets:
                some = pl.ds(facets[0], len(facets))
                copy = pltpu.make_async_copy(
                    out_ref.at[some, part], out_hbm.at[some, part], out_sem.at[part * chunks + k]
                )
                copy.start()
                done.append(copy)
    for copy in done:
        copy.wait()


def exchange_call(groups, columns, slot_subgrid, vis_count, offset, contributions, uv, obs, weight):
    per_group, _, members, _, side, _ = contributions.shape
    slots, lanes = weight.shape[2:]
    tiles = lanes // 128
    across = min(per_group, FACET_SIDE)
    width = (SUBGRID - side) // (FACET_SIDE - 1) * (across - 1) + side
    kept = -(-width // 256) * 128
    dma = pltpu.SemaphoreType.DMA
    f32, bf16 = jnp.float32, jnp.bfloat16

    def rows(n, unit=8):
        return -(-n // unit) * unit

    uv_rows = 2 * members * tiles + 1
    resid_rows = rows(2 * members * tiles, 16)
    return pl.pallas_call(
        functools.partial(exchange_kernel, groups, columns, per_group),
        out_shape=(
            jax.ShapeDtypeStruct((columns, uv_rows, 128), jnp.int32),
            jax.ShapeDtypeStruct((columns, 128), jnp.int32),
            jax.ShapeDtypeStruct((columns, resid_rows, 128), bf16),
        ),
        in_specs=[pl.BlockSpec(memory_space=pl.ANY)] * 7,
        out_specs=(pl.BlockSpec(memory_space=pl.ANY),) * 3,
        scratch_shapes=[
            pltpu.SMEM(slot_subgrid.shape, jnp.int32),
            pltpu.SMEM(vis_count.shape, jnp.int32),
            pltpu.SMEM(offset.shape, jnp.int32),
            pltpu.VMEM(uv.shape, f32),
            pltpu.VMEM(obs.shape, f32),
            pltpu.VMEM(weight.shape, f32),
            pltpu.VMEM((per_group, members, 2, side, side), bf16),
            pltpu.VMEM((across * side, 2 * kept), bf16),
            pltpu.VMEM((members, per_group // across, 2 * side, 2 * kept), bf16),
            [pltpu.VMEM((2 * kept, lanes), bf16)] * 2,
            pltpu.VMEM((groups, rows(2 * slots * tiles), 128), f32),
            pltpu.VMEM((groups, rows(3 * slots * tiles), 128), f32),
            pltpu.VMEM((uv_rows, 128), f32),
            pltpu.VMEM((columns, uv_rows, 128), f32),
            pltpu.VMEM((rows(2 * members * tiles), 128), f32),
            pltpu.VMEM((groups, rows(2 * members * tiles), 128), f32),
            pltpu.VMEM((resid_rows, 128), f32),
            pltpu.VMEM((resid_rows, 128), bf16),
            pltpu.VMEM((columns, uv_rows, 128), jnp.int32),
            pltpu.VMEM((columns, 128), jnp.int32),
            dma((6,)),
            dma((members,)),
            pltpu.SemaphoreType.REGULAR((max(columns.bit_length(), 1),)),
            dma((groups,)),
            dma((groups,)),
            dma((groups,)),
            dma((groups,)),
            dma((groups,)),
            dma((groups,)),
            dma((2,)),
            dma((2,)),
            dma((2,)),
            dma((3,)),
        ],
        compiler_params=pltpu.CompilerParams(collective_id=0, has_side_effects=True),
    )(slot_subgrid, vis_count, offset, contributions, uv, obs, weight)


def grid_call(phases, offsets, resid, per_group, members, lanes, side, rows, gain):
    base = -(-per_group * rows // 128) * 128
    half = side // 2
    return pl.pallas_call(
        functools.partial(grid_kernel, per_group, members, side, gain),
        out_shape=jax.ShapeDtypeStruct((per_group, 2, rows, WIN), jnp.float32),
        in_specs=[pl.BlockSpec(memory_space=pl.ANY)] * 3,
        out_specs=pl.BlockSpec(memory_space=pl.ANY),
        scratch_shapes=[
            pltpu.SMEM(offsets.shape, jnp.int32),
            pltpu.VMEM(phases.shape, jnp.int32),
            pltpu.VMEM(resid.shape, jnp.bfloat16),
            pltpu.VMEM((per_group, 2, rows, WIN), jnp.float32),
            pltpu.VMEM((base // 64, WIN + half, 128), jnp.float32),
            pltpu.VMEM((base // 64, WIN + half, 128), jnp.float32),
            [pltpu.VMEM((2 * base, lanes), jnp.bfloat16)] * 2,
            [pltpu.VMEM((2 * half, lanes), jnp.bfloat16)] * 2,
            pltpu.VMEM((2, -(-per_group // 8) * 8, lanes), jnp.float32),
            pltpu.VMEM(resid.shape, jnp.float32),
            pltpu.SMEM((offsets.shape[0] * members + 8,), jnp.int32),
            pltpu.SemaphoreType.DMA((3,)),
            pltpu.SemaphoreType.DMA((base // 64,)),
        ],
    )(offsets, phases, resid)


def body(contributions, slot_subgrid, vis_count, vis_uv, vis_obs, vis_weight, subgrid_offset):
    groups = lax.axis_size("facet")
    columns = lax.axis_size("sub")
    per_group, _, members, _, side, _ = contributions.shape
    lanes = vis_weight.shape[-1]
    phases, offsets, resid = exchange_call(
        groups,
        columns,
        slot_subgrid,
        vis_count,
        subgrid_offset,
        contributions,
        vis_uv,
        vis_obs,
        vis_weight,
    )
    gain = WIN / (side * math.sqrt(members * columns)) / math.sqrt(lanes)
    return grid_call(phases, offsets, resid, per_group, members, lanes, side, WIN // columns, gain)


def solution(mesh):
    placed = (
        P("facet", "sub", None, None, None, None),
        P("sub", None, None),
        P("facet", "sub", None),
        P("facet", "sub", None, None, None),
        P("facet", "sub", None, None, None),
        P("facet", "sub", None, None),
        P("sub", None, None),
    )
    return jax.shard_map(
        body, mesh=mesh, in_specs=placed, out_specs=P("facet", None, "sub", None), check_vma=False
    )
```

```python
import functools
import math

import jax
import jax.numpy as jnp
from jax import lax
from jax.experimental import pallas as pl
from jax.experimental.pallas import tpu as pltpu
from jax.sharding import PartitionSpec as P

SUBGRID = 512
FACET_SIDE = 4
WIN = 512
MESH = pl.DeviceIdType.MESH


def cmul(a, b):
    return a[0] * b[0] - a[1] * b[1], a[0] * b[1] + a[1] * b[0]


def row_iota(rows, lanes):
    return lax.broadcasted_iota(jnp.int32, (rows, lanes), 0)


SIN = (3.14159027, -5.16740673, 2.54401052, -0.55946246)
COS = (0.99999995, -4.93479283, 4.05841135, -1.33187657, 0.21968961)


def fraction(w):
    t = w * (1.0 / SUBGRID)
    t = t - jnp.where(t >= 0.5, 1.0, 0.0)
    return (t * 4294967296.0).astype(jnp.int32)


def wave(phase):
    t = phase.astype(jnp.float32) * (1.0 / 4294967296.0)
    q = t * t
    s = SIN[3]
    for a in SIN[2::-1]:
        s = s * q + a
    s = s * t
    c = COS[4]
    for a in COS[3::-1]:
        c = c * q + a
    s2 = s + s
    return 1.0 - s2 * s, s2 * c


def chebyshev(first, step, count):
    double = step[0] + step[0]
    seq = [first]
    if count > 1:
        seq.append(cmul(first, step))
    while len(seq) < count:
        seq.append(tuple(double * p - q for p, q in zip(seq[-1], seq[-2])))
    return seq


def fold_matrix(across, side, stride, fold):
    rows, cols = fold.shape
    kept = cols // 2
    low = side // 128 * 128
    high = side - low
    width = (across - 1) * stride + side
    spans = [(b, y, 64) for b in range(across) for y in range(0, low, 64)]
    spans += [(b, low, high) for b in range(across)]
    lines = lax.broadcasted_iota(jnp.int32, (64, 128), 0)
    lane = lax.broadcasted_iota(jnp.int32, (64, 128), 1)
    at = 0
    for b, y, count in spans:
        turn = 2 * (b * stride + y) - (width - 1) + 2 * lines
        sign = jnp.where(turn < 0, -1.0, 1.0)
        cell = lax.shift_right_arithmetic(jnp.abs(turn), 1) - lane
        for k in range(0, kept, 128):
            hit = cell == k
            fold[at : at + count, k : k + 128] = jnp.where(hit, 1.0, 0.0)[:count].astype(jnp.bfloat16)
            fold[at : at + count, kept + k : kept + k + 128] = jnp.where(hit, sign, 0.0)[:count].astype(
                jnp.bfloat16
            )
        at += count


def fold_image(c_ref, fold, images, j):
    per_group, _, _, side, _ = c_ref.shape
    across = min(per_group, FACET_SIDE)
    low = side // 128 * 128
    kept = fold.shape[1] // 2
    for a in range(per_group // across):
        for part in range(2):
            blocks = [c_ref[a * across + b, j, part] for b in range(across)]
            strip = jnp.concatenate([x[:, :low] for x in blocks] + [x[:, low:] for x in blocks], axis=1)
            res = jnp.dot(strip, fold[...], preferred_element_type=jnp.float32)
            images[j, a, part * side : (part + 1) * side, :kept] = res[:, :kept].astype(jnp.bfloat16)
            odd = res[:, kept:] if part == 1 else -res[:, kept:]
            images[j, a, (1 - part) * side : (2 - part) * side, kept:] = odd.astype(jnp.bfloat16)


def partial_model(first_a, first_b, stride, across, u, v, images, rhs):
    kept, lanes = rhs.shape[0] // 2, rhs.shape[1]
    side = images.shape[1] // 2
    width = (across - 1) * stride + side
    lines8 = row_iota(8, lanes)
    fu = fraction(u)
    hv = lax.shift_right_arithmetic(fraction(v), 1)

    def wide(x):
        return jnp.broadcast_to(x, (8, lanes))

    now = wave((2 * lines8 + 1) * hv)
    step = cmul(tuple(wide(t[7:8]) for t in now), tuple(wide(t[0:1]) for t in now))
    seq = chebyshev(now, step, kept // 8)
    for h in range(kept // 16):
        for part in range(2):
            both = jnp.concatenate([seq[2 * h][part], seq[2 * h + 1][part]], axis=0)
            rhs[part * kept + h * 16 : part * kept + (h + 1) * 16, :] = both.astype(jnp.bfloat16)

    now = wave(lines8 * fu)
    half = tuple(wide(t[4:5]) for t in now)
    seq = chebyshev(now, cmul(half, half), side // 8)
    model_r = jnp.zeros((1, lanes), jnp.float32)
    model_i = jnp.zeros((1, lanes), jnp.float32)
    for a in range(images.shape[0]):
        res = jnp.dot(images[a], rhs[...], preferred_element_type=jnp.float32)
        total_r = jnp.zeros((8, lanes), jnp.float32)
        total_i = jnp.zeros((8, lanes), jnp.float32)
        for h in range(side // 8):
            real = res[h * 8 : (h + 1) * 8]
            imag = res[side + h * 8 : side + (h + 1) * 8]
            c, s = seq[h]
            total_r = total_r + (c * real + s * imag)
            total_i = total_i + (c * imag - s * real)
        total_r = jnp.sum(total_r, axis=0, keepdims=True)
        total_i = jnp.sum(total_i, axis=0, keepdims=True)
        c, s = wave(((first_a + a) * stride) * fu + (2 * stride * first_b + (width - 1)) * hv)
        model_r = model_r + (c * total_r + s * total_i)
        model_i = model_i + (c * total_i - s * total_r)
    return model_r * (1.0 / SUBGRID), model_i * (1.0 / SUBGRID)


def exchange_kernel(
    groups,
    columns,
    per_group,
    table_hbm,
    count_hbm,
    off_hbm,
    c_hbm,
    uv_hbm,
    obs_hbm,
    weight_hbm,
    phase_ref,
    where_ref,
    resid_ref,
    table_ref,
    count_ref,
    off_ref,
    uv_ref,
    obs_ref,
    weight_ref,
    c_ref,
    fold,
    images,
    rhs,
    uv_all,
    ow_all,
    uv_mine,
    uv_cols,
    part_mine,
    part_all,
    resid_wide,
    resid_mine,
    phases,
    where,
    in_sem,
    c_sem,
    known,
    uv_send,
    uv_recv,
    ow_send,
    ow_recv,
    part_send,
    part_recv,
    high_sem,
    low_sem,
    resid_sem,
    out_sem,
):
    members = c_ref.shape[1]
    side = c_ref.shape[-1]
    slots = uv_ref.shape[2]
    lanes = uv_ref.shape[-1]
    tiles = lanes // 128
    across = min(per_group, FACET_SIDE)
    stride = (SUBGRID - side) // (FACET_SIDE - 1)
    group = lax.axis_index("facet")
    column = lax.axis_index("sub")
    barrier = pltpu.get_barrier_semaphore()
    rounds = columns.bit_length() - 1
    paired = columns == 1 << rounds
    low_bits = rounds // 2 if paired else 0
    low = 1 << low_bits
    high = columns // low
    order = list(range(low_bits, rounds)) + list(range(low_bits))
    mine_low = lax.rem(column, low)
    mine_high = lax.div(column, low)
    mine = mine_low * high + mine_high

    def peer_group(p):
        return lax.rem(group + p, groups)

    def peer_column(p):
        return lax.rem(column + p, columns)

    def partner(r):
        bit = 1 << r
        return column + bit - 2 * bit * lax.rem(lax.div(column, bit), 2)

    for p in range(1, groups):
        pl.semaphore_signal(barrier, inc=1, device_id={"facet": peer_group(p)}, device_id_type=MESH)
    near = [partner(r) for r in order] if paired else [peer_column(p) for p in range(1, columns)]
    for other in near:
        pl.semaphore_signal(barrier, inc=1, device_id={"sub": other}, device_id_type=MESH)

    def tell(r):
        if paired and 1 <= r < rounds:
            pl.semaphore_signal(known.at[r], inc=1, device_id={"sub": partner(order[r])}, device_id_type=MESH)

    def hear(r):
        if paired and 1 <= r < rounds:
            pl.semaphore_wait(known.at[r], 1)

    smalls = [
        pltpu.make_async_copy(src, dst, in_sem.at[i])
        for i, (src, dst) in enumerate(
            (
                (uv_hbm, uv_ref),
                (count_hbm, count_ref),
                (obs_hbm, obs_ref),
                (weight_hbm, weight_ref),
                (table_hbm, table_ref),
                (off_hbm, off_ref),
            )
        )
    ]
    loads = [
        pltpu.make_async_copy(c_hbm.at[:, 0, j], c_ref.at[:, j], c_sem.at[j]) for j in range(members)
    ]
    for load in smalls + loads:
        load.start()
    fold_matrix(across, side, stride, fold)
    for load in smalls:
        load.wait()

    lane = lax.broadcasted_iota(jnp.int32, (1, 128), 1)
    for k in range(slots):
        for i in range(tiles):
            part = slice(128 * i, 128 * (i + 1))
            for p in range(2):
                uv_all[group, (2 * k + p) * tiles + i : (2 * k + p) * tiles + i + 1, :] = uv_ref[0, 0, k, p : p + 1, part]
                ow_all[group, (3 * k + p) * tiles + i : (3 * k + p) * tiles + i + 1, :] = obs_ref[0, 0, k, p : p + 1, part]
            live = jnp.where(lane + 128 * i < count_ref[0, 0, k], 1.0, 0.0)
            at = (3 * k + 2) * tiles + i
            ow_all[group, at : at + 1, :] = weight_ref[0, 0, k : k + 1, part] * live
    pl.semaphore_wait(barrier, groups - 1 + len(near))
    tell(1)

    def to_group(buf, send, recv, p):
        return pltpu.make_async_remote_copy(
            src_ref=buf.at[group],
            dst_ref=buf.at[group],
            send_sem=send.at[p],
            recv_sem=recv.at[p],
            device_id={"facet": peer_group(p)},
            device_id_type=MESH,
        )

    def each_group(buf, send, recv, act):
        @pl.loop(1, groups)
        def _(p):
            act(to_group(buf, send, recv, p))

    def send(src, dst, sems, other):
        copy = pltpu.make_async_remote_copy(
            src_ref=src,
            dst_ref=dst,
            send_sem=sems.at[0],
            recv_sem=sems.at[1],
            device_id={"sub": other},
            device_id_type=MESH,
        )
        copy.start()

    def send_high():
        for p in range(1, high):
            other = lax.rem(mine_high + p, high) * low + mine_low
            send(uv_mine, uv_cols.at[mine], high_sem, other)

    def send_low():
        block = uv_cols.at[pl.ds(mine_low * high, high)]
        for p in range(1, low):
            send(block, block, low_sem, mine_high * low + lax.rem(mine_low + p, low))

    def send_resid():
        @pl.loop(1, columns)
        def _(p):
            send(resid_mine, resid_ref.at[column], resid_sem, peer_column(p))

    def wait_bytes(dst, count, sem):
        if count > 0:
            shown = dst.at[pl.ds(0, count)]
            pltpu.make_async_copy(shown, shown, sem).wait()

    def start(copy):
        copy.start()

    def wait(copy):
        copy.wait()

    each_group(uv_all, uv_send, uv_recv, start)
    each_group(ow_all, ow_send, ow_recv, start)
    for load in loads:
        load.wait()
    if members <= 2:
        for j in range(members):
            fold_image(c_ref, fold, images, j)
    else:

        @pl.loop(0, members)
        def _(j):
            fold_image(c_ref, fold, images, j)

    each_group(uv_all, uv_send, uv_recv, wait)

    def holds(g, k, j):
        return jnp.where(table_ref[0, g, k] == j, 1.0, 0.0)

    spots = jnp.zeros((1, 128), jnp.float32)
    for j in range(members):
        picked = jnp.zeros((2 * tiles, 128), jnp.float32)
        for g in range(groups):
            for k in range(slots):
                at = 2 * tiles * k
                picked = picked + uv_all[g, at : at + 2 * tiles, :] * holds(g, k, j)
        uv_mine[2 * tiles * j : 2 * tiles * (j + 1), :] = picked
        for axis in range(2):
            spots = jnp.where(lane == 2 * j + axis, off_ref[0, j, axis].astype(jnp.float32), spots)
    place = 2 * tiles * members
    uv_mine[place : place + 1, :] = spots
    uv_cols[mine] = uv_mine[...]
    for r in range(1, rounds - low_bits):
        hear(r)
        tell(r + 1)
    send_high()

    first_a = lax.div(group * per_group, FACET_SIDE)
    first_b = lax.rem(group * per_group, FACET_SIDE)

    def models(j, slot):
        at = 2 * tiles * j
        u = jnp.concatenate([uv_mine[pl.ds(at + i, 1), :] for i in range(tiles)], axis=1)
        v = jnp.concatenate([uv_mine[pl.ds(at + tiles + i, 1), :] for i in range(tiles)], axis=1)
        both = partial_model(first_a, first_b, stride, across, u, v, images.at[j], rhs[slot])
        for p in range(2):
            for i in range(tiles):
                part_mine[pl.ds(at + p * tiles + i, 1), :] = both[p][:, 128 * i : 128 * (i + 1)]

    if members <= 2:
        for j in range(members):
            models(j, j % 2)
    else:

        @pl.loop(0, members)
        def _(j):
            models(j, 0)

    part_all[group] = part_mine[...]
    each_group(part_all, part_send, part_recv, start)
    for r in range(max(rounds - low_bits, 1), rounds):
        hear(r)
        tell(r + 1)
    wait_bytes(uv_cols, high - 1, high_sem.at[1])
    send_low()
    each_group(ow_all, ow_send, ow_recv, wait)
    each_group(part_all, part_send, part_recv, wait)

    for j in range(members):
        picked = jnp.zeros((3 * tiles, 128), jnp.float32)
        model = jnp.zeros((2 * tiles, 128), jnp.float32)
        at = 2 * tiles * j
        for g in range(groups):
            model = model + part_all[g, at : at + 2 * tiles, :]
            for k in range(slots):
                first = 3 * tiles * k
                picked = picked + ow_all[g, first : first + 3 * tiles, :] * holds(g, k, j)
        weight = picked[2 * tiles :]
        weight = jnp.concatenate([weight, weight], axis=0)
        resid_wide[at : at + 2 * tiles, :] = weight * (picked[: 2 * tiles] - model)
    resid_mine[...] = resid_wide[...].astype(jnp.bfloat16)
    send_resid()
    own = pltpu.make_async_copy(resid_mine, resid_ref.at[column], out_sem.at[0])
    own.start()

    wait_bytes(uv_cols, columns - high, low_sem.at[1])
    row = row_iota(uv_cols.shape[1], 128)
    halved = lax.rem(row, 2 * tiles) >= tiles
    for i in range(columns):
        c = i % high * low + i // high
        full = fraction(uv_cols[i])
        phases[c] = jnp.where(halved, lax.shift_right_arithmetic(full, 1), full)
        where[c : c + 1, :] = uv_cols[i, place : place + 1, :].astype(jnp.int32)
    outs = [
        pltpu.make_async_copy(phases, phase_ref, out_sem.at[1]),
        pltpu.make_async_copy(where, where_ref, out_sem.at[2]),
    ]
    for out in outs:
        out.start()
    wait_bytes(uv_cols, high - 1, high_sem.at[0])
    wait_bytes(uv_cols, columns - high, low_sem.at[0])
    for out in [own] + outs:
        out.wait()
    wait_bytes(resid_ref, columns - 1, resid_sem.at[0])
    wait_bytes(resid_ref, columns - 1, resid_sem.at[1])


def grid_kernel(
    per_group,
    members,
    side,
    gain,
    off_hbm,
    phase_hbm,
    resid_hbm,
    out_hbm,
    off_ref,
    phase_ref,
    resid_ref,
    out_ref,
    front,
    back,
    lefts,
    rights,
    readies,
    resid_f,
    hits,
    in_sem,
    out_sem,
):
    loads = [
        pltpu.make_async_copy(off_hbm, off_ref, in_sem.at[0]),
        pltpu.make_async_copy(phase_hbm, phase_ref, in_sem.at[1]),
        pltpu.make_async_copy(resid_hbm, resid_ref, in_sem.at[2]),
    ]
    for load in loads:
        load.start()
    columns = phase_ref.shape[0]
    lanes = lefts[0].shape[1]
    tiles = lanes // 128
    rows = out_ref.shape[2]
    chunks = front.shape[0] // 2
    half = side // 2
    base = lefts[0].shape[0] // 2
    stride = (SUBGRID - side) // (FACET_SIDE - 1)
    facet_here = lax.axis_index("facet") * per_group
    first_line = lax.axis_index("sub") * rows
    facet_rows = readies[0].shape[1]
    first_a = lax.div(facet_here, FACET_SIDE)
    lines8 = row_iota(8, lanes)
    facet = row_iota(facet_rows, lanes) + facet_here
    lead_u = (lax.div(facet, FACET_SIDE) - first_a) * stride
    lead_v = lax.rem(facet, FACET_SIDE) * (2 * stride) + (side - 1)
    front[...] = jnp.zeros_like(front)
    back[...] = jnp.zeros_like(back)
    if base > per_group * rows:
        for left in lefts:
            left[...] = jnp.zeros_like(left)
    for load in loads:
        load.wait()
    resid_f[...] = resid_ref[...].astype(jnp.float32)

    total = columns * members

    def begin(s):
        start = lax.rem(first_line - off_ref[lax.div(s, members), 2 * lax.rem(s, members)] + WIN, WIN)
        return jnp.where(start > WIN - rows, start - WIN, start)

    def scan(s, found):
        hits[found] = s
        ahead = first_line + (WIN + rows - 1) - off_ref[lax.div(s, members), 2 * lax.rem(s, members)]
        return found + jnp.where(lax.bitwise_and(ahead, WIN - 1) < side + rows - 1, 1, 0)

    if total <= 64:
        found = jnp.int32(0)
        for s in range(total):
            hits[found] = s
            ahead = first_line + (WIN + rows - 1) - off_ref[s // members, 2 * (s % members)]
            found = found + jnp.where(lax.bitwise_and(ahead, WIN - 1) < side + rows - 1, 1, 0)
    else:
        found = lax.fori_loop(0, total, scan, jnp.int32(0), unroll=8)

    def wide(x):
        return jnp.broadcast_to(x, (8, lanes))

    def conj_mul(a, b):
        return a[0] * b[0] + a[1] * b[1], a[1] * b[0] - a[0] * b[1]

    def lane_row(ref, c, at):
        return jnp.concatenate([ref[c, pl.ds(at + i, 1), :] for i in range(tiles)], axis=1)

    def choose(index):
        return jnp.where(index < found, hits[jnp.minimum(index, total - 1)], 0)

    def column_of(index):
        s = choose(index)
        return off_ref[lax.div(s, members), 2 * lax.rem(s, members) + 1]

    def prepare(index, ready):
        s = choose(index)
        scale = jnp.where(index < found, gain, 0.0)
        column = lax.div(s, members)
        j = lax.rem(s, members)
        fu = lane_row(phase_ref, column, 2 * tiles * j)
        hv = lane_row(phase_ref, column, 2 * tiles * j + tiles)
        rr = lane_row(resid_f, column, 2 * tiles * j) * scale
        ri = lane_row(resid_f, column, 2 * tiles * j + tiles) * scale
        head = cmul(wave(lead_u * fu + lead_v * hv), (rr, ri))
        across = wave((2 * lines8 + 1) * hv)
        along = wave((lines8 + (begin(s) + first_a * stride)) * fu)
        for part in range(2):
            ready[part] = head[part]
            ready[2 + part, :8] = across[part]
            ready[4 + part, :8] = along[part]

    def fill(index, ready, left, right):
        start = begin(choose(index))
        now = ready[2, :8], ready[3, :8]
        step = cmul(tuple(wide(t[7:8]) for t in now), tuple(wide(t[0:1]) for t in now))
        seq = chebyshev(now, step, half // 8)
        for h in range(half // 16):
            for part in range(2):
                both = jnp.concatenate([seq[2 * h][part], seq[2 * h + 1][part]], axis=0)
                right[part * half + h * 16 : part * half + (h + 1) * 16, :] = both.astype(jnp.bfloat16)

        now = ready[4, :8], ready[5, :8]
        step = conj_mul(tuple(wide(t[4:5]) for t in now), tuple(wide(t[0:1]) for t in now))
        step = cmul(step, step)
        seq = chebyshev(now, step, rows // 8)
        shown = []
        for h in range(rows // 8):
            cell = lines8 + (h * 8 + start)
            live = (cell >= 0) & (cell < side)
            shown.append(tuple(jnp.where(live, t, 0.0) for t in seq[h]))
        tall = min(rows, 16)
        per = 16 // tall
        if per == 2:
            table = [tuple(jnp.concatenate([t, t], axis=0).astype(jnp.bfloat16) for t in shown[0])]
        else:
            table = [
                tuple(jnp.concatenate([p, q], axis=0).astype(jnp.bfloat16) for p, q in zip(a, b))
                for a, b in zip(shown[0::2], shown[1::2])
            ]
        for f in range(0, per_group, per):
            own = tuple(
                jnp.concatenate(
                    [jnp.broadcast_to(ready[part, f + i : f + i + 1, :], (tall, lanes)) for i in range(per)], axis=0
                ).astype(jnp.bfloat16)
                for part in range(2)
            )
            for h, t in enumerate(table):
                at = f * rows + h * 16
                value = cmul(t, own)
                left[at : at + 16, :] = value[0]
                left[base + at : base + at + 16, :] = value[1]

    def add(index, left, right):
        offset = column_of(index)
        prod = lax.dot_general(
            right[...], left[...], (((1,), (1,)), ((), ())), preferred_element_type=jnp.float32
        )
        ahead = pl.ds(offset, half)
        behind = pl.ds(WIN - offset, half)
        for k in range(chunks):
            real = slice(128 * k, 128 * (k + 1))
            imag = slice(base + 128 * k, base + 128 * (k + 1))
            front[k, ahead, :] += prod[:half, real] - prod[half:, imag]
            back[k, behind, :] += prod[:half, real] + prod[half:, imag]
            front[chunks + k, ahead, :] += prod[:half, imag] + prod[half:, real]
            back[chunks + k, behind, :] += prod[:half, imag] - prod[half:, real]

    def pair(i, carry):
        add(2 * i, lefts[0], rights[0])
        fill(2 * i + 1, readies[1], lefts[1], rights[1])
        add(2 * i + 1, lefts[1], rights[1])
        fill(2 * i + 2, readies[0], lefts[0], rights[0])
        prepare(2 * i + 3, readies[1])
        prepare(2 * i + 4, readies[0])
        return carry

    prepare(0, readies[0])
    prepare(1, readies[1])
    fill(0, readies[0], lefts[0], rights[0])
    prepare(2, readies[0])
    lax.fori_loop(0, lax.div(found + 1, 2), pair, 0)

    turned = 7 - row_iota(8, 128)
    done = []
    for part in range(2):
        for k in range(chunks):
            x = front.at[part * chunks + k]
            y = back.at[part * chunks + k]
            ahead = [x[WIN - half : WIN], x[0:half] + x[WIN : WIN + half], x[half : WIN - half]]
            behind = []
            for at in range(WIN + half - 8, half - 8, -8):
                tile = y[at : at + 8]
                if at >= WIN:
                    tile = tile + y[at - WIN : at - WIN + 8]
                behind.append(jnp.take_along_axis(tile, turned, axis=0))
            whole = (jnp.concatenate(ahead, axis=0) + jnp.concatenate(behind, axis=0)).T
            facets = [f for f in range(per_group) if 0 <= f * rows - 128 * k < 128]
            for f in facets:
                at = f * rows - 128 * k
                out_ref[f, part] = whole[at : at + rows]
            if facets:
                some = pl.ds(facets[0], len(facets))
                copy = pltpu.make_async_copy(
                    out_ref.at[some, part], out_hbm.at[some, part], out_sem.at[part * chunks + k]
                )
                copy.start()
                done.append(copy)
    for copy in done:
        copy.wait()


def exchange_call(groups, columns, slot_subgrid, vis_count, offset, contributions, uv, obs, weight):
    per_group, _, members, _, side, _ = contributions.shape
    slots, lanes = weight.shape[2:]
    tiles = lanes // 128
    across = min(per_group, FACET_SIDE)
    width = (SUBGRID - side) // (FACET_SIDE - 1) * (across - 1) + side
    kept = -(-width // 256) * 128
    dma = pltpu.SemaphoreType.DMA
    f32, bf16 = jnp.float32, jnp.bfloat16

    def rows(n, unit=8):
        return -(-n // unit) * unit

    uv_rows = 2 * members * tiles + 1
    resid_rows = rows(2 * members * tiles, 16)
    return pl.pallas_call(
        functools.partial(exchange_kernel, groups, columns, per_group),
        out_shape=(
            jax.ShapeDtypeStruct((columns, uv_rows, 128), jnp.int32),
            jax.ShapeDtypeStruct((columns, 128), jnp.int32),
            jax.ShapeDtypeStruct((columns, resid_rows, 128), bf16),
        ),
        in_specs=[pl.BlockSpec(memory_space=pl.ANY)] * 7,
        out_specs=(pl.BlockSpec(memory_space=pl.ANY),) * 3,
        scratch_shapes=[
            pltpu.SMEM(slot_subgrid.shape, jnp.int32),
            pltpu.SMEM(vis_count.shape, jnp.int32),
            pltpu.SMEM(offset.shape, jnp.int32),
            pltpu.VMEM(uv.shape, f32),
            pltpu.VMEM(obs.shape, f32),
            pltpu.VMEM(weight.shape, f32),
            pltpu.VMEM((per_group, members, 2, side, side), bf16),
            pltpu.VMEM((across * side, 2 * kept), bf16),
            pltpu.VMEM((members, per_group // across, 2 * side, 2 * kept), bf16),
            [pltpu.VMEM((2 * kept, lanes), bf16)] * 2,
            pltpu.VMEM((groups, rows(2 * slots * tiles), 128), f32),
            pltpu.VMEM((groups, rows(3 * slots * tiles), 128), f32),
            pltpu.VMEM((uv_rows, 128), f32),
            pltpu.VMEM((columns, uv_rows, 128), f32),
            pltpu.VMEM((rows(2 * members * tiles), 128), f32),
            pltpu.VMEM((groups, rows(2 * members * tiles), 128), f32),
            pltpu.VMEM((resid_rows, 128), f32),
            pltpu.VMEM((resid_rows, 128), bf16),
            pltpu.VMEM((columns, uv_rows, 128), jnp.int32),
            pltpu.VMEM((columns, 128), jnp.int32),
            dma((6,)),
            dma((members,)),
            pltpu.SemaphoreType.REGULAR((max(columns.bit_length(), 1),)),
            dma((groups,)),
            dma((groups,)),
            dma((groups,)),
            dma((groups,)),
            dma((groups,)),
            dma((groups,)),
            dma((2,)),
            dma((2,)),
            dma((2,)),
            dma((3,)),
        ],
        compiler_params=pltpu.CompilerParams(collective_id=0, has_side_effects=True),
    )(slot_subgrid, vis_count, offset, contributions, uv, obs, weight)


def grid_call(phases, offsets, resid, per_group, members, lanes, side, rows, gain):
    base = -(-per_group * rows // 128) * 128
    half = side // 2
    return pl.pallas_call(
        functools.partial(grid_kernel, per_group, members, side, gain),
        out_shape=jax.ShapeDtypeStruct((per_group, 2, rows, WIN), jnp.float32),
        in_specs=[pl.BlockSpec(memory_space=pl.ANY)] * 3,
        out_specs=pl.BlockSpec(memory_space=pl.ANY),
        scratch_shapes=[
            pltpu.SMEM(offsets.shape, jnp.int32),
            pltpu.VMEM(phases.shape, jnp.int32),
            pltpu.VMEM(resid.shape, jnp.bfloat16),
            pltpu.VMEM((per_group, 2, rows, WIN), jnp.float32),
            pltpu.VMEM((base // 64, WIN + half, 128), jnp.float32),
            pltpu.VMEM((base // 64, WIN + half, 128), jnp.float32),
            [pltpu.VMEM((2 * base, lanes), jnp.bfloat16)] * 2,
            [pltpu.VMEM((2 * half, lanes), jnp.bfloat16)] * 2,
            [pltpu.VMEM((6, -(-per_group // 8) * 8, lanes), jnp.float32)] * 2,
            pltpu.VMEM(resid.shape, jnp.float32),
            pltpu.SMEM((offsets.shape[0] * members + 8,), jnp.int32),
            pltpu.SemaphoreType.DMA((3,)),
            pltpu.SemaphoreType.DMA((base // 64,)),
        ],
    )(offsets, phases, resid)


def body(contributions, slot_subgrid, vis_count, vis_uv, vis_obs, vis_weight, subgrid_offset):
    groups = lax.axis_size("facet")
    columns = lax.axis_size("sub")
    per_group, _, members, _, side, _ = contributions.shape
    lanes = vis_weight.shape[-1]
    phases, offsets, resid = exchange_call(
        groups,
        columns,
        slot_subgrid,
        vis_count,
        subgrid_offset,
        contributions,
        vis_uv,
        vis_obs,
        vis_weight,
    )
    gain = WIN / (side * math.sqrt(members * columns)) / math.sqrt(lanes)
    return grid_call(phases, offsets, resid, per_group, members, lanes, side, WIN // columns, gain)


def solution(mesh):
    placed = (
        P("facet", "sub", None, None, None, None),
        P("sub", None, None),
        P("facet", "sub", None),
        P("facet", "sub", None, None, None),
        P("facet", "sub", None, None, None),
        P("facet", "sub", None, None),
        P("sub", None, None),
    )
    return jax.shard_map(
        body, mesh=mesh, in_specs=placed, out_specs=P("facet", None, "sub", None), check_vma=False
    )
```

```python
import functools
import math

import jax
import jax.numpy as jnp
from jax import lax
from jax.experimental import pallas as pl
from jax.experimental.pallas import tpu as pltpu
from jax.sharding import PartitionSpec as P

SUBGRID = 512
FACET_SIDE = 4
WIN = 512
MESH = pl.DeviceIdType.MESH


def cmul(a, b):
    return a[0] * b[0] - a[1] * b[1], a[0] * b[1] + a[1] * b[0]


def row_iota(rows, lanes):
    return lax.broadcasted_iota(jnp.int32, (rows, lanes), 0)


SIN = (3.14159027, -5.16740673, 2.54401052, -0.55946246)
COS = (0.99999995, -4.93479283, 4.05841135, -1.33187657, 0.21968961)


def fraction(w):
    t = w * (1.0 / SUBGRID)
    t = t - jnp.where(t >= 0.5, 1.0, 0.0)
    return (t * 4294967296.0).astype(jnp.int32)


def wave(phase):
    t = phase.astype(jnp.float32) * (1.0 / 4294967296.0)
    q = t * t
    s = SIN[3]
    for a in SIN[2::-1]:
        s = s * q + a
    s = s * t
    c = COS[4]
    for a in COS[3::-1]:
        c = c * q + a
    s2 = s + s
    return 1.0 - s2 * s, s2 * c


def chebyshev(first, step, count):
    double = step[0] + step[0]
    seq = [first]
    if count > 1:
        seq.append(cmul(first, step))
    while len(seq) < count:
        seq.append(tuple(double * p - q for p, q in zip(seq[-1], seq[-2])))
    return seq


def fold_matrix(across, side, stride, fold):
    rows, cols = fold.shape
    kept = cols // 2
    low = side // 128 * 128
    high = side - low
    width = (across - 1) * stride + side
    spans = [(b, y, 64) for b in range(across) for y in range(0, low, 64)]
    spans += [(b, low, high) for b in range(across)]
    lines = lax.broadcasted_iota(jnp.int32, (64, 128), 0)
    lane = lax.broadcasted_iota(jnp.int32, (64, 128), 1)
    at = 0
    for b, y, count in spans:
        turn = 2 * (b * stride + y) - (width - 1) + 2 * lines
        sign = jnp.where(turn < 0, -1.0, 1.0)
        cell = lax.shift_right_arithmetic(jnp.abs(turn), 1) - lane
        for k in range(0, kept, 128):
            hit = cell == k
            fold[at : at + count, k : k + 128] = jnp.where(hit, 1.0, 0.0)[:count].astype(jnp.bfloat16)
            fold[at : at + count, kept + k : kept + k + 128] = jnp.where(hit, sign, 0.0)[:count].astype(
                jnp.bfloat16
            )
        at += count


def fold_image(c_ref, fold, images, j):
    per_group, _, _, side, _ = c_ref.shape
    across = min(per_group, FACET_SIDE)
    low = side // 128 * 128
    kept = fold.shape[1] // 2
    for a in range(per_group // across):
        for part in range(2):
            blocks = [c_ref[a * across + b, j, part] for b in range(across)]
            strip = jnp.concatenate([x[:, :low] for x in blocks] + [x[:, low:] for x in blocks], axis=1)
            res = jnp.dot(strip, fold[...], preferred_element_type=jnp.float32)
            images[j, a, part * side : (part + 1) * side, :kept] = res[:, :kept].astype(jnp.bfloat16)
            odd = res[:, kept:] if part == 1 else -res[:, kept:]
            images[j, a, (1 - part) * side : (2 - part) * side, kept:] = odd.astype(jnp.bfloat16)


def partial_model(first_a, first_b, stride, across, u, v, images, rhs):
    kept, lanes = rhs.shape[0] // 2, rhs.shape[1]
    side = images.shape[1] // 2
    width = (across - 1) * stride + side
    lines8 = row_iota(8, lanes)
    fu = fraction(u)
    hv = lax.shift_right_arithmetic(fraction(v), 1)

    def wide(x):
        return jnp.broadcast_to(x, (8, lanes))

    now = wave((2 * lines8 + 1) * hv)
    step = cmul(tuple(wide(t[7:8]) for t in now), tuple(wide(t[0:1]) for t in now))
    seq = chebyshev(now, step, kept // 8)
    for h in range(kept // 16):
        for part in range(2):
            both = jnp.concatenate([seq[2 * h][part], seq[2 * h + 1][part]], axis=0)
            rhs[part * kept + h * 16 : part * kept + (h + 1) * 16, :] = both.astype(jnp.bfloat16)

    now = wave(lines8 * fu)
    half = tuple(wide(t[4:5]) for t in now)
    seq = chebyshev(now, cmul(half, half), side // 8)
    model_r = jnp.zeros((1, lanes), jnp.float32)
    model_i = jnp.zeros((1, lanes), jnp.float32)
    for a in range(images.shape[0]):
        res = jnp.dot(images[a], rhs[...], preferred_element_type=jnp.float32)
        total_r = jnp.zeros((8, lanes), jnp.float32)
        total_i = jnp.zeros((8, lanes), jnp.float32)
        for h in range(side // 8):
            real = res[h * 8 : (h + 1) * 8]
            imag = res[side + h * 8 : side + (h + 1) * 8]
            c, s = seq[h]
            total_r = total_r + (c * real + s * imag)
            total_i = total_i + (c * imag - s * real)
        total_r = jnp.sum(total_r, axis=0, keepdims=True)
        total_i = jnp.sum(total_i, axis=0, keepdims=True)
        c, s = wave(((first_a + a) * stride) * fu + (2 * stride * first_b + (width - 1)) * hv)
        model_r = model_r + (c * total_r + s * total_i)
        model_i = model_i + (c * total_i - s * total_r)
    return model_r * (1.0 / SUBGRID), model_i * (1.0 / SUBGRID)


def exchange_kernel(
    groups,
    columns,
    per_group,
    table_hbm,
    count_hbm,
    off_hbm,
    c_hbm,
    uv_hbm,
    obs_hbm,
    weight_hbm,
    phase_ref,
    where_ref,
    resid_ref,
    table_ref,
    count_ref,
    off_ref,
    uv_ref,
    obs_ref,
    weight_ref,
    c_ref,
    fold,
    images,
    rhs,
    uv_all,
    ow_all,
    uv_mine,
    uv_cols,
    part_mine,
    part_all,
    resid_wide,
    resid_mine,
    phases,
    where,
    in_sem,
    c_sem,
    known,
    uv_send,
    uv_recv,
    ow_send,
    ow_recv,
    part_send,
    part_recv,
    high_sem,
    low_sem,
    resid_sem,
    out_sem,
):
    members = c_ref.shape[1]
    side = c_ref.shape[-1]
    slots = uv_ref.shape[2]
    lanes = uv_ref.shape[-1]
    tiles = lanes // 128
    across = min(per_group, FACET_SIDE)
    stride = (SUBGRID - side) // (FACET_SIDE - 1)
    group = lax.axis_index("facet")
    column = lax.axis_index("sub")
    barrier = pltpu.get_barrier_semaphore()
    rounds = columns.bit_length() - 1
    paired = columns == 1 << rounds
    low_bits = rounds // 2 if paired else 0
    low = 1 << low_bits
    high = columns // low
    order = list(range(low_bits, rounds)) + list(range(low_bits))
    mine_low = lax.rem(column, low)
    mine_high = lax.div(column, low)
    mine = mine_low * high + mine_high

    def peer_group(p):
        return lax.rem(group + p, groups)

    def peer_column(p):
        return lax.rem(column + p, columns)

    def partner(r):
        bit = 1 << r
        return column + bit - 2 * bit * lax.rem(lax.div(column, bit), 2)

    for p in range(1, groups):
        pl.semaphore_signal(barrier, inc=1, device_id={"facet": peer_group(p)}, device_id_type=MESH)
    near = [partner(r) for r in order] if paired else [peer_column(p) for p in range(1, columns)]
    for other in near:
        pl.semaphore_signal(barrier, inc=1, device_id={"sub": other}, device_id_type=MESH)

    def tell(r):
        if paired and 1 <= r < rounds:
            pl.semaphore_signal(known.at[r], inc=1, device_id={"sub": partner(order[r])}, device_id_type=MESH)

    def hear(r):
        if paired and 1 <= r < rounds:
            pl.semaphore_wait(known.at[r], 1)

    smalls = [
        pltpu.make_async_copy(src, dst, in_sem.at[i])
        for i, (src, dst) in enumerate(
            (
                (uv_hbm, uv_ref),
                (count_hbm, count_ref),
                (obs_hbm, obs_ref),
                (weight_hbm, weight_ref),
                (table_hbm, table_ref),
                (off_hbm, off_ref),
            )
        )
    ]
    loads = [
        pltpu.make_async_copy(c_hbm.at[:, 0, j], c_ref.at[:, j], c_sem.at[j]) for j in range(members)
    ]
    for load in smalls + loads:
        load.start()
    fold_matrix(across, side, stride, fold)
    for load in smalls:
        load.wait()

    lane = lax.broadcasted_iota(jnp.int32, (1, 128), 1)
    for k in range(slots):
        for i in range(tiles):
            part = slice(128 * i, 128 * (i + 1))
            for p in range(2):
                uv_all[group, (2 * k + p) * tiles + i : (2 * k + p) * tiles + i + 1, :] = uv_ref[0, 0, k, p : p + 1, part]
                ow_all[group, (3 * k + p) * tiles + i : (3 * k + p) * tiles + i + 1, :] = obs_ref[0, 0, k, p : p + 1, part]
            live = jnp.where(lane + 128 * i < count_ref[0, 0, k], 1.0, 0.0)
            at = (3 * k + 2) * tiles + i
            ow_all[group, at : at + 1, :] = weight_ref[0, 0, k : k + 1, part] * live
    pl.semaphore_wait(barrier, groups - 1 + len(near))
    tell(1)

    def to_group(buf, send, recv, p):
        return pltpu.make_async_remote_copy(
            src_ref=buf.at[group],
            dst_ref=buf.at[group],
            send_sem=send.at[p],
            recv_sem=recv.at[p],
            device_id={"facet": peer_group(p)},
            device_id_type=MESH,
        )

    def each_group(buf, send, recv, act):
        @pl.loop(1, groups)
        def _(p):
            act(to_group(buf, send, recv, p))

    def send(src, dst, sems, other):
        copy = pltpu.make_async_remote_copy(
            src_ref=src,
            dst_ref=dst,
            send_sem=sems.at[0],
            recv_sem=sems.at[1],
            device_id={"sub": other},
            device_id_type=MESH,
        )
        copy.start()

    def send_high():
        for p in range(1, high):
            other = lax.rem(mine_high + p, high) * low + mine_low
            send(uv_mine, uv_cols.at[mine], high_sem, other)

    def send_low():
        block = uv_cols.at[pl.ds(mine_low * high, high)]
        for p in range(1, low):
            send(block, block, low_sem, mine_high * low + lax.rem(mine_low + p, low))

    def send_resid():
        @pl.loop(1, columns)
        def _(p):
            send(resid_mine, resid_ref.at[column], resid_sem, peer_column(p))

    def wait_bytes(dst, count, sem):
        if count > 0:
            shown = dst.at[pl.ds(0, count)]
            pltpu.make_async_copy(shown, shown, sem).wait()

    def start(copy):
        copy.start()

    def wait(copy):
        copy.wait()

    each_group(uv_all, uv_send, uv_recv, start)
    each_group(ow_all, ow_send, ow_recv, start)
    for load in loads:
        load.wait()
    if members <= 2:
        for j in range(members):
            fold_image(c_ref, fold, images, j)
    else:

        @pl.loop(0, members)
        def _(j):
            fold_image(c_ref, fold, images, j)

    each_group(uv_all, uv_send, uv_recv, wait)

    def holds(g, k, j):
        return jnp.where(table_ref[0, g, k] == j, 1.0, 0.0)

    spots = jnp.zeros((1, 128), jnp.float32)
    for j in range(members):
        picked = jnp.zeros((2 * tiles, 128), jnp.float32)
        for g in range(groups):
            for k in range(slots):
                at = 2 * tiles * k
                picked = picked + uv_all[g, at : at + 2 * tiles, :] * holds(g, k, j)
        uv_mine[2 * tiles * j : 2 * tiles * (j + 1), :] = picked
        for axis in range(2):
            spots = jnp.where(lane == 2 * j + axis, off_ref[0, j, axis].astype(jnp.float32), spots)
    place = 2 * tiles * members
    uv_mine[place : place + 1, :] = spots
    uv_cols[mine] = uv_mine[...]
    for r in range(1, rounds - low_bits):
        hear(r)
        tell(r + 1)
    send_high()

    first_a = lax.div(group * per_group, FACET_SIDE)
    first_b = lax.rem(group * per_group, FACET_SIDE)

    def models(j, slot):
        at = 2 * tiles * j
        u = jnp.concatenate([uv_mine[pl.ds(at + i, 1), :] for i in range(tiles)], axis=1)
        v = jnp.concatenate([uv_mine[pl.ds(at + tiles + i, 1), :] for i in range(tiles)], axis=1)
        both = partial_model(first_a, first_b, stride, across, u, v, images.at[j], rhs[slot])
        for p in range(2):
            for i in range(tiles):
                part_mine[pl.ds(at + p * tiles + i, 1), :] = both[p][:, 128 * i : 128 * (i + 1)]

    if members <= 2:
        for j in range(members):
            models(j, j % 2)
    else:

        @pl.loop(0, members)
        def _(j):
            models(j, 0)

    part_all[group] = part_mine[...]
    each_group(part_all, part_send, part_recv, start)
    for r in range(max(rounds - low_bits, 1), rounds):
        hear(r)
        tell(r + 1)
    wait_bytes(uv_cols, high - 1, high_sem.at[1])
    send_low()
    each_group(ow_all, ow_send, ow_recv, wait)
    each_group(part_all, part_send, part_recv, wait)

    for j in range(members):
        picked = jnp.zeros((3 * tiles, 128), jnp.float32)
        model = jnp.zeros((2 * tiles, 128), jnp.float32)
        at = 2 * tiles * j
        for g in range(groups):
            model = model + part_all[g, at : at + 2 * tiles, :]
            for k in range(slots):
                first = 3 * tiles * k
                picked = picked + ow_all[g, first : first + 3 * tiles, :] * holds(g, k, j)
        weight = picked[2 * tiles :]
        weight = jnp.concatenate([weight, weight], axis=0)
        resid_wide[at : at + 2 * tiles, :] = weight * (picked[: 2 * tiles] - model)
    resid_mine[...] = resid_wide[...].astype(jnp.bfloat16)
    send_resid()
    own = pltpu.make_async_copy(resid_mine, resid_ref.at[column], out_sem.at[0])
    own.start()

    wait_bytes(uv_cols, columns - high, low_sem.at[1])
    row = row_iota(uv_cols.shape[1], 128)
    halved = lax.rem(row, 2 * tiles) >= tiles
    for i in range(columns):
        c = i % high * low + i // high
        full = fraction(uv_cols[i])
        phases[c] = jnp.where(halved, lax.shift_right_arithmetic(full, 1), full)
        where[c : c + 1, :] = uv_cols[i, place : place + 1, :].astype(jnp.int32)
    outs = [
        pltpu.make_async_copy(phases, phase_ref, out_sem.at[1]),
        pltpu.make_async_copy(where, where_ref, out_sem.at[2]),
    ]
    for out in outs:
        out.start()
    wait_bytes(uv_cols, high - 1, high_sem.at[0])
    wait_bytes(uv_cols, columns - high, low_sem.at[0])
    for out in [own] + outs:
        out.wait()
    wait_bytes(resid_ref, columns - 1, resid_sem.at[0])
    wait_bytes(resid_ref, columns - 1, resid_sem.at[1])


def grid_kernel(
    per_group,
    members,
    side,
    gain,
    off_hbm,
    phase_hbm,
    resid_hbm,
    out_hbm,
    off_ref,
    phase_ref,
    resid_ref,
    out_ref,
    front,
    back,
    lefts,
    rights,
    readies,
    resid_f,
    hits,
    in_sem,
    out_sem,
):
    loads = [
        pltpu.make_async_copy(off_hbm, off_ref, in_sem.at[0]),
        pltpu.make_async_copy(phase_hbm, phase_ref, in_sem.at[1]),
        pltpu.make_async_copy(resid_hbm, resid_ref, in_sem.at[2]),
    ]
    for load in loads:
        load.start()
    columns = phase_ref.shape[0]
    lanes = lefts[0].shape[1]
    tiles = lanes // 128
    rows = out_ref.shape[2]
    chunks = front.shape[0] // 2
    half = side // 2
    base = lefts[0].shape[0] // 2
    stride = (SUBGRID - side) // (FACET_SIDE - 1)
    facet_here = lax.axis_index("facet") * per_group
    first_line = lax.axis_index("sub") * rows
    facet_rows = readies[0].shape[1]
    first_a = lax.div(facet_here, FACET_SIDE)
    lines8 = row_iota(8, lanes)
    across = min(per_group, FACET_SIDE)
    deep = per_group // across
    mirrored = rows % 16 == 0 and across % 2 == 0 and deep + across // 2 <= facet_rows
    row = row_iota(facet_rows, lanes)
    if mirrored:
        first_b = lax.rem(facet_here, FACET_SIDE)
        middle = stride * (2 * first_b + across - 1) + (side - 1)
        lead_u = jnp.where(row < deep, row * stride, 0)
        lead_v = jnp.where(row < deep, middle, stride * (2 * (row - deep) + 1))
    else:
        facet = row + facet_here
        lead_u = (lax.div(facet, FACET_SIDE) - first_a) * stride
        lead_v = lax.rem(facet, FACET_SIDE) * (2 * stride) + (side - 1)
    front[...] = jnp.zeros_like(front)
    back[...] = jnp.zeros_like(back)
    if base > per_group * rows:
        for left in lefts:
            left[...] = jnp.zeros_like(left)
    for load in loads:
        load.wait()
    resid_f[...] = resid_ref[...].astype(jnp.float32)

    total = columns * members

    def begin(s):
        start = lax.rem(first_line - off_ref[lax.div(s, members), 2 * lax.rem(s, members)] + WIN, WIN)
        return jnp.where(start > WIN - rows, start - WIN, start)

    def scan(s, found):
        hits[found] = s
        ahead = first_line + (WIN + rows - 1) - off_ref[lax.div(s, members), 2 * lax.rem(s, members)]
        return found + jnp.where(lax.bitwise_and(ahead, WIN - 1) < side + rows - 1, 1, 0)

    if total <= 64:
        found = jnp.int32(0)
        for s in range(total):
            hits[found] = s
            ahead = first_line + (WIN + rows - 1) - off_ref[s // members, 2 * (s % members)]
            found = found + jnp.where(lax.bitwise_and(ahead, WIN - 1) < side + rows - 1, 1, 0)
    else:
        found = lax.fori_loop(0, total, scan, jnp.int32(0), unroll=8)

    def wide(x):
        return jnp.broadcast_to(x, (8, lanes))

    def conj_mul(a, b):
        return a[0] * b[0] + a[1] * b[1], a[1] * b[0] - a[0] * b[1]

    def lane_row(ref, c, at):
        return jnp.concatenate([ref[c, pl.ds(at + i, 1), :] for i in range(tiles)], axis=1)

    def choose(index):
        return jnp.where(index < found, hits[jnp.minimum(index, total - 1)], 0)

    def column_of(index):
        s = choose(index)
        return off_ref[lax.div(s, members), 2 * lax.rem(s, members) + 1]

    def prepare(index, ready):
        s = choose(index)
        scale = jnp.where(index < found, gain, 0.0)
        column = lax.div(s, members)
        j = lax.rem(s, members)
        fu = lane_row(phase_ref, column, 2 * tiles * j)
        hv = lane_row(phase_ref, column, 2 * tiles * j + tiles)
        rr = lane_row(resid_f, column, 2 * tiles * j) * scale
        ri = lane_row(resid_f, column, 2 * tiles * j + tiles) * scale
        plain = wave(lead_u * fu + lead_v * hv)
        head = cmul(plain, (rr, ri))
        abreast = wave((2 * lines8 + 1) * hv)
        along = wave((lines8 + (begin(s) + first_a * stride)) * fu)
        for part in range(2):
            ready[part] = head[part]
            ready[2 + part, :8] = abreast[part]
            ready[6 + part] = plain[part]
            ready[4 + part, :8] = along[part]

    def fill(index, ready, left, right):
        start = begin(choose(index))
        now = ready[2, :8], ready[3, :8]
        step = cmul(tuple(wide(t[7:8]) for t in now), tuple(wide(t[0:1]) for t in now))
        seq = chebyshev(now, step, half // 8)
        for h in range(half // 16):
            for part in range(2):
                both = jnp.concatenate([seq[2 * h][part], seq[2 * h + 1][part]], axis=0)
                right[part * half + h * 16 : part * half + (h + 1) * 16, :] = both.astype(jnp.bfloat16)

        now = ready[4, :8], ready[5, :8]
        step = conj_mul(tuple(wide(t[4:5]) for t in now), tuple(wide(t[0:1]) for t in now))
        step = cmul(step, step)
        seq = chebyshev(now, step, rows // 8)
        shown = []
        for h in range(rows // 8):
            cell = lines8 + (h * 8 + start)
            live = (cell >= 0) & (cell < side)
            shown.append(tuple(jnp.where(live, t, 0.0) for t in seq[h]))
        tall = min(rows, 16)
        per = 16 // tall
        if per == 2:
            table = [tuple(jnp.concatenate([t, t], axis=0).astype(jnp.bfloat16) for t in shown[0])]
        else:
            table = [
                tuple(jnp.concatenate([p, q], axis=0).astype(jnp.bfloat16) for p, q in zip(a, b))
                for a, b in zip(shown[0::2], shown[1::2])
            ]

        def spread(at, line):
            return tuple(
                jnp.broadcast_to(ready[at + part, line : line + 1, :], (16, lanes)).astype(jnp.bfloat16)
                for part in range(2)
            )

        def put(f, h, real, imag):
            at = f * rows + h * 16
            left[at : at + 16, :] = real
            left[base + at : base + at + 16, :] = imag

        if mirrored:
            turn = [spread(6, deep + k) for k in range(across // 2)]
            for a in range(deep):
                own = spread(0, a)
                for h, t in enumerate(table):
                    real, imag = cmul(t, own)
                    for k, (c, sn) in enumerate(turn):
                        upper = a * across + across // 2 + k
                        lower = a * across + across // 2 - 1 - k
                        rc, rs, ic, si = real * c, real * sn, imag * c, imag * sn
                        put(upper, h, rc - si, ic + rs)
                        put(lower, h, rc + si, ic - rs)
            return
        for f in range(0, per_group, per):
            own = tuple(
                jnp.concatenate(
                    [jnp.broadcast_to(ready[part, f + i : f + i + 1, :], (tall, lanes)) for i in range(per)], axis=0
                ).astype(jnp.bfloat16)
                for part in range(2)
            )
            for h, t in enumerate(table):
                at = f * rows + h * 16
                value = cmul(t, own)
                left[at : at + 16, :] = value[0]
                left[base + at : base + at + 16, :] = value[1]

    def add(index, left, right):
        offset = column_of(index)
        prod = lax.dot_general(
            right[...], left[...], (((1,), (1,)), ((), ())), preferred_element_type=jnp.float32
        )
        ahead = pl.ds(offset, half)
        behind = pl.ds(WIN - offset, half)
        for k in range(chunks):
            real = slice(128 * k, 128 * (k + 1))
            imag = slice(base + 128 * k, base + 128 * (k + 1))
            front[k, ahead, :] += prod[:half, real] - prod[half:, imag]
            back[k, behind, :] += prod[:half, real] + prod[half:, imag]
            front[chunks + k, ahead, :] += prod[:half, imag] + prod[half:, real]
            back[chunks + k, behind, :] += prod[:half, imag] - prod[half:, real]

    def pair(i, carry):
        add(2 * i, lefts[0], rights[0])
        fill(2 * i + 1, readies[1], lefts[1], rights[1])
        add(2 * i + 1, lefts[1], rights[1])
        fill(2 * i + 2, readies[0], lefts[0], rights[0])
        prepare(2 * i + 3, readies[1])
        prepare(2 * i + 4, readies[0])
        return carry

    prepare(0, readies[0])
    prepare(1, readies[1])
    fill(0, readies[0], lefts[0], rights[0])
    prepare(2, readies[0])
    lax.fori_loop(0, lax.div(found + 1, 2), pair, 0)

    turned = 7 - row_iota(8, 128)
    done = []
    for part in range(2):
        for k in range(chunks):
            x = front.at[part * chunks + k]
            y = back.at[part * chunks + k]
            ahead = [x[WIN - half : WIN], x[0:half] + x[WIN : WIN + half], x[half : WIN - half]]
            behind = []
            for at in range(WIN + half - 8, half - 8, -8):
                tile = y[at : at + 8]
                if at >= WIN:
                    tile = tile + y[at - WIN : at - WIN + 8]
                behind.append(jnp.take_along_axis(tile, turned, axis=0))
            whole = (jnp.concatenate(ahead, axis=0) + jnp.concatenate(behind, axis=0)).T
            facets = [f for f in range(per_group) if 0 <= f * rows - 128 * k < 128]
            for f in facets:
                at = f * rows - 128 * k
                out_ref[f, part] = whole[at : at + rows]
            if facets:
                some = pl.ds(facets[0], len(facets))
                copy = pltpu.make_async_copy(
                    out_ref.at[some, part], out_hbm.at[some, part], out_sem.at[part * chunks + k]
                )
                copy.start()
                done.append(copy)
    for copy in done:
        copy.wait()


def exchange_call(groups, columns, slot_subgrid, vis_count, offset, contributions, uv, obs, weight):
    per_group, _, members, _, side, _ = contributions.shape
    slots, lanes = weight.shape[2:]
    tiles = lanes // 128
    across = min(per_group, FACET_SIDE)
    width = (SUBGRID - side) // (FACET_SIDE - 1) * (across - 1) + side
    kept = -(-width // 256) * 128
    dma = pltpu.SemaphoreType.DMA
    f32, bf16 = jnp.float32, jnp.bfloat16

    def rows(n, unit=8):
        return -(-n // unit) * unit

    uv_rows = 2 * members * tiles + 1
    resid_rows = rows(2 * members * tiles, 16)
    return pl.pallas_call(
        functools.partial(exchange_kernel, groups, columns, per_group),
        out_shape=(
            jax.ShapeDtypeStruct((columns, uv_rows, 128), jnp.int32),
            jax.ShapeDtypeStruct((columns, 128), jnp.int32),
            jax.ShapeDtypeStruct((columns, resid_rows, 128), bf16),
        ),
        in_specs=[pl.BlockSpec(memory_space=pl.ANY)] * 7,
        out_specs=(pl.BlockSpec(memory_space=pl.ANY),) * 3,
        scratch_shapes=[
            pltpu.SMEM(slot_subgrid.shape, jnp.int32),
            pltpu.SMEM(vis_count.shape, jnp.int32),
            pltpu.SMEM(offset.shape, jnp.int32),
            pltpu.VMEM(uv.shape, f32),
            pltpu.VMEM(obs.shape, f32),
            pltpu.VMEM(weight.shape, f32),
            pltpu.VMEM((per_group, members, 2, side, side), bf16),
            pltpu.VMEM((across * side, 2 * kept), bf16),
            pltpu.VMEM((members, per_group // across, 2 * side, 2 * kept), bf16),
            [pltpu.VMEM((2 * kept, lanes), bf16)] * 2,
            pltpu.VMEM((groups, rows(2 * slots * tiles), 128), f32),
            pltpu.VMEM((groups, rows(3 * slots * tiles), 128), f32),
            pltpu.VMEM((uv_rows, 128), f32),
            pltpu.VMEM((columns, uv_rows, 128), f32),
            pltpu.VMEM((rows(2 * members * tiles), 128), f32),
            pltpu.VMEM((groups, rows(2 * members * tiles), 128), f32),
            pltpu.VMEM((resid_rows, 128), f32),
            pltpu.VMEM((resid_rows, 128), bf16),
            pltpu.VMEM((columns, uv_rows, 128), jnp.int32),
            pltpu.VMEM((columns, 128), jnp.int32),
            dma((6,)),
            dma((members,)),
            pltpu.SemaphoreType.REGULAR((max(columns.bit_length(), 1),)),
            dma((groups,)),
            dma((groups,)),
            dma((groups,)),
            dma((groups,)),
            dma((groups,)),
            dma((groups,)),
            dma((2,)),
            dma((2,)),
            dma((2,)),
            dma((3,)),
        ],
        compiler_params=pltpu.CompilerParams(collective_id=0, has_side_effects=True),
    )(slot_subgrid, vis_count, offset, contributions, uv, obs, weight)


def grid_call(phases, offsets, resid, per_group, members, lanes, side, rows, gain):
    base = -(-per_group * rows // 128) * 128
    half = side // 2
    return pl.pallas_call(
        functools.partial(grid_kernel, per_group, members, side, gain),
        out_shape=jax.ShapeDtypeStruct((per_group, 2, rows, WIN), jnp.float32),
        in_specs=[pl.BlockSpec(memory_space=pl.ANY)] * 3,
        out_specs=pl.BlockSpec(memory_space=pl.ANY),
        scratch_shapes=[
            pltpu.SMEM(offsets.shape, jnp.int32),
            pltpu.VMEM(phases.shape, jnp.int32),
            pltpu.VMEM(resid.shape, jnp.bfloat16),
            pltpu.VMEM((per_group, 2, rows, WIN), jnp.float32),
            pltpu.VMEM((base // 64, WIN + half, 128), jnp.float32),
            pltpu.VMEM((base // 64, WIN + half, 128), jnp.float32),
            [pltpu.VMEM((2 * base, lanes), jnp.bfloat16)] * 2,
            [pltpu.VMEM((2 * half, lanes), jnp.bfloat16)] * 2,
            [pltpu.VMEM((8, -(-per_group // 8) * 8, lanes), jnp.float32)] * 2,
            pltpu.VMEM(resid.shape, jnp.float32),
            pltpu.SMEM((offsets.shape[0] * members + 8,), jnp.int32),
            pltpu.SemaphoreType.DMA((3,)),
            pltpu.SemaphoreType.DMA((base // 64,)),
        ],
    )(offsets, phases, resid)


def body(contributions, slot_subgrid, vis_count, vis_uv, vis_obs, vis_weight, subgrid_offset):
    groups = lax.axis_size("facet")
    columns = lax.axis_size("sub")
    per_group, _, members, _, side, _ = contributions.shape
    lanes = vis_weight.shape[-1]
    phases, offsets, resid = exchange_call(
        groups,
        columns,
        slot_subgrid,
        vis_count,
        subgrid_offset,
        contributions,
        vis_uv,
        vis_obs,
        vis_weight,
    )
    gain = WIN / (side * math.sqrt(members * columns)) / math.sqrt(lanes)
    return grid_call(phases, offsets, resid, per_group, members, lanes, side, WIN // columns, gain)


def solution(mesh):
    placed = (
        P("facet", "sub", None, None, None, None),
        P("sub", None, None),
        P("facet", "sub", None),
        P("facet", "sub", None, None, None),
        P("facet", "sub", None, None, None),
        P("facet", "sub", None, None),
        P("sub", None, None),
    )
    return jax.shard_map(
        body, mesh=mesh, in_specs=placed, out_specs=P("facet", None, "sub", None), check_vma=False
    )
```

```python
import functools
import math

import jax
import jax.numpy as jnp
from jax import lax
from jax.experimental import pallas as pl
from jax.experimental.pallas import tpu as pltpu
from jax.sharding import PartitionSpec as P

SUBGRID = 512
FACET_SIDE = 4
WIN = 512
MESH = pl.DeviceIdType.MESH


def cmul(a, b):
    return a[0] * b[0] - a[1] * b[1], a[0] * b[1] + a[1] * b[0]


def row_iota(rows, lanes):
    return lax.broadcasted_iota(jnp.int32, (rows, lanes), 0)


SIN = (3.14159027, -5.16740673, 2.54401052, -0.55946246)
COS = (0.99999995, -4.93479283, 4.05841135, -1.33187657, 0.21968961)


def fraction(w):
    t = w * (1.0 / SUBGRID)
    t = t - jnp.where(t >= 0.5, 1.0, 0.0)
    return (t * 4294967296.0).astype(jnp.int32)


def wave(phase):
    t = phase.astype(jnp.float32) * (1.0 / 4294967296.0)
    q = t * t
    s = SIN[3]
    for a in SIN[2::-1]:
        s = s * q + a
    s = s * t
    c = COS[4]
    for a in COS[3::-1]:
        c = c * q + a
    s2 = s + s
    return 1.0 - s2 * s, s2 * c


def chebyshev(first, step, count):
    double = step[0] + step[0]
    seq = [first]
    if count > 1:
        seq.append(cmul(first, step))
    while len(seq) < count:
        seq.append(tuple(double * p - q for p, q in zip(seq[-1], seq[-2])))
    return seq


def fold_matrix(across, side, stride, fold):
    rows, cols = fold.shape
    kept = cols // 2
    low = side // 128 * 128
    high = side - low
    width = (across - 1) * stride + side
    spans = [(b, y, 64) for b in range(across) for y in range(0, low, 64)]
    spans += [(b, low, high) for b in range(across)]
    lines = lax.broadcasted_iota(jnp.int32, (64, 128), 0)
    lane = lax.broadcasted_iota(jnp.int32, (64, 128), 1)
    at = 0
    for b, y, count in spans:
        turn = 2 * (b * stride + y) - (width - 1) + 2 * lines
        sign = jnp.where(turn < 0, -1.0, 1.0)
        cell = lax.shift_right_arithmetic(jnp.abs(turn), 1) - lane
        for k in range(0, kept, 128):
            hit = cell == k
            fold[at : at + count, k : k + 128] = jnp.where(hit, 1.0, 0.0)[:count].astype(jnp.bfloat16)
            fold[at : at + count, kept + k : kept + k + 128] = jnp.where(hit, sign, 0.0)[:count].astype(
                jnp.bfloat16
            )
        at += count


def fold_image(c_ref, fold, images, j):
    per_group, _, _, side, _ = c_ref.shape
    across = min(per_group, FACET_SIDE)
    low = side // 128 * 128
    kept = fold.shape[1] // 2
    for a in range(per_group // across):
        for part in range(2):
            blocks = [c_ref[a * across + b, j, part] for b in range(across)]
            strip = jnp.concatenate([x[:, :low] for x in blocks] + [x[:, low:] for x in blocks], axis=1)
            res = jnp.dot(strip, fold[...], preferred_element_type=jnp.float32)
            images[j, a, part * side : (part + 1) * side, :kept] = res[:, :kept].astype(jnp.bfloat16)
            odd = res[:, kept:] if part == 1 else -res[:, kept:]
            images[j, a, (1 - part) * side : (2 - part) * side, kept:] = odd.astype(jnp.bfloat16)


def partial_model(first_a, first_b, stride, across, u, v, images, rhs):
    kept, lanes = rhs.shape[0] // 2, rhs.shape[1]
    side = images.shape[1] // 2
    width = (across - 1) * stride + side
    lines8 = row_iota(8, lanes)
    fu = fraction(u)
    hv = lax.shift_right_arithmetic(fraction(v), 1)

    def wide(x):
        return jnp.broadcast_to(x, (8, lanes))

    now = wave((2 * lines8 + 1) * hv)
    step = cmul(tuple(wide(t[7:8]) for t in now), tuple(wide(t[0:1]) for t in now))
    seq = chebyshev(now, step, kept // 8)
    for h in range(kept // 16):
        for part in range(2):
            both = jnp.concatenate([seq[2 * h][part], seq[2 * h + 1][part]], axis=0)
            rhs[part * kept + h * 16 : part * kept + (h + 1) * 16, :] = both.astype(jnp.bfloat16)

    now = wave(lines8 * fu)
    half = tuple(wide(t[4:5]) for t in now)
    seq = chebyshev(now, cmul(half, half), side // 8)
    model_r = jnp.zeros((1, lanes), jnp.float32)
    model_i = jnp.zeros((1, lanes), jnp.float32)
    for a in range(images.shape[0]):
        res = jnp.dot(images[a], rhs[...], preferred_element_type=jnp.float32)
        total_r = jnp.zeros((8, lanes), jnp.float32)
        total_i = jnp.zeros((8, lanes), jnp.float32)
        for h in range(side // 8):
            real = res[h * 8 : (h + 1) * 8]
            imag = res[side + h * 8 : side + (h + 1) * 8]
            c, s = seq[h]
            total_r = total_r + (c * real + s * imag)
            total_i = total_i + (c * imag - s * real)
        total_r = jnp.sum(total_r, axis=0, keepdims=True)
        total_i = jnp.sum(total_i, axis=0, keepdims=True)
        c, s = wave(((first_a + a) * stride) * fu + (2 * stride * first_b + (width - 1)) * hv)
        model_r = model_r + (c * total_r + s * total_i)
        model_i = model_i + (c * total_i - s * total_r)
    return model_r * (1.0 / SUBGRID), model_i * (1.0 / SUBGRID)


def exchange_kernel(
    groups,
    columns,
    per_group,
    table_hbm,
    count_hbm,
    off_hbm,
    c_hbm,
    uv_hbm,
    obs_hbm,
    weight_hbm,
    phase_ref,
    where_ref,
    resid_ref,
    table_ref,
    count_ref,
    off_ref,
    uv_ref,
    obs_ref,
    weight_ref,
    c_ref,
    fold,
    images,
    rhs,
    uv_all,
    ow_all,
    uv_mine,
    uv_cols,
    part_mine,
    part_all,
    resid_wide,
    resid_mine,
    phases,
    where,
    in_sem,
    c_sem,
    known,
    uv_send,
    uv_recv,
    ow_send,
    ow_recv,
    part_send,
    part_recv,
    high_sem,
    low_sem,
    resid_sem,
    out_sem,
):
    members = c_ref.shape[1]
    side = c_ref.shape[-1]
    slots = uv_ref.shape[2]
    lanes = uv_ref.shape[-1]
    tiles = lanes // 128
    across = min(per_group, FACET_SIDE)
    stride = (SUBGRID - side) // (FACET_SIDE - 1)
    group = lax.axis_index("facet")
    column = lax.axis_index("sub")
    barrier = pltpu.get_barrier_semaphore()
    rounds = columns.bit_length() - 1
    paired = columns == 1 << rounds
    low_bits = rounds // 2 if paired else 0
    low = 1 << low_bits
    high = columns // low
    order = list(range(low_bits, rounds)) + list(range(low_bits))
    mine_low = lax.rem(column, low)
    mine_high = lax.div(column, low)
    mine = mine_low * high + mine_high

    def peer_group(p):
        return lax.rem(group + p, groups)

    def peer_column(p):
        return lax.rem(column + p, columns)

    def partner(r):
        bit = 1 << r
        return column + bit - 2 * bit * lax.rem(lax.div(column, bit), 2)

    for p in range(1, groups):
        pl.semaphore_signal(barrier, inc=1, device_id={"facet": peer_group(p)}, device_id_type=MESH)
    near = [partner(r) for r in order] if paired else [peer_column(p) for p in range(1, columns)]
    for other in near:
        pl.semaphore_signal(barrier, inc=1, device_id={"sub": other}, device_id_type=MESH)

    def tell(r):
        if paired and 1 <= r < rounds:
            pl.semaphore_signal(known.at[r], inc=1, device_id={"sub": partner(order[r])}, device_id_type=MESH)

    def hear(r):
        if paired and 1 <= r < rounds:
            pl.semaphore_wait(known.at[r], 1)

    smalls = [
        pltpu.make_async_copy(src, dst, in_sem.at[i])
        for i, (src, dst) in enumerate(
            (
                (uv_hbm, uv_ref),
                (count_hbm, count_ref),
                (obs_hbm, obs_ref),
                (weight_hbm, weight_ref),
                (table_hbm, table_ref),
                (off_hbm, off_ref),
            )
        )
    ]
    loads = [
        pltpu.make_async_copy(c_hbm.at[:, 0, j], c_ref.at[:, j], c_sem.at[j]) for j in range(members)
    ]
    for load in smalls + loads:
        load.start()
    fold_matrix(across, side, stride, fold)
    for load in smalls:
        load.wait()

    lane = lax.broadcasted_iota(jnp.int32, (1, 128), 1)
    for k in range(slots):
        for i in range(tiles):
            part = slice(128 * i, 128 * (i + 1))
            for p in range(2):
                uv_all[group, (2 * k + p) * tiles + i : (2 * k + p) * tiles + i + 1, :] = uv_ref[0, 0, k, p : p + 1, part]
                ow_all[group, (3 * k + p) * tiles + i : (3 * k + p) * tiles + i + 1, :] = obs_ref[0, 0, k, p : p + 1, part]
            live = jnp.where(lane + 128 * i < count_ref[0, 0, k], 1.0, 0.0)
            at = (3 * k + 2) * tiles + i
            ow_all[group, at : at + 1, :] = weight_ref[0, 0, k : k + 1, part] * live
    pl.semaphore_wait(barrier, groups - 1 + len(near))
    tell(1)

    def to_group(buf, send, recv, p):
        return pltpu.make_async_remote_copy(
            src_ref=buf.at[group],
            dst_ref=buf.at[group],
            send_sem=send.at[p],
            recv_sem=recv.at[p],
            device_id={"facet": peer_group(p)},
            device_id_type=MESH,
        )

    def each_group(buf, send, recv, act):
        @pl.loop(1, groups)
        def _(p):
            act(to_group(buf, send, recv, p))

    def send(src, dst, sems, other):
        copy = pltpu.make_async_remote_copy(
            src_ref=src,
            dst_ref=dst,
            send_sem=sems.at[0],
            recv_sem=sems.at[1],
            device_id={"sub": other},
            device_id_type=MESH,
        )
        copy.start()

    def send_high():
        for p in range(1, high):
            other = lax.rem(mine_high + p, high) * low + mine_low
            send(uv_mine, uv_cols.at[mine], high_sem, other)

    def send_low():
        block = uv_cols.at[pl.ds(mine_low * high, high)]
        for p in range(1, low):
            send(block, block, low_sem, mine_high * low + lax.rem(mine_low + p, low))

    def send_resid():
        @pl.loop(1, columns)
        def _(p):
            send(resid_mine, resid_ref.at[column], resid_sem, peer_column(p))

    def wait_bytes(dst, count, sem):
        if count > 0:
            shown = dst.at[pl.ds(0, count)]
            pltpu.make_async_copy(shown, shown, sem).wait()

    def start(copy):
        copy.start()

    def wait(copy):
        copy.wait()

    each_group(uv_all, uv_send, uv_recv, start)
    for load in loads:
        load.wait()
    if members <= 2:
        for j in range(members):
            fold_image(c_ref, fold, images, j)
    else:

        @pl.loop(0, members)
        def _(j):
            fold_image(c_ref, fold, images, j)

    each_group(uv_all, uv_send, uv_recv, wait)

    def holds(g, k, j):
        return jnp.where(table_ref[0, g, k] == j, 1.0, 0.0)

    spots = jnp.zeros((1, 128), jnp.float32)
    for j in range(members):
        picked = jnp.zeros((2 * tiles, 128), jnp.float32)
        for g in range(groups):
            for k in range(slots):
                at = 2 * tiles * k
                picked = picked + uv_all[g, at : at + 2 * tiles, :] * holds(g, k, j)
        uv_mine[2 * tiles * j : 2 * tiles * (j + 1), :] = picked
        for axis in range(2):
            spots = jnp.where(lane == 2 * j + axis, off_ref[0, j, axis].astype(jnp.float32), spots)
    place = 2 * tiles * members
    uv_mine[place : place + 1, :] = spots
    uv_cols[mine] = uv_mine[...]
    for r in range(1, rounds - low_bits):
        hear(r)
        tell(r + 1)
    send_high()
    each_group(ow_all, ow_send, ow_recv, start)

    first_a = lax.div(group * per_group, FACET_SIDE)
    first_b = lax.rem(group * per_group, FACET_SIDE)

    def models(j, slot):
        at = 2 * tiles * j
        u = jnp.concatenate([uv_mine[pl.ds(at + i, 1), :] for i in range(tiles)], axis=1)
        v = jnp.concatenate([uv_mine[pl.ds(at + tiles + i, 1), :] for i in range(tiles)], axis=1)
        both = partial_model(first_a, first_b, stride, across, u, v, images.at[j], rhs[slot])
        for p in range(2):
            for i in range(tiles):
                part_mine[pl.ds(at + p * tiles + i, 1), :] = both[p][:, 128 * i : 128 * (i + 1)]

    if members <= 2:
        for j in range(members):
            models(j, j % 2)
    else:

        @pl.loop(0, members)
        def _(j):
            models(j, 0)

    part_all[group] = part_mine[...]
    each_group(part_all, part_send, part_recv, start)
    for r in range(max(rounds - low_bits, 1), rounds):
        hear(r)
        tell(r + 1)
    wait_bytes(uv_cols, high - 1, high_sem.at[1])
    send_low()
    each_group(ow_all, ow_send, ow_recv, wait)
    each_group(part_all, part_send, part_recv, wait)

    for j in range(members):
        picked = jnp.zeros((3 * tiles, 128), jnp.float32)
        model = jnp.zeros((2 * tiles, 128), jnp.float32)
        at = 2 * tiles * j
        for g in range(groups):
            model = model + part_all[g, at : at + 2 * tiles, :]
            for k in range(slots):
                first = 3 * tiles * k
                picked = picked + ow_all[g, first : first + 3 * tiles, :] * holds(g, k, j)
        weight = picked[2 * tiles :]
        weight = jnp.concatenate([weight, weight], axis=0)
        resid_wide[at : at + 2 * tiles, :] = weight * (picked[: 2 * tiles] - model)
    resid_mine[...] = resid_wide[...].astype(jnp.bfloat16)
    send_resid()
    own = pltpu.make_async_copy(resid_mine, resid_ref.at[column], out_sem.at[0])
    own.start()

    wait_bytes(uv_cols, columns - high, low_sem.at[1])
    row = row_iota(uv_cols.shape[1], 128)
    halved = lax.rem(row, 2 * tiles) >= tiles
    for i in range(columns):
        c = i % high * low + i // high
        full = fraction(uv_cols[i])
        phases[c] = jnp.where(halved, lax.shift_right_arithmetic(full, 1), full)
        where[c : c + 1, :] = uv_cols[i, place : place + 1, :].astype(jnp.int32)
    outs = [
        pltpu.make_async_copy(phases, phase_ref, out_sem.at[1]),
        pltpu.make_async_copy(where, where_ref, out_sem.at[2]),
    ]
    for out in outs:
        out.start()
    wait_bytes(uv_cols, high - 1, high_sem.at[0])
    wait_bytes(uv_cols, columns - high, low_sem.at[0])
    for out in [own] + outs:
        out.wait()
    wait_bytes(resid_ref, columns - 1, resid_sem.at[0])
    wait_bytes(resid_ref, columns - 1, resid_sem.at[1])


def grid_kernel(
    per_group,
    members,
    side,
    gain,
    off_hbm,
    phase_hbm,
    resid_hbm,
    out_hbm,
    off_ref,
    phase_ref,
    resid_ref,
    out_ref,
    front,
    back,
    lefts,
    rights,
    readies,
    resid_f,
    hits,
    in_sem,
    out_sem,
):
    loads = [
        pltpu.make_async_copy(off_hbm, off_ref, in_sem.at[0]),
        pltpu.make_async_copy(phase_hbm, phase_ref, in_sem.at[1]),
        pltpu.make_async_copy(resid_hbm, resid_ref, in_sem.at[2]),
    ]
    for load in loads:
        load.start()
    columns = phase_ref.shape[0]
    lanes = lefts[0].shape[1]
    tiles = lanes // 128
    rows = out_ref.shape[2]
    chunks = front.shape[0] // 2
    half = side // 2
    base = lefts[0].shape[0] // 2
    stride = (SUBGRID - side) // (FACET_SIDE - 1)
    facet_here = lax.axis_index("facet") * per_group
    first_line = lax.axis_index("sub") * rows
    facet_rows = readies[0].shape[1]
    first_a = lax.div(facet_here, FACET_SIDE)
    lines8 = row_iota(8, lanes)
    across = min(per_group, FACET_SIDE)
    deep = per_group // across
    mirrored = rows % 16 == 0 and across % 2 == 0 and deep + across // 2 <= facet_rows
    row = row_iota(facet_rows, lanes)
    if mirrored:
        first_b = lax.rem(facet_here, FACET_SIDE)
        middle = stride * (2 * first_b + across - 1) + (side - 1)
        lead_u = jnp.where(row < deep, row * stride, 0)
        lead_v = jnp.where(row < deep, middle, stride * (2 * (row - deep) + 1))
    else:
        facet = row + facet_here
        lead_u = (lax.div(facet, FACET_SIDE) - first_a) * stride
        lead_v = lax.rem(facet, FACET_SIDE) * (2 * stride) + (side - 1)
    front[...] = jnp.zeros_like(front)
    back[...] = jnp.zeros_like(back)
    if base > per_group * rows:
        for left in lefts:
            left[...] = jnp.zeros_like(left)
    for load in loads:
        load.wait()
    resid_f[...] = resid_ref[...].astype(jnp.float32)

    total = columns * members

    def begin(s):
        start = lax.rem(first_line - off_ref[lax.div(s, members), 2 * lax.rem(s, members)] + WIN, WIN)
        return jnp.where(start > WIN - rows, start - WIN, start)

    def scan(s, found):
        hits[found] = s
        ahead = first_line + (WIN + rows - 1) - off_ref[lax.div(s, members), 2 * lax.rem(s, members)]
        return found + jnp.where(lax.bitwise_and(ahead, WIN - 1) < side + rows - 1, 1, 0)

    if total <= 64:
        found = jnp.int32(0)
        for s in range(total):
            hits[found] = s
            ahead = first_line + (WIN + rows - 1) - off_ref[s // members, 2 * (s % members)]
            found = found + jnp.where(lax.bitwise_and(ahead, WIN - 1) < side + rows - 1, 1, 0)
    else:
        found = lax.fori_loop(0, total, scan, jnp.int32(0), unroll=8)

    def wide(x):
        return jnp.broadcast_to(x, (8, lanes))

    def conj_mul(a, b):
        return a[0] * b[0] + a[1] * b[1], a[1] * b[0] - a[0] * b[1]

    def lane_row(ref, c, at):
        return jnp.concatenate([ref[c, pl.ds(at + i, 1), :] for i in range(tiles)], axis=1)

    def choose(index):
        return jnp.where(index < found, hits[jnp.minimum(index, total - 1)], 0)

    def column_of(index):
        s = choose(index)
        return off_ref[lax.div(s, members), 2 * lax.rem(s, members) + 1]

    def prepare(index, ready):
        s = choose(index)
        scale = jnp.where(index < found, gain, 0.0)
        column = lax.div(s, members)
        j = lax.rem(s, members)
        fu = lane_row(phase_ref, column, 2 * tiles * j)
        hv = lane_row(phase_ref, column, 2 * tiles * j + tiles)
        rr = lane_row(resid_f, column, 2 * tiles * j) * scale
        ri = lane_row(resid_f, column, 2 * tiles * j + tiles) * scale
        plain = wave(lead_u * fu + lead_v * hv)
        head = cmul(plain, (rr, ri))
        abreast = wave((2 * lines8 + 1) * hv)
        along = wave((lines8 + (begin(s) + first_a * stride)) * fu)
        for part in range(2):
            ready[part] = head[part]
            ready[2 + part, :8] = abreast[part]
            ready[6 + part] = plain[part]
            ready[4 + part, :8] = along[part]

    def fill(index, ready, left, right):
        start = begin(choose(index))
        now = ready[2, :8], ready[3, :8]
        step = cmul(tuple(wide(t[7:8]) for t in now), tuple(wide(t[0:1]) for t in now))
        seq = chebyshev(now, step, half // 8)
        for h in range(half // 16):
            for part in range(2):
                both = jnp.concatenate([seq[2 * h][part], seq[2 * h + 1][part]], axis=0)
                right[part * half + h * 16 : part * half + (h + 1) * 16, :] = both.astype(jnp.bfloat16)

        now = ready[4, :8], ready[5, :8]
        step = conj_mul(tuple(wide(t[4:5]) for t in now), tuple(wide(t[0:1]) for t in now))
        step = cmul(step, step)
        seq = chebyshev(now, step, rows // 8)
        shown = []
        for h in range(rows // 8):
            cell = lines8 + (h * 8 + start)
            live = (cell >= 0) & (cell < side)
            shown.append(tuple(jnp.where(live, t, 0.0) for t in seq[h]))
        tall = min(rows, 16)
        per = 16 // tall
        if per == 2:
            table = [tuple(jnp.concatenate([t, t], axis=0).astype(jnp.bfloat16) for t in shown[0])]
        else:
            table = [
                tuple(jnp.concatenate([p, q], axis=0).astype(jnp.bfloat16) for p, q in zip(a, b))
                for a, b in zip(shown[0::2], shown[1::2])
            ]

        def spread(at, line):
            return tuple(
                jnp.broadcast_to(ready[at + part, line : line + 1, :], (16, lanes)).astype(jnp.bfloat16)
                for part in range(2)
            )

        def put(f, h, real, imag):
            at = f * rows + h * 16
            left[at : at + 16, :] = real
            left[base + at : base + at + 16, :] = imag

        if mirrored:
            turn = [spread(6, deep + k) for k in range(across // 2)]
            for a in range(deep):
                own = spread(0, a)
                for h, t in enumerate(table):
                    real, imag = cmul(t, own)
                    for k, (c, sn) in enumerate(turn):
                        upper = a * across + across // 2 + k
                        lower = a * across + across // 2 - 1 - k
                        rc, rs, ic, si = real * c, real * sn, imag * c, imag * sn
                        put(upper, h, rc - si, ic + rs)
                        put(lower, h, rc + si, ic - rs)
            return
        for f in range(0, per_group, per):
            own = tuple(
                jnp.concatenate(
                    [jnp.broadcast_to(ready[part, f + i : f + i + 1, :], (tall, lanes)) for i in range(per)], axis=0
                ).astype(jnp.bfloat16)
                for part in range(2)
            )
            for h, t in enumerate(table):
                at = f * rows + h * 16
                value = cmul(t, own)
                left[at : at + 16, :] = value[0]
                left[base + at : base + at + 16, :] = value[1]

    def add(index, left, right):
        offset = column_of(index)
        prod = lax.dot_general(
            right[...], left[...], (((1,), (1,)), ((), ())), preferred_element_type=jnp.float32
        )
        ahead = pl.ds(offset, half)
        behind = pl.ds(WIN - offset, half)
        for k in range(chunks):
            real = slice(128 * k, 128 * (k + 1))
            imag = slice(base + 128 * k, base + 128 * (k + 1))
            front[k, ahead, :] += prod[:half, real] - prod[half:, imag]
            back[k, behind, :] += prod[:half, real] + prod[half:, imag]
            front[chunks + k, ahead, :] += prod[:half, imag] + prod[half:, real]
            back[chunks + k, behind, :] += prod[:half, imag] - prod[half:, real]

    def pair(i, carry):
        add(2 * i, lefts[0], rights[0])
        fill(2 * i + 1, readies[1], lefts[1], rights[1])
        add(2 * i + 1, lefts[1], rights[1])
        fill(2 * i + 2, readies[0], lefts[0], rights[0])
        prepare(2 * i + 3, readies[1])
        prepare(2 * i + 4, readies[0])
        return carry

    prepare(0, readies[0])
    prepare(1, readies[1])
    fill(0, readies[0], lefts[0], rights[0])
    prepare(2, readies[0])
    lax.fori_loop(0, lax.div(found + 1, 2), pair, 0)

    turned = 7 - row_iota(8, 128)
    done = []
    for part in range(2):
        for k in range(chunks):
            x = front.at[part * chunks + k]
            y = back.at[part * chunks + k]
            ahead = [x[WIN - half : WIN], x[0:half] + x[WIN : WIN + half], x[half : WIN - half]]
            behind = []
            for at in range(WIN + half - 8, half - 8, -8):
                tile = y[at : at + 8]
                if at >= WIN:
                    tile = tile + y[at - WIN : at - WIN + 8]
                behind.append(jnp.take_along_axis(tile, turned, axis=0))
            whole = (jnp.concatenate(ahead, axis=0) + jnp.concatenate(behind, axis=0)).T
            facets = [f for f in range(per_group) if 0 <= f * rows - 128 * k < 128]
            for f in facets:
                at = f * rows - 128 * k
                out_ref[f, part] = whole[at : at + rows]
            if facets:
                some = pl.ds(facets[0], len(facets))
                copy = pltpu.make_async_copy(
                    out_ref.at[some, part], out_hbm.at[some, part], out_sem.at[part * chunks + k]
                )
                copy.start()
                done.append(copy)
    for copy in done:
        copy.wait()


def exchange_call(groups, columns, slot_subgrid, vis_count, offset, contributions, uv, obs, weight):
    per_group, _, members, _, side, _ = contributions.shape
    slots, lanes = weight.shape[2:]
    tiles = lanes // 128
    across = min(per_group, FACET_SIDE)
    width = (SUBGRID - side) // (FACET_SIDE - 1) * (across - 1) + side
    kept = -(-width // 256) * 128
    dma = pltpu.SemaphoreType.DMA
    f32, bf16 = jnp.float32, jnp.bfloat16

    def rows(n, unit=8):
        return -(-n // unit) * unit

    uv_rows = 2 * members * tiles + 1
    resid_rows = rows(2 * members * tiles, 16)
    return pl.pallas_call(
        functools.partial(exchange_kernel, groups, columns, per_group),
        out_shape=(
            jax.ShapeDtypeStruct((columns, uv_rows, 128), jnp.int32),
            jax.ShapeDtypeStruct((columns, 128), jnp.int32),
            jax.ShapeDtypeStruct((columns, resid_rows, 128), bf16),
        ),
        in_specs=[pl.BlockSpec(memory_space=pl.ANY)] * 7,
        out_specs=(pl.BlockSpec(memory_space=pl.ANY),) * 3,
        scratch_shapes=[
            pltpu.SMEM(slot_subgrid.shape, jnp.int32),
            pltpu.SMEM(vis_count.shape, jnp.int32),
            pltpu.SMEM(offset.shape, jnp.int32),
            pltpu.VMEM(uv.shape, f32),
            pltpu.VMEM(obs.shape, f32),
            pltpu.VMEM(weight.shape, f32),
            pltpu.VMEM((per_group, members, 2, side, side), bf16),
            pltpu.VMEM((across * side, 2 * kept), bf16),
            pltpu.VMEM((members, per_group // across, 2 * side, 2 * kept), bf16),
            [pltpu.VMEM((2 * kept, lanes), bf16)] * 2,
            pltpu.VMEM((groups, rows(2 * slots * tiles), 128), f32),
            pltpu.VMEM((groups, rows(3 * slots * tiles), 128), f32),
            pltpu.VMEM((uv_rows, 128), f32),
            pltpu.VMEM((columns, uv_rows, 128), f32),
            pltpu.VMEM((rows(2 * members * tiles), 128), f32),
            pltpu.VMEM((groups, rows(2 * members * tiles), 128), f32),
            pltpu.VMEM((resid_rows, 128), f32),
            pltpu.VMEM((resid_rows, 128), bf16),
            pltpu.VMEM((columns, uv_rows, 128), jnp.int32),
            pltpu.VMEM((columns, 128), jnp.int32),
            dma((6,)),
            dma((members,)),
            pltpu.SemaphoreType.REGULAR((max(columns.bit_length(), 1),)),
            dma((groups,)),
            dma((groups,)),
            dma((groups,)),
            dma((groups,)),
            dma((groups,)),
            dma((groups,)),
            dma((2,)),
            dma((2,)),
            dma((2,)),
            dma((3,)),
        ],
        compiler_params=pltpu.CompilerParams(collective_id=0, has_side_effects=True),
    )(slot_subgrid, vis_count, offset, contributions, uv, obs, weight)


def grid_call(phases, offsets, resid, per_group, members, lanes, side, rows, gain):
    base = -(-per_group * rows // 128) * 128
    half = side // 2
    return pl.pallas_call(
        functools.partial(grid_kernel, per_group, members, side, gain),
        out_shape=jax.ShapeDtypeStruct((per_group, 2, rows, WIN), jnp.float32),
        in_specs=[pl.BlockSpec(memory_space=pl.ANY)] * 3,
        out_specs=pl.BlockSpec(memory_space=pl.ANY),
        scratch_shapes=[
            pltpu.SMEM(offsets.shape, jnp.int32),
            pltpu.VMEM(phases.shape, jnp.int32),
            pltpu.VMEM(resid.shape, jnp.bfloat16),
            pltpu.VMEM((per_group, 2, rows, WIN), jnp.float32),
            pltpu.VMEM((base // 64, WIN + half, 128), jnp.float32),
            pltpu.VMEM((base // 64, WIN + half, 128), jnp.float32),
            [pltpu.VMEM((2 * base, lanes), jnp.bfloat16)] * 2,
            [pltpu.VMEM((2 * half, lanes), jnp.bfloat16)] * 2,
            [pltpu.VMEM((8, -(-per_group // 8) * 8, lanes), jnp.float32)] * 2,
            pltpu.VMEM(resid.shape, jnp.float32),
            pltpu.SMEM((offsets.shape[0] * members + 8,), jnp.int32),
            pltpu.SemaphoreType.DMA((3,)),
            pltpu.SemaphoreType.DMA((base // 64,)),
        ],
    )(offsets, phases, resid)


def body(contributions, slot_subgrid, vis_count, vis_uv, vis_obs, vis_weight, subgrid_offset):
    groups = lax.axis_size("facet")
    columns = lax.axis_size("sub")
    per_group, _, members, _, side, _ = contributions.shape
    lanes = vis_weight.shape[-1]
    phases, offsets, resid = exchange_call(
        groups,
        columns,
        slot_subgrid,
        vis_count,
        subgrid_offset,
        contributions,
        vis_uv,
        vis_obs,
        vis_weight,
    )
    gain = WIN / (side * math.sqrt(members * columns)) / math.sqrt(lanes)
    return grid_call(phases, offsets, resid, per_group, members, lanes, side, WIN // columns, gain)


def solution(mesh):
    placed = (
        P("facet", "sub", None, None, None, None),
        P("sub", None, None),
        P("facet", "sub", None),
        P("facet", "sub", None, None, None),
        P("facet", "sub", None, None, None),
        P("facet", "sub", None, None),
        P("sub", None, None),
    )
    return jax.shard_map(
        body, mesh=mesh, in_specs=placed, out_specs=P("facet", None, "sub", None), check_vma=False
    )
```

```python
import functools
import math

import jax
import jax.numpy as jnp
from jax import lax
from jax.experimental import pallas as pl
from jax.experimental.pallas import tpu as pltpu
from jax.sharding import PartitionSpec as P

SUBGRID = 512
FACET_SIDE = 4
WIN = 512
MESH = pl.DeviceIdType.MESH


def cmul(a, b):
    return a[0] * b[0] - a[1] * b[1], a[0] * b[1] + a[1] * b[0]


def row_iota(rows, lanes):
    return lax.broadcasted_iota(jnp.int32, (rows, lanes), 0)


SIN = (3.14159027, -5.16740673, 2.54401052, -0.55946246)
COS = (0.99999995, -4.93479283, 4.05841135, -1.33187657, 0.21968961)


def fraction(w):
    t = w * (1.0 / SUBGRID)
    t = t - jnp.where(t >= 0.5, 1.0, 0.0)
    return (t * 4294967296.0).astype(jnp.int32)


def wave(phase):
    t = phase.astype(jnp.float32) * (1.0 / 4294967296.0)
    q = t * t
    s = SIN[3]
    for a in SIN[2::-1]:
        s = s * q + a
    s = s * t
    c = COS[4]
    for a in COS[3::-1]:
        c = c * q + a
    s2 = s + s
    return 1.0 - s2 * s, s2 * c


def chebyshev(first, step, count):
    double = step[0] + step[0]
    seq = [first]
    if count > 1:
        seq.append(cmul(first, step))
    while len(seq) < count:
        seq.append(tuple(double * p - q for p, q in zip(seq[-1], seq[-2])))
    return seq


def fold_matrix(across, side, stride, fold):
    rows, cols = fold.shape
    kept = cols // 2
    low = side // 128 * 128
    high = side - low
    width = (across - 1) * stride + side
    spans = [(b, y, 64) for b in range(across) for y in range(0, low, 64)]
    spans += [(b, low, high) for b in range(across)]
    lines = lax.broadcasted_iota(jnp.int32, (64, 128), 0)
    lane = lax.broadcasted_iota(jnp.int32, (64, 128), 1)
    at = 0
    for b, y, count in spans:
        turn = 2 * (b * stride + y) - (width - 1) + 2 * lines
        sign = jnp.where(turn < 0, -1.0, 1.0)
        cell = lax.shift_right_arithmetic(jnp.abs(turn), 1) - lane
        for k in range(0, kept, 128):
            hit = cell == k
            fold[at : at + count, k : k + 128] = jnp.where(hit, 1.0, 0.0)[:count].astype(jnp.bfloat16)
            fold[at : at + count, kept + k : kept + k + 128] = jnp.where(hit, sign, 0.0)[:count].astype(
                jnp.bfloat16
            )
        at += count


def fold_image(c_ref, fold, images, j):
    per_group, _, _, side, _ = c_ref.shape
    across = min(per_group, FACET_SIDE)
    low = side // 128 * 128
    kept = fold.shape[1] // 2
    for a in range(per_group // across):
        for part in range(2):
            blocks = [c_ref[a * across + b, j, part] for b in range(across)]
            strip = jnp.concatenate([x[:, :low] for x in blocks] + [x[:, low:] for x in blocks], axis=1)
            res = jnp.dot(strip, fold[...], preferred_element_type=jnp.float32)
            images[j, a, part * side : (part + 1) * side, :kept] = res[:, :kept].astype(jnp.bfloat16)
            odd = res[:, kept:] if part == 1 else -res[:, kept:]
            images[j, a, (1 - part) * side : (2 - part) * side, kept:] = odd.astype(jnp.bfloat16)


def partial_model(first_a, first_b, stride, across, u, v, images, rhs):
    kept, lanes = rhs.shape[0] // 2, rhs.shape[1]
    side = images.shape[1] // 2
    width = (across - 1) * stride + side
    lines8 = row_iota(8, lanes)
    fu = fraction(u)
    hv = lax.shift_right_arithmetic(fraction(v), 1)

    def wide(x):
        return jnp.broadcast_to(x, (8, lanes))

    now = wave((2 * lines8 + 1) * hv)
    step = cmul(tuple(wide(t[7:8]) for t in now), tuple(wide(t[0:1]) for t in now))
    seq = chebyshev(now, step, kept // 8)
    for h in range(kept // 16):
        for part in range(2):
            both = jnp.concatenate([seq[2 * h][part], seq[2 * h + 1][part]], axis=0)
            rhs[part * kept + h * 16 : part * kept + (h + 1) * 16, :] = both.astype(jnp.bfloat16)

    now = wave(lines8 * fu)
    half = tuple(wide(t[4:5]) for t in now)
    seq = chebyshev(now, cmul(half, half), side // 8)
    model_r = jnp.zeros((1, lanes), jnp.float32)
    model_i = jnp.zeros((1, lanes), jnp.float32)
    for a in range(images.shape[0]):
        res = jnp.dot(images[a], rhs[...], preferred_element_type=jnp.float32)
        total_r = jnp.zeros((8, lanes), jnp.float32)
        total_i = jnp.zeros((8, lanes), jnp.float32)
        for h in range(side // 8):
            real = res[h * 8 : (h + 1) * 8]
            imag = res[side + h * 8 : side + (h + 1) * 8]
            c, s = seq[h]
            total_r = total_r + (c * real + s * imag)
            total_i = total_i + (c * imag - s * real)
        total_r = jnp.sum(total_r, axis=0, keepdims=True)
        total_i = jnp.sum(total_i, axis=0, keepdims=True)
        c, s = wave(((first_a + a) * stride) * fu + (2 * stride * first_b + (width - 1)) * hv)
        model_r = model_r + (c * total_r + s * total_i)
        model_i = model_i + (c * total_i - s * total_r)
    return model_r * (1.0 / SUBGRID), model_i * (1.0 / SUBGRID)


def exchange_kernel(
    groups,
    columns,
    per_group,
    table_hbm,
    count_hbm,
    off_hbm,
    c_hbm,
    uv_hbm,
    obs_hbm,
    weight_hbm,
    phase_ref,
    where_ref,
    resid_ref,
    table_ref,
    count_ref,
    off_ref,
    uv_ref,
    obs_ref,
    weight_ref,
    c_ref,
    fold,
    images,
    rhs,
    uv_all,
    ow_all,
    uv_mine,
    uv_cols,
    part_mine,
    part_all,
    resid_wide,
    resid_mine,
    phases,
    where,
    in_sem,
    c_sem,
    known,
    uv_send,
    uv_recv,
    ow_send,
    ow_recv,
    part_send,
    part_recv,
    high_sem,
    low_sem,
    resid_sem,
    out_sem,
):
    members = c_ref.shape[1]
    side = c_ref.shape[-1]
    slots = uv_ref.shape[2]
    lanes = uv_ref.shape[-1]
    tiles = lanes // 128
    across = min(per_group, FACET_SIDE)
    stride = (SUBGRID - side) // (FACET_SIDE - 1)
    group = lax.axis_index("facet")
    column = lax.axis_index("sub")
    barrier = pltpu.get_barrier_semaphore()
    rounds = columns.bit_length() - 1
    paired = columns == 1 << rounds
    low_bits = rounds // 2 if paired else 0
    low = 1 << low_bits
    high = columns // low
    order = list(range(low_bits, rounds)) + list(range(low_bits))
    mine_low = lax.rem(column, low)
    mine_high = lax.div(column, low)
    mine = mine_low * high + mine_high

    def peer_group(p):
        return lax.rem(group + p, groups)

    def peer_column(p):
        return lax.rem(column + p, columns)

    def partner(r):
        bit = 1 << r
        return column + bit - 2 * bit * lax.rem(lax.div(column, bit), 2)

    for p in range(1, groups):
        pl.semaphore_signal(barrier, inc=1, device_id={"facet": peer_group(p)}, device_id_type=MESH)
    near = [partner(r) for r in order] if paired else [peer_column(p) for p in range(1, columns)]
    for other in near:
        pl.semaphore_signal(barrier, inc=1, device_id={"sub": other}, device_id_type=MESH)

    def tell(r):
        if paired and 1 <= r < rounds:
            pl.semaphore_signal(known.at[r], inc=1, device_id={"sub": partner(order[r])}, device_id_type=MESH)

    def hear(r):
        if paired and 1 <= r < rounds:
            pl.semaphore_wait(known.at[r], 1)

    smalls = [
        pltpu.make_async_copy(src, dst, in_sem.at[i])
        for i, (src, dst) in enumerate(
            (
                (uv_hbm, uv_ref),
                (count_hbm, count_ref),
                (obs_hbm, obs_ref),
                (weight_hbm, weight_ref),
                (table_hbm, table_ref),
                (off_hbm, off_ref),
            )
        )
    ]
    loads = [
        pltpu.make_async_copy(c_hbm.at[:, 0, j], c_ref.at[:, j], c_sem.at[j]) for j in range(members)
    ]
    for load in smalls + loads:
        load.start()
    fold_matrix(across, side, stride, fold)
    for load in smalls:
        load.wait()

    lane = lax.broadcasted_iota(jnp.int32, (1, 128), 1)
    for k in range(slots):
        for i in range(tiles):
            part = slice(128 * i, 128 * (i + 1))
            for p in range(2):
                uv_all[group, (2 * k + p) * tiles + i : (2 * k + p) * tiles + i + 1, :] = uv_ref[0, 0, k, p : p + 1, part]
                ow_all[group, (3 * k + p) * tiles + i : (3 * k + p) * tiles + i + 1, :] = obs_ref[0, 0, k, p : p + 1, part]
            live = jnp.where(lane + 128 * i < count_ref[0, 0, k], 1.0, 0.0)
            at = (3 * k + 2) * tiles + i
            ow_all[group, at : at + 1, :] = weight_ref[0, 0, k : k + 1, part] * live
    pl.semaphore_wait(barrier, groups - 1 + len(near))
    tell(1)

    def to_group(buf, send, recv, p):
        return pltpu.make_async_remote_copy(
            src_ref=buf.at[group],
            dst_ref=buf.at[group],
            send_sem=send.at[p],
            recv_sem=recv.at[p],
            device_id={"facet": peer_group(p)},
            device_id_type=MESH,
        )

    def each_group(buf, send, recv, act):
        @pl.loop(1, groups)
        def _(p):
            act(to_group(buf, send, recv, p))

    def send(src, dst, sems, other):
        copy = pltpu.make_async_remote_copy(
            src_ref=src,
            dst_ref=dst,
            send_sem=sems.at[0],
            recv_sem=sems.at[1],
            device_id={"sub": other},
            device_id_type=MESH,
        )
        copy.start()

    def send_high():
        for p in range(1, high):
            other = lax.rem(mine_high + p, high) * low + mine_low
            send(uv_mine, uv_cols.at[mine], high_sem, other)

    def send_low():
        block = uv_cols.at[pl.ds(mine_low * high, high)]
        for p in range(1, low):
            send(block, block, low_sem, mine_high * low + lax.rem(mine_low + p, low))

    def send_resid():
        @pl.loop(1, columns)
        def _(p):
            send(resid_mine, resid_ref.at[column], resid_sem, peer_column(p))

    def wait_bytes(dst, count, sem):
        if count > 0:
            shown = dst.at[pl.ds(0, count)]
            pltpu.make_async_copy(shown, shown, sem).wait()

    def start(copy):
        copy.start()

    def wait(copy):
        copy.wait()

    each_group(uv_all, uv_send, uv_recv, start)
    for load in loads:
        load.wait()
    if members <= 2:
        for j in range(members):
            fold_image(c_ref, fold, images, j)
    else:

        @pl.loop(0, members)
        def _(j):
            fold_image(c_ref, fold, images, j)

    each_group(uv_all, uv_send, uv_recv, wait)

    def holds(g, k, j):
        return jnp.where(table_ref[0, g, k] == j, 1.0, 0.0)

    spots = jnp.zeros((1, 128), jnp.float32)
    for j in range(members):
        picked = jnp.zeros((2 * tiles, 128), jnp.float32)
        for g in range(groups):
            for k in range(slots):
                at = 2 * tiles * k
                picked = picked + uv_all[g, at : at + 2 * tiles, :] * holds(g, k, j)
        uv_mine[2 * tiles * j : 2 * tiles * (j + 1), :] = picked
        for axis in range(2):
            spots = jnp.where(lane == 2 * j + axis, off_ref[0, j, axis].astype(jnp.float32), spots)
    place = 2 * tiles * members
    uv_mine[place : place + 1, :] = spots
    uv_cols[mine] = uv_mine[...]
    for r in range(1, rounds - low_bits):
        hear(r)
        tell(r + 1)
    send_high()
    each_group(ow_all, ow_send, ow_recv, start)

    first_a = lax.div(group * per_group, FACET_SIDE)
    first_b = lax.rem(group * per_group, FACET_SIDE)

    def models(j, slot):
        at = 2 * tiles * j
        u = jnp.concatenate([uv_mine[pl.ds(at + i, 1), :] for i in range(tiles)], axis=1)
        v = jnp.concatenate([uv_mine[pl.ds(at + tiles + i, 1), :] for i in range(tiles)], axis=1)
        both = partial_model(first_a, first_b, stride, across, u, v, images.at[j], rhs[slot])
        for p in range(2):
            for i in range(tiles):
                part_mine[pl.ds(at + p * tiles + i, 1), :] = both[p][:, 128 * i : 128 * (i + 1)]

    if members <= 2:
        for j in range(members):
            models(j, j % 2)
    else:

        @pl.loop(0, members)
        def _(j):
            models(j, 0)

    part_all[group] = part_mine[...]
    each_group(part_all, part_send, part_recv, start)
    for r in range(max(rounds - low_bits, 1), rounds):
        hear(r)
        tell(r + 1)
    wait_bytes(uv_cols, high - 1, high_sem.at[1])
    send_low()
    each_group(ow_all, ow_send, ow_recv, wait)
    each_group(part_all, part_send, part_recv, wait)

    for j in range(members):
        picked = jnp.zeros((3 * tiles, 128), jnp.float32)
        model = jnp.zeros((2 * tiles, 128), jnp.float32)
        at = 2 * tiles * j
        for g in range(groups):
            model = model + part_all[g, at : at + 2 * tiles, :]
            for k in range(slots):
                first = 3 * tiles * k
                picked = picked + ow_all[g, first : first + 3 * tiles, :] * holds(g, k, j)
        weight = picked[2 * tiles :]
        weight = jnp.concatenate([weight, weight], axis=0)
        resid_wide[at : at + 2 * tiles, :] = weight * (picked[: 2 * tiles] - model)
    resid_mine[...] = resid_wide[...].astype(jnp.bfloat16)
    send_resid()
    own = pltpu.make_async_copy(resid_mine, resid_ref.at[column], out_sem.at[0])
    own.start()

    wait_bytes(uv_cols, columns - high, low_sem.at[1])
    row = row_iota(uv_cols.shape[1], 128)
    halved = lax.rem(row, 2 * tiles) >= tiles
    for i in range(columns):
        c = i % high * low + i // high
        full = fraction(uv_cols[i])
        phases[c] = jnp.where(halved, lax.shift_right_arithmetic(full, 1), full)
        where[c : c + 1, :] = uv_cols[i, place : place + 1, :].astype(jnp.int32)
    outs = [
        pltpu.make_async_copy(phases, phase_ref, out_sem.at[1]),
        pltpu.make_async_copy(where, where_ref, out_sem.at[2]),
    ]
    for out in outs:
        out.start()
    wait_bytes(uv_cols, high - 1, high_sem.at[0])
    wait_bytes(uv_cols, columns - high, low_sem.at[0])
    for out in [own] + outs:
        out.wait()
    wait_bytes(resid_ref, columns - 1, resid_sem.at[0])
    wait_bytes(resid_ref, columns - 1, resid_sem.at[1])


def grid_kernel(
    per_group,
    members,
    side,
    gain,
    off_hbm,
    phase_hbm,
    resid_hbm,
    out_hbm,
    off_ref,
    phase_ref,
    resid_ref,
    out_ref,
    front,
    back,
    lefts,
    rights,
    readies,
    resid_f,
    hits,
    in_sem,
    out_sem,
):
    loads = [
        pltpu.make_async_copy(off_hbm, off_ref, in_sem.at[0]),
        pltpu.make_async_copy(phase_hbm, phase_ref, in_sem.at[1]),
        pltpu.make_async_copy(resid_hbm, resid_ref, in_sem.at[2]),
    ]
    for load in loads:
        load.start()
    columns = phase_ref.shape[0]
    lanes = lefts[0].shape[1]
    tiles = lanes // 128
    rows = out_ref.shape[2]
    chunks = front.shape[0] // 2
    half = side // 2
    base = lefts[0].shape[0] // 2
    stride = (SUBGRID - side) // (FACET_SIDE - 1)
    facet_here = lax.axis_index("facet") * per_group
    first_line = lax.axis_index("sub") * rows
    facet_rows = readies[0].shape[1]
    first_a = lax.div(facet_here, FACET_SIDE)
    lines8 = row_iota(8, lanes)
    across = min(per_group, FACET_SIDE)
    deep = per_group // across
    extra = deep + across // 2
    mirrored = rows % 16 == 0 and across % 2 == 0 and extra + 2 <= facet_rows
    row = row_iota(facet_rows, lanes)
    if mirrored:
        first_b = lax.rem(facet_here, FACET_SIDE)
        middle = stride * (2 * first_b + across - 1) + (side - 1)
        lead_u = jnp.where(row < deep, row * stride, jnp.where(row == extra, 8, 0))
        lead_v = jnp.where(row < deep, middle, jnp.where(row < extra, stride * (2 * (row - deep) + 1), 0))
        lead_v = jnp.where(row == extra + 1, 16, lead_v)
    else:
        facet = row + facet_here
        lead_u = (lax.div(facet, FACET_SIDE) - first_a) * stride
        lead_v = lax.rem(facet, FACET_SIDE) * (2 * stride) + (side - 1)
    front[...] = jnp.zeros_like(front)
    back[...] = jnp.zeros_like(back)
    if base > per_group * rows:
        for left in lefts:
            left[...] = jnp.zeros_like(left)
    for load in loads:
        load.wait()
    resid_f[...] = resid_ref[...].astype(jnp.float32)

    total = columns * members

    def begin(s):
        start = lax.rem(first_line - off_ref[lax.div(s, members), 2 * lax.rem(s, members)] + WIN, WIN)
        return jnp.where(start > WIN - rows, start - WIN, start)

    def scan(s, found):
        hits[found] = s
        ahead = first_line + (WIN + rows - 1) - off_ref[lax.div(s, members), 2 * lax.rem(s, members)]
        return found + jnp.where(lax.bitwise_and(ahead, WIN - 1) < side + rows - 1, 1, 0)

    if total <= 64:
        found = jnp.int32(0)
        for s in range(total):
            hits[found] = s
            ahead = first_line + (WIN + rows - 1) - off_ref[s // members, 2 * (s % members)]
            found = found + jnp.where(lax.bitwise_and(ahead, WIN - 1) < side + rows - 1, 1, 0)
    else:
        found = lax.fori_loop(0, total, scan, jnp.int32(0), unroll=8)

    def wide(x):
        return jnp.broadcast_to(x, (8, lanes))

    def conj_mul(a, b):
        return a[0] * b[0] + a[1] * b[1], a[1] * b[0] - a[0] * b[1]

    def lane_row(ref, c, at):
        return jnp.concatenate([ref[c, pl.ds(at + i, 1), :] for i in range(tiles)], axis=1)

    def choose(index):
        return jnp.where(index < found, hits[jnp.minimum(index, total - 1)], 0)

    def column_of(index):
        s = choose(index)
        return off_ref[lax.div(s, members), 2 * lax.rem(s, members) + 1]

    def prepare(index, ready):
        s = choose(index)
        scale = jnp.where(index < found, gain, 0.0)
        column = lax.div(s, members)
        j = lax.rem(s, members)
        fu = lane_row(phase_ref, column, 2 * tiles * j)
        hv = lane_row(phase_ref, column, 2 * tiles * j + tiles)
        rr = lane_row(resid_f, column, 2 * tiles * j) * scale
        ri = lane_row(resid_f, column, 2 * tiles * j + tiles) * scale
        plain = wave(lead_u * fu + lead_v * hv)
        head = cmul(plain, (rr, ri))
        abreast = wave((2 * lines8 + 1) * hv)
        along = wave((lines8 + (begin(s) + first_a * stride)) * fu)
        for part in range(2):
            ready[part] = head[part]
            ready[2 + part, :8] = abreast[part]
            ready[6 + part] = plain[part]
            ready[4 + part, :8] = along[part]

    def fill(index, ready, left, right):
        start = begin(choose(index))
        now = ready[2, :8], ready[3, :8]
        if mirrored:
            step = tuple(wide(ready[6 + part, extra + 1 : extra + 2, :]) for part in range(2))
        else:
            step = cmul(tuple(wide(t[7:8]) for t in now), tuple(wide(t[0:1]) for t in now))
        seq = chebyshev(now, step, half // 8)
        for h in range(half // 16):
            for part in range(2):
                both = jnp.concatenate([seq[2 * h][part], seq[2 * h + 1][part]], axis=0)
                right[part * half + h * 16 : part * half + (h + 1) * 16, :] = both.astype(jnp.bfloat16)

        now = ready[4, :8], ready[5, :8]
        if mirrored:
            step = tuple(wide(ready[6 + part, extra : extra + 1, :]) for part in range(2))
        else:
            step = conj_mul(tuple(wide(t[4:5]) for t in now), tuple(wide(t[0:1]) for t in now))
            step = cmul(step, step)
        seq = chebyshev(now, step, rows // 8)
        shown = []
        for h in range(rows // 8):
            cell = lines8 + (h * 8 + start)
            live = (cell >= 0) & (cell < side)
            shown.append(tuple(jnp.where(live, t, 0.0) for t in seq[h]))
        tall = min(rows, 16)
        per = 16 // tall
        if per == 2:
            table = [tuple(jnp.concatenate([t, t], axis=0).astype(jnp.bfloat16) for t in shown[0])]
        else:
            table = [
                tuple(jnp.concatenate([p, q], axis=0).astype(jnp.bfloat16) for p, q in zip(a, b))
                for a, b in zip(shown[0::2], shown[1::2])
            ]

        def spread(at, line):
            return tuple(
                jnp.broadcast_to(ready[at + part, line : line + 1, :], (16, lanes)).astype(jnp.bfloat16)
                for part in range(2)
            )

        def put(f, h, real, imag):
            at = f * rows + h * 16
            left[at : at + 16, :] = real
            left[base + at : base + at + 16, :] = imag

        if mirrored:
            turn = [spread(6, deep + k) for k in range(across // 2)]
            for a in range(deep):
                own = spread(0, a)
                for h, t in enumerate(table):
                    real, imag = cmul(t, own)
                    for k, (c, sn) in enumerate(turn):
                        upper = a * across + across // 2 + k
                        lower = a * across + across // 2 - 1 - k
                        rc, rs, ic, si = real * c, real * sn, imag * c, imag * sn
                        put(upper, h, rc - si, ic + rs)
                        put(lower, h, rc + si, ic - rs)
            return
        for f in range(0, per_group, per):
            own = tuple(
                jnp.concatenate(
                    [jnp.broadcast_to(ready[part, f + i : f + i + 1, :], (tall, lanes)) for i in range(per)], axis=0
                ).astype(jnp.bfloat16)
                for part in range(2)
            )
            for h, t in enumerate(table):
                at = f * rows + h * 16
                value = cmul(t, own)
                left[at : at + 16, :] = value[0]
                left[base + at : base + at + 16, :] = value[1]

    def add(index, left, right):
        offset = column_of(index)
        prod = lax.dot_general(
            right[...], left[...], (((1,), (1,)), ((), ())), preferred_element_type=jnp.float32
        )
        ahead = pl.ds(offset, half)
        behind = pl.ds(WIN - offset, half)
        for k in range(chunks):
            real = slice(128 * k, 128 * (k + 1))
            imag = slice(base + 128 * k, base + 128 * (k + 1))
            front[k, ahead, :] += prod[:half, real] - prod[half:, imag]
            back[k, behind, :] += prod[:half, real] + prod[half:, imag]
            front[chunks + k, ahead, :] += prod[:half, imag] + prod[half:, real]
            back[chunks + k, behind, :] += prod[:half, imag] - prod[half:, real]

    def pair(i, carry):
        add(2 * i, lefts[0], rights[0])
        fill(2 * i + 1, readies[1], lefts[1], rights[1])
        add(2 * i + 1, lefts[1], rights[1])
        fill(2 * i + 2, readies[0], lefts[0], rights[0])
        prepare(2 * i + 3, readies[1])
        prepare(2 * i + 4, readies[0])
        return carry

    prepare(0, readies[0])
    prepare(1, readies[1])
    fill(0, readies[0], lefts[0], rights[0])
    prepare(2, readies[0])
    lax.fori_loop(0, lax.div(found + 1, 2), pair, 0)

    turned = 7 - row_iota(8, 128)
    done = []
    for part in range(2):
        for k in range(chunks):
            x = front.at[part * chunks + k]
            y = back.at[part * chunks + k]
            ahead = [x[WIN - half : WIN], x[0:half] + x[WIN : WIN + half], x[half : WIN - half]]
            behind = []
            for at in range(WIN + half - 8, half - 8, -8):
                tile = y[at : at + 8]
                if at >= WIN:
                    tile = tile + y[at - WIN : at - WIN + 8]
                behind.append(jnp.take_along_axis(tile, turned, axis=0))
            whole = (jnp.concatenate(ahead, axis=0) + jnp.concatenate(behind, axis=0)).T
            facets = [f for f in range(per_group) if 0 <= f * rows - 128 * k < 128]
            for f in facets:
                at = f * rows - 128 * k
                out_ref[f, part] = whole[at : at + rows]
            if facets:
                some = pl.ds(facets[0], len(facets))
                copy = pltpu.make_async_copy(
                    out_ref.at[some, part], out_hbm.at[some, part], out_sem.at[part * chunks + k]
                )
                copy.start()
                done.append(copy)
    for copy in done:
        copy.wait()


def exchange_call(groups, columns, slot_subgrid, vis_count, offset, contributions, uv, obs, weight):
    per_group, _, members, _, side, _ = contributions.shape
    slots, lanes = weight.shape[2:]
    tiles = lanes // 128
    across = min(per_group, FACET_SIDE)
    width = (SUBGRID - side) // (FACET_SIDE - 1) * (across - 1) + side
    kept = -(-width // 256) * 128
    dma = pltpu.SemaphoreType.DMA
    f32, bf16 = jnp.float32, jnp.bfloat16

    def rows(n, unit=8):
        return -(-n // unit) * unit

    uv_rows = 2 * members * tiles + 1
    resid_rows = rows(2 * members * tiles, 16)
    return pl.pallas_call(
        functools.partial(exchange_kernel, groups, columns, per_group),
        out_shape=(
            jax.ShapeDtypeStruct((columns, uv_rows, 128), jnp.int32),
            jax.ShapeDtypeStruct((columns, 128), jnp.int32),
            jax.ShapeDtypeStruct((columns, resid_rows, 128), bf16),
        ),
        in_specs=[pl.BlockSpec(memory_space=pl.ANY)] * 7,
        out_specs=(pl.BlockSpec(memory_space=pl.ANY),) * 3,
        scratch_shapes=[
            pltpu.SMEM(slot_subgrid.shape, jnp.int32),
            pltpu.SMEM(vis_count.shape, jnp.int32),
            pltpu.SMEM(offset.shape, jnp.int32),
            pltpu.VMEM(uv.shape, f32),
            pltpu.VMEM(obs.shape, f32),
            pltpu.VMEM(weight.shape, f32),
            pltpu.VMEM((per_group, members, 2, side, side), bf16),
            pltpu.VMEM((across * side, 2 * kept), bf16),
            pltpu.VMEM((members, per_group // across, 2 * side, 2 * kept), bf16),
            [pltpu.VMEM((2 * kept, lanes), bf16)] * 2,
            pltpu.VMEM((groups, rows(2 * slots * tiles), 128), f32),
            pltpu.VMEM((groups, rows(3 * slots * tiles), 128), f32),
            pltpu.VMEM((uv_rows, 128), f32),
            pltpu.VMEM((columns, uv_rows, 128), f32),
            pltpu.VMEM((rows(2 * members * tiles), 128), f32),
            pltpu.VMEM((groups, rows(2 * members * tiles), 128), f32),
            pltpu.VMEM((resid_rows, 128), f32),
            pltpu.VMEM((resid_rows, 128), bf16),
            pltpu.VMEM((columns, uv_rows, 128), jnp.int32),
            pltpu.VMEM((columns, 128), jnp.int32),
            dma((6,)),
            dma((members,)),
            pltpu.SemaphoreType.REGULAR((max(columns.bit_length(), 1),)),
            dma((groups,)),
            dma((groups,)),
            dma((groups,)),
            dma((groups,)),
            dma((groups,)),
            dma((groups,)),
            dma((2,)),
            dma((2,)),
            dma((2,)),
            dma((3,)),
        ],
        compiler_params=pltpu.CompilerParams(collective_id=0, has_side_effects=True),
    )(slot_subgrid, vis_count, offset, contributions, uv, obs, weight)


def grid_call(phases, offsets, resid, per_group, members, lanes, side, rows, gain):
    base = -(-per_group * rows // 128) * 128
    half = side // 2
    return pl.pallas_call(
        functools.partial(grid_kernel, per_group, members, side, gain),
        out_shape=jax.ShapeDtypeStruct((per_group, 2, rows, WIN), jnp.float32),
        in_specs=[pl.BlockSpec(memory_space=pl.ANY)] * 3,
        out_specs=pl.BlockSpec(memory_space=pl.ANY),
        scratch_shapes=[
            pltpu.SMEM(offsets.shape, jnp.int32),
            pltpu.VMEM(phases.shape, jnp.int32),
            pltpu.VMEM(resid.shape, jnp.bfloat16),
            pltpu.VMEM((per_group, 2, rows, WIN), jnp.float32),
            pltpu.VMEM((base // 64, WIN + half, 128), jnp.float32),
            pltpu.VMEM((base // 64, WIN + half, 128), jnp.float32),
            [pltpu.VMEM((2 * base, lanes), jnp.bfloat16)] * 2,
            [pltpu.VMEM((2 * half, lanes), jnp.bfloat16)] * 2,
            [pltpu.VMEM((8, -(-per_group // 8) * 8, lanes), jnp.float32)] * 2,
            pltpu.VMEM(resid.shape, jnp.float32),
            pltpu.SMEM((offsets.shape[0] * members + 8,), jnp.int32),
            pltpu.SemaphoreType.DMA((3,)),
            pltpu.SemaphoreType.DMA((base // 64,)),
        ],
    )(offsets, phases, resid)


def body(contributions, slot_subgrid, vis_count, vis_uv, vis_obs, vis_weight, subgrid_offset):
    groups = lax.axis_size("facet")
    columns = lax.axis_size("sub")
    per_group, _, members, _, side, _ = contributions.shape
    lanes = vis_weight.shape[-1]
    phases, offsets, resid = exchange_call(
        groups,
        columns,
        slot_subgrid,
        vis_count,
        subgrid_offset,
        contributions,
        vis_uv,
        vis_obs,
        vis_weight,
    )
    gain = WIN / (side * math.sqrt(members * columns)) / math.sqrt(lanes)
    return grid_call(phases, offsets, resid, per_group, members, lanes, side, WIN // columns, gain)


def solution(mesh):
    placed = (
        P("facet", "sub", None, None, None, None),
        P("sub", None, None),
        P("facet", "sub", None),
        P("facet", "sub", None, None, None),
        P("facet", "sub", None, None, None),
        P("facet", "sub", None, None),
        P("sub", None, None),
    )
    return jax.shard_map(
        body, mesh=mesh, in_specs=placed, out_specs=P("facet", None, "sub", None), check_vma=False
    )
```
